128 devices in a mesh: frame: 8 (over x, y_lo), band: 16 (over y_hi, z, core).
Axes of the slice: x: 4, y: 4 (y_hi: 2, y_lo: 2; y = y_hi * 2 + y_lo), z: 4, core: 2. Of those that a mesh axis runs over, the one named last changes fastest.
Arguments:
- features: bfloat16 [24, 64, 128, 128], P('frame', 'band'), may hold values from -6 to 6
- frame_pairs: int32 [24, 2], P('frame'), may hold values from 0 to 23, as said below
- conv_weight: float32 [4, 2, 2, 3, 3], replicated, may hold values from -1.5 to 1.5
- conv_bias: float32 [4, 2], replicated, may hold values from -1 to 1
Outputs:
- flows: float32 [24, 2, 2, 64, 128], P('frame', None, None, 'band')
The draws below stay inside these ranges and needn't reach their ends.
Inputs may be any that keep to these rules, and one draw needn't show every extreme that they name: `frame_pairs`: each pair names two different frames.
All inputs are finite; a program needn't handle non-finite values.
Results may differ from the reference program's by a relative error of at most 0.0003.
Values may be sent and summed in bfloat16 or wider, within the bound.
No kernel may reach another device: no remote copies, remote signals or barrier semaphores. Data moves between devices by JAX's collectives and lax.ppermute only.
A program may use at most 128 MiB of HBM per device.

```python
import math
import jax
import jax.numpy as jnp
from jax import lax

C = 128
W = 128
BAND_ROWS = 4
LAYERS = 4
H = 64
FRAMES = 24
PAIRS = 24
N_BAND = 16


def draw_features(key, part):
    key_base = jax.random.fold_in(key, 0)
    base = jnp.clip(jax.random.normal(key_base, (FRAMES, H, W, C), jnp.float32), -6.0, 6.0)
    return base.astype(jnp.bfloat16)


def draw_frame_pairs(key, part):
    key_src, key_off = jax.random.split(jax.random.fold_in(key, 17))
    sources = jax.random.randint(key_src, (PAIRS,), 0, FRAMES)
    sources = sources.at[0].set(FRAMES - 1)
    sources = sources.at[PAIRS - 1].set(0)
    offsets = jax.random.randint(key_off, (PAIRS,), 1, FRAMES)
    targets = (sources + offsets) % FRAMES
    return jnp.stack([sources, targets], axis=1).astype(jnp.int32)


def normal_values(rng, shape, scale, bound, kind=jnp.bfloat16):
    array = jax.random.normal(rng, shape, jnp.float32) * scale
    return jnp.minimum(jnp.maximum(array, -bound), bound).astype(kind)


def setup_inputs(seed: int = 0) -> dict:
    seeds = jax.random.split(jax.random.key(seed), 5)
    features = draw_features(jax.random.fold_in(seeds[4], 71), 0)
    frame_pairs = draw_frame_pairs(jax.random.fold_in(seeds[4], 71), 0)
    conv_weight = normal_values(seeds[2], (LAYERS, 2, 2, 3, 3), 18 ** -0.5, 1.5, jnp.float32)
    conv_bias = normal_values(seeds[3], (LAYERS, 2), 0.3, 1.0, jnp.float32)
    return {"features": features, "frame_pairs": frame_pairs, "conv_weight": conv_weight, "conv_bias": conv_bias}


score_gain = 2.5

def cell_coords(count, offset, total):
    return ((offset + jnp.arange(count)).astype(jnp.float32) + 0.5) / total * 2.0 - 1.0

def merge_stats(first, second):
    top = jnp.maximum(first[0], second[0])
    left = jnp.exp(first[0] - top)
    right = jnp.exp(second[0] - top)
    return (top, first[1] * left + second[1] * right, first[2] * left + second[2] * right, first[3] * left + second[3] * right)

def conv_layer(activated, weight, bias):
    out_rows = activated.shape[-2] - 2
    grid_cols = activated.shape[-1]
    pad_spec = [(0, 0)] * (activated.ndim - 1) + [(1, 1)]
    padded = jnp.pad(activated, pad_spec)
    summed = jnp.zeros(activated.shape[:-2] + (out_rows, grid_cols), jnp.float32)
    for shift_row in range(3):
        for shift_col in range(3):
            window = padded[..., shift_row:shift_row + out_rows, shift_col:shift_col + grid_cols]
            summed = summed + jnp.einsum('oc,...chw->...ohw', weight[:, :, shift_row, shift_col], window, precision=lax.Precision.HIGHEST)
    return summed + bias[:, None, None]

def reference(features, frame_pairs, conv_weight, conv_bias):
    height = H
    grid_cols = W
    cells = height * grid_cols
    block_cells = BAND_ROWS * grid_cols
    factor = score_gain / math.sqrt(C)
    col_coord = cell_coords(grid_cols, 0, grid_cols)
    row_coord = cell_coords(height, 0, height)
    all_cols = jnp.tile(col_coord, height)
    all_rows = jnp.repeat(row_coord, grid_cols)

    def one_pair(pair_row):
        source = features[pair_row[0]].reshape(cells, C)
        target = features[pair_row[1]].reshape(cells, C)
        source_blocks = source.reshape(N_BAND, block_cells, C)
        row_blocks = row_coord.reshape(N_BAND, BAND_ROWS)

        def scan_step(running, inputs):
            src_block, block_rows = inputs
            scores = lax.dot_general(src_block, target, (((1,), (1,)), ((), ())), preferred_element_type=jnp.float32) * factor
            row_max = lax.optimization_barrier(jnp.max(scores, axis=1))
            weights = jnp.exp(scores - row_max[:, None])
            shaped = weights.reshape(block_cells, height, grid_cols)
            weight_sum = lax.optimization_barrier(jnp.sum(weights, axis=1))
            col_mean = lax.optimization_barrier(jnp.sum(shaped * col_coord, axis=(1, 2))) / weight_sum
            row_mean = lax.optimization_barrier(jnp.sum(lax.optimization_barrier(jnp.sum(shaped, axis=2)) * row_coord, axis=1)) / weight_sum
            src_cols = jnp.tile(col_coord, BAND_ROWS)
            src_rows = jnp.repeat(block_rows, grid_cols)
            forward = jnp.stack([col_mean - src_cols, row_mean - src_rows]).reshape(2, BAND_ROWS, grid_cols)
            col_max = lax.optimization_barrier(jnp.max(scores, axis=0))
            rev_weights = jnp.exp(scores - col_max[None, :])
            partial_stats = (col_max, lax.optimization_barrier(jnp.sum(rev_weights, axis=0)), lax.optimization_barrier(jnp.sum(rev_weights * src_cols[:, None], axis=0)), lax.optimization_barrier(jnp.sum(rev_weights * src_rows[:, None], axis=0)))
            return (merge_stats(running, partial_stats), forward)
        initial = (jnp.full((cells,), -1e+30, jnp.float32), jnp.zeros((cells,), jnp.float32), jnp.zeros((cells,), jnp.float32), jnp.zeros((cells,), jnp.float32))
        stats, forwards = lax.scan(scan_step, initial, (source_blocks, row_blocks))
        forward = jnp.transpose(forwards, (1, 0, 2, 3)).reshape(2, height, grid_cols)
        backward = jnp.stack([stats[2] / stats[1] - all_cols, stats[3] / stats[1] - all_rows])
        return jnp.stack([forward, backward.reshape(2, height, grid_cols)])
    flows = lax.map(one_pair, frame_pairs)
    for layer_index in range(LAYERS):
        activated = jnp.tanh(2.0 * flows)
        pad_spec = [(0, 0)] * 3 + [(1, 1), (0, 0)]
        flows = flows + conv_layer(jnp.pad(activated, pad_spec), conv_weight[layer_index], conv_bias[layer_index])
    return flows
```

```python
import functools
import itertools
import math

import jax
import jax.numpy as jnp
from jax import lax
from jax.experimental import pallas as pl
from jax.experimental.pallas import tpu as pltpu
from jax.sharding import Mesh
from jax.sharding import PartitionSpec as P

score_gain = 2.5
AXES = ("fx", "fy", "bh", "bz", "bc")
SIZES = (4, 2, 2, 4, 2)
VMEM = pl.BlockSpec(memory_space=pltpu.VMEM)
SMEM = pl.BlockSpec(memory_space=pltpu.SMEM)
ANY = pl.BlockSpec(memory_space=pl.ANY)


def flat(coords):
    index = 0
    for value, size in zip(coords, SIZES):
        index = index * size + value
    return index


def hop(value, move):
    route = []
    for coords in itertools.product(*(range(size) for size in SIZES)):
        target = move(*coords)
        if target is not None:
            route.append((flat(coords), flat(target)))
    return lax.ppermute(value, AXES, route)


def flip_y(x, y, h, z, c):
    return x, 1 - y, h, z, c


def flip_a(x, y, h, z, c):
    return x ^ 1, y, h, z, c


def flip_b(x, y, h, z, c):
    return 3 - x, y, h, z, c


def flip_h(x, y, h, z, c):
    return x, y, 1 - h, z, c


def flip_c(x, y, h, z, c):
    return x, y, h, z, 1 - c


def flip_hc(x, y, h, z, c):
    return x, y, 1 - h, z, 1 - c


def turn_z(step):
    def move(x, y, h, z, c):
        return x, y, h, (z + step) % SIZES[3], c

    return move


def next_band(step):
    def move(x, y, h, z, c):
        band = (h * SIZES[3] + z) * SIZES[4] + c + step
        if band < 0 or band >= SIZES[2] * SIZES[3] * SIZES[4]:
            return None
        return x, y, band // (SIZES[3] * SIZES[4]), band // SIZES[4] % SIZES[3], band % SIZES[4]

    return move


def gray(x):
    return (x ^ (x >> 1)) & 1, x >> 1


def pick_kernel(table_ref, *refs, variants, slots):
    pieces = [refs[4 * v : 4 * v + 4] for v in range(variants)]
    outs = refs[4 * variants : 4 * variants + 2]
    sems = refs[4 * variants + 2]
    me_x, me_y = lax.axis_index("fx"), lax.axis_index("fy")
    me_a, me_b = gray(me_x)
    for stage in range(2):
        for slot in range(slots):
            for side in range(2):
                frame = table_ref[slot, side]
                variant, group = frame % variants, frame // variants
                to_a, to_b = gray(group // 2)
                fa, fb, fy = to_a ^ me_a, to_b ^ me_b, (group % 2) ^ me_y
                for v, bits in enumerate(((fy, fa, fb), (fa, fb, fy), (fb, fy, fa))):
                    place = bits[0] + 2 * bits[1] + 4 * bits[2]
                    for n, (low, count) in enumerate(((0, 1), (1, 1), (2, 2), (4, 4))):

                        @pl.when((variant == v) & (place >= low) & (place < low + count))
                        def _():
                            copy = pltpu.make_async_copy(
                                pieces[v][n].at[place - low], outs[side].at[slot], sems.at[slot, side]
                            )
                            if stage == 0:
                                copy.start()
                            else:
                                copy.wait()


def pick(table, pieces, slots):
    block = pieces[0][0].shape[1:]
    shape = jax.ShapeDtypeStruct((slots,) + block, pieces[0][0].dtype)
    flat_pieces = [piece for group in pieces for piece in group]
    return pl.pallas_call(
        functools.partial(pick_kernel, variants=len(pieces), slots=slots),
        out_shape=[shape, shape],
        in_specs=[SMEM] + [ANY] * len(flat_pieces),
        out_specs=[VMEM, VMEM],
        scratch_shapes=[pltpu.SemaphoreType.DMA((slots, 2))],
    )(table, *flat_pieces)


def match_kernel(rows_ref, *refs, nsrc, ntgt, pairs, span, cells, width):
    src = refs[:nsrc]
    tgt = refs[nsrc:nsrc + ntgt]
    fwd = refs[nsrc + ntgt : 2 * nsrc + ntgt]
    rev = refs[2 * nsrc + ntgt : 2 * nsrc + 2 * ntgt]
    rhs, acc, accy, g0, gq, gy, shift_r, shift_c = refs[2 * nsrc + 2 * ntgt :]
    chans = src[0].shape[-1]
    band_rows = cells // width
    groups = width // 8
    scale = score_gain / math.sqrt(chans) * math.log2(math.e)
    nt = (((1,), (1,)), ((), ()))
    lane = lax.broadcasted_iota(jnp.int32, (16, width), 1)
    row16 = lax.broadcasted_iota(jnp.int32, (16, width), 0)
    pick = jnp.where(row16 == 0, 1.0, jnp.where(row16 == 1, (2 * lane - (width - 1)).astype(jnp.float32), 0.0)).astype(jnp.bfloat16)
    pick = jnp.concatenate([pick, pick], axis=1)
    sub = lax.broadcasted_iota(jnp.int32, (8, width), 0).astype(jnp.float32)

    def block(jb, p, mode):
        yj = rows_ref[nsrc + jb]
        b = rhs[pl.ds(pl.multiple_of(jb * cells, cells), cells), :]
        for lo in range(0, nsrc, span):
            parts = [src[i][p] for i in range(lo, lo + span)]
            a = jnp.concatenate(parts, axis=0) if span > 1 else parts[0]
            s = lax.dot_general(jnp.concatenate([a, a], axis=1), b, nt, preferred_element_type=jnp.float32)
            for i in range(span):
                yi = rows_ref[lo + i]
                tt = [None] * band_rows
                uu = [None] * band_rows
                xx = [None] * band_rows
                for q in range(band_rows):
                    ps = [None] * band_rows
                    qs = [None] * band_rows
                    for k in range(groups):
                        r0 = i * cells + q * width + k * 8
                        t = [s[r0:r0 + 8, c * width:(c + 1) * width] for c in range(band_rows)]
                        rsl = slice(lo * cells + r0, lo * cells + r0 + 8)
                        if mode == 0:
                            w = [jnp.exp2(v) for v in t]
                            v = w
                        else:
                            m = shift_r[rsl, :]
                            w = [jnp.exp2(x - m) for x in t]
                            v = [jnp.exp2(x - shift_c[jb, :, c * width:(c + 1) * width]) for c, x in enumerate(t)]
                        a1 = w[0]
                        b1 = w[0]
                        for c in range(1, band_rows):
                            a1 = a1 + w[c]
                            b1 = b1 + a1
                        acc[rsl, :] = acc[rsl, :] + a1
                        accy[rsl, :] = accy[rsl, :] + (yj * a1 - b1)
                        for c in range(band_rows):
                            ps[c] = v[c] if k == 0 else ps[c] + v[c]
                            qs[c] = ps[c] if k == 0 else qs[c] + ps[c]
                    for c in range(band_rows):
                        tt[c] = ps[c] if q == 0 else tt[c] + ps[c]
                        uu[c] = tt[c] if q == 0 else uu[c] + tt[c]
                        xx[c] = qs[c] if q == 0 else xx[c] + qs[c]
                for c in range(band_rows):
                    cs = slice(c * width, (c + 1) * width)
                    if lo + i == 0:
                        g0[jb, :, cs] = tt[c]
                        gy[jb, :, cs] = yi * tt[c] - uu[c]
                        gq[jb, :, cs] = xx[c]
                    else:
                        g0[jb, :, cs] = g0[jb, :, cs] + tt[c]
                        gy[jb, :, cs] = gy[jb, :, cs] + (yi * tt[c] - uu[c])
                        gq[jb, :, cs] = gq[jb, :, cs] + xx[c]

    def sweep(p, mode):
        acc[...] = jnp.zeros_like(acc)
        accy[...] = jnp.zeros_like(accy)
        def body(jb, c):
            block(jb, p, mode)
            return c
        lax.fori_loop(0, ntgt, body, 0)

    def emit(p, shift_f, shift_b):
        ok = None
        for i in range(nsrc):
            sl = slice(i * cells, (i + 1) * cells)
            def lanes(ref):
                x = ref[sl, :]
                hi = x.astype(jnp.bfloat16)
                lo = (x - hi.astype(jnp.float32)).astype(jnp.bfloat16)
                both = jnp.concatenate([hi, lo], axis=1)
                return lax.dot_general(pick, both, nt, preferred_element_type=jnp.float32)
            one = lanes(acc)
            two = lanes(accy)
            tot = one[0:1]
            good = jnp.all((tot > 2.0 ** -90) & (tot < 2.0 ** 110))
            ok = good if ok is None else ok & good
            for r in range(band_rows):
                cs = slice(r * width, (r + 1) * width)
                fwd[i][p, band_rows + r:band_rows + r + 1, :] = one[0:1, cs]
                fwd[i][p, 2 * band_rows + r:2 * band_rows + r + 1, :] = one[1:2, cs] * (1.0 / width)
                fwd[i][p, 3 * band_rows + r:3 * band_rows + r + 1, :] = two[0:1, cs] * (1.0 / 32)
            if shift_f is None:
                fwd[i][p, 0:band_rows, :] = jnp.zeros((band_rows, width), jnp.float32)
            else:
                shift_f(i, p)
        for j in range(ntgt):
            for r in range(band_rows):
                cs = slice(r * width, (r + 1) * width)
                t = g0[j, :, cs]
                x = (129.0 + 2.0 * sub) * t - 16.0 * gq[j, :, cs]
                tot = jnp.sum(t, axis=0, keepdims=True)
                ok = ok & jnp.all((tot > 2.0 ** -90) & (tot < 2.0 ** 110))
                rev[j][p, band_rows + r:band_rows + r + 1, :] = tot
                rev[j][p, 2 * band_rows + r:2 * band_rows + r + 1, :] = jnp.sum(x, axis=0, keepdims=True) * (1.0 / width)
                rev[j][p, 3 * band_rows + r:3 * band_rows + r + 1, :] = jnp.sum(gy[j, :, cs], axis=0, keepdims=True) * (1.0 / 32)
                rev[j][p, r:r + 1, :] = jnp.zeros((1, width), jnp.float32) if shift_b is None else shift_b[j, 0:1, cs]
        return ok

    def pair(p, carry):
        for j in range(ntgt):
            b = tgt[j][p].astype(jnp.float32) * scale
            hi = b.astype(jnp.bfloat16)
            lo = (b - hi.astype(jnp.float32)).astype(jnp.bfloat16)
            rhs[j * cells:(j + 1) * cells, :] = jnp.concatenate([hi, lo], axis=1)
        sweep(p, 0)
        ok = emit(p, None, None)

        @pl.when(jnp.logical_not(ok))
        def _():
            shift_r[...] = jnp.full_like(shift_r, -1e30)
            shift_c[...] = jnp.full_like(shift_c, -1e30)
            def tops(jb, c):
                b = rhs[pl.ds(pl.multiple_of(jb * cells, cells), cells), :]
                for i in range(nsrc):
                    def part(q, c2):
                        a = src[i][p, pl.ds(pl.multiple_of(q * width, width), width), :]
                        s = lax.dot_general(jnp.concatenate([a, a], axis=1), b, nt, preferred_element_type=jnp.float32)
                        sl = pl.ds(pl.multiple_of(i * cells + q * width, width), width)
                        m = shift_r[sl, :]
                        for c3 in range(band_rows):
                            m = jnp.maximum(m, s[:, c3 * width:(c3 + 1) * width])
                        shift_r[sl, :] = m
                        t = shift_c[jb]
                        shift_c[jb] = jnp.maximum(t, jnp.broadcast_to(jnp.max(s, axis=0, keepdims=True), t.shape))
                        return c2
                    lax.fori_loop(0, band_rows, part, 0)
                return c
            lax.fori_loop(0, ntgt, tops, 0)
            def level(n, c):
                sl = pl.ds(pl.multiple_of(n * width, width), width)
                m = shift_r[sl, :]
                shift_r[sl, :] = jnp.broadcast_to(jnp.max(m, axis=1, keepdims=True), m.shape)
                return c
            lax.fori_loop(0, nsrc * (cells // width), level, 0)
            sweep(p, 1)
            def put(i, p_):
                for r in range(band_rows):
                    m = shift_r[i * cells + r * width:i * cells + (r + 1) * width, :]
                    fwd[i][p_, r:r + 1, :] = jnp.transpose(m)[0:1, :]
            emit(p, put, shift_c)
        return carry
    lax.fori_loop(0, pairs, pair, 0)


def match(src, tgt, rows):
    pairs, cells, chans = src[0].shape
    width = 128
    nsrc, ntgt = len(src), len(tgt)
    kern = functools.partial(match_kernel, nsrc=nsrc, ntgt=ntgt, pairs=pairs, span=nsrc, cells=cells, width=width)
    stats = jax.ShapeDtypeStruct((pairs, 4 * cells // width, width), jnp.float32)
    out = pl.pallas_call(
        kern,
        out_shape=[stats] * (nsrc + ntgt),
        in_specs=[SMEM] + [VMEM] * (nsrc + ntgt),
        out_specs=[VMEM] * (nsrc + ntgt),
        scratch_shapes=[
            pltpu.VMEM((ntgt * cells, 2 * chans), jnp.bfloat16),
            pltpu.VMEM((nsrc * cells, width), jnp.float32),
            pltpu.VMEM((nsrc * cells, width), jnp.float32),
            pltpu.VMEM((ntgt, 8, cells), jnp.float32),
            pltpu.VMEM((ntgt, 8, cells), jnp.float32),
            pltpu.VMEM((ntgt, 8, cells), jnp.float32),
            pltpu.VMEM((nsrc * cells, width), jnp.float32),
            pltpu.VMEM((ntgt, 8, cells), jnp.float32),
        ],
        cost_estimate=pl.CostEstimate(flops=6_000_000_000, bytes_accessed=4_000_000, transcendentals=12_600_000),
    )(rows, *src, *tgt)
    return out[:nsrc], out[nsrc:]


def merge_kernel(*refs, band_rows, width):
    out = refs[8]
    band = (lax.axis_index("bh") * SIZES[3] + lax.axis_index("bz")) * SIZES[4] + lax.axis_index("bc")
    col = (2 * lax.broadcasted_iota(jnp.int32, (band_rows, width), 1) - (width - 1)).astype(jnp.float32) * (1.0 / width)
    row = lax.broadcasted_iota(jnp.int32, (band_rows, width), 0) + band * band_rows
    row = (2 * row - 63).astype(jnp.float32) * (1.0 / 64)
    for p in range(out.shape[0]):
        for way in range(2):
            part = [refs[4 * way + n][p] for n in range(4)]
            get = [[x[k * band_rows : (k + 1) * band_rows] for x in part] for k in range(4)]
            top = functools.reduce(jnp.maximum, get[0])
            scale = [jnp.exp2(m - top) for m in get[0]]
            total, cols, rows = (sum(v * s for v, s in zip(get[k], scale)) for k in (1, 2, 3))
            out[p, way, 0] = cols / total - col
            out[p, way, 1] = rows / total - row


def merge(fwd, rev, band_rows, width):
    pairs = fwd[0].shape[0]
    return pl.pallas_call(
        functools.partial(merge_kernel, band_rows=band_rows, width=width),
        out_shape=jax.ShapeDtypeStruct((pairs, 2, 2, band_rows, width), jnp.float32),
        in_specs=[VMEM] * 8,
        out_specs=VMEM,
    )(*fwd, *rev)


def refine_kernel(weight, bias, before, own, after, out, *cur, layers):
    pairs, ways, comps, band_rows, width = own.shape
    high = 16
    total = pairs * ways * high
    band = (lax.axis_index("bh") * SIZES[3] + lax.axis_index("bz")) * SIZES[4] + lax.axis_index("bc")
    last = SIZES[2] * SIZES[3] * SIZES[4] - 1
    for i in range(comps):
        for p in range(pairs):
            for d in range(ways):
                base = (p * ways + d) * high
                cur[i][base : base + band_rows] = before[p, d, i]
                cur[i][base + band_rows : base + 2 * band_rows] = own[p, d, i]
                cur[i][base + 2 * band_rows : base + 3 * band_rows] = after[p, d, i]
                cur[i][base + 3 * band_rows : base + high] = jnp.zeros((high - 3 * band_rows, width), jnp.float32)
    row = lax.broadcasted_iota(jnp.int32, (total, width), 0) & (high - 1)
    lane = lax.broadcasted_iota(jnp.int32, (total, width), 1)
    low = jnp.where(band == 0, band_rows, 0)
    top = jnp.where(band == last, 2 * band_rows, 3 * band_rows)
    inside = ((row >= low) & (row < top)).astype(jnp.float32)
    keep_left = (lane > 0).astype(jnp.float32)
    keep_right = (lane < width - 1).astype(jnp.float32)
    for layer in range(layers):
        taps = []
        for i in range(comps):
            act = jnp.tanh(2.0 * cur[i][...]) * inside
            taps.append((pltpu.roll(act, 1, 1) * keep_left, act, pltpu.roll(act, width - 1, 1) * keep_right))
        for o in range(comps):
            lines = []
            for r in range(3):
                line = None
                for i in range(comps):
                    for c in range(3):
                        term = taps[i][c] * weight[(((layer * comps + o) * comps + i) * 3 + r) * 3 + c]
                        line = term if line is None else line + term
                lines.append(line)
            grown = pltpu.roll(lines[0], 1, 0) + lines[1] + pltpu.roll(lines[2], total - 1, 0)
            cur[o][...] = cur[o][...] + (grown + bias[layer * comps + o])
    for i in range(comps):
        for p in range(pairs):
            for d in range(ways):
                base = (p * ways + d) * high + band_rows
                out[p, d, i] = cur[i][base : base + band_rows]


def refine(weight, bias, before, own, after):
    pairs, ways, comps, band_rows, width = own.shape
    return pl.pallas_call(
        functools.partial(refine_kernel, layers=weight.shape[0]),
        out_shape=jax.ShapeDtypeStruct(own.shape, jnp.float32),
        in_specs=[SMEM, SMEM, VMEM, VMEM, VMEM],
        out_specs=VMEM,
        scratch_shapes=[pltpu.VMEM((pairs * ways * 16, width), jnp.float32)] * comps,
    )(weight.reshape(-1), bias.reshape(-1), before, own, after)


def gather_frames(blocks):
    orders = ((flip_y, flip_a, flip_b), (flip_a, flip_b, flip_y), (flip_b, flip_y, flip_a))
    held = [[block] for block in blocks]
    for stage in range(3):
        got = []
        for v, order in enumerate(orders):
            have = held[v]
            send = have[0] if len(have) == 1 else jnp.concatenate(have, axis=0)
            got.append(hop(send, order[stage]))
        for v in range(len(orders)):
            held[v].append(got[v])
    return held


def shards(features, frame_pairs, conv_weight, conv_bias):
    frames, band_rows, width, chans = features.shape
    pairs = frame_pairs.shape[0]
    cells = band_rows * width
    h, z, c = lax.axis_index("bh"), lax.axis_index("bz"), lax.axis_index("bc")
    flat_features = features.reshape(frames, cells, chans)
    held = gather_frames([flat_features[v : v + 1] for v in range(frames)])
    src0, tgt0 = pick(frame_pairs, held, pairs)
    tgt1 = hop(tgt0, turn_z(1))
    tgt2 = hop(tgt0, turn_z(-1))
    src1 = hop(src0, flip_h)
    src2 = hop(src0, flip_c)
    far_up = hop(tgt1[:2], turn_z(1))
    far_down = hop(tgt2[2:], turn_z(-1))
    src3 = hop(src1, flip_c)
    tgt3 = jnp.concatenate([far_up, far_down], axis=0)

    def band_of(hh, zz, cc):
        return (hh * SIZES[3] + zz % SIZES[3]) * SIZES[4] + cc

    bands = [band_of(h, z, c), band_of(1 - h, z, c), band_of(h, z, 1 - c), band_of(1 - h, z, 1 - c)]
    bands += [band_of(h, z, c), band_of(h, z + 3, c), band_of(h, z + 1, c), band_of(h, z + 2, c)]
    rows = jnp.stack(bands).astype(jnp.float32) * band_rows - 27.5
    fwd, rev = match((src0, src1, src2, src3), (tgt0, tgt1, tgt2, tgt3), rows)
    fwd_parts = [fwd[0], hop(fwd[1], flip_h), hop(fwd[2], flip_c), hop(fwd[3], flip_hc)]
    rev_parts = [rev[0], hop(rev[1], turn_z(-1)), hop(rev[2], turn_z(1)), hop(rev[3], turn_z(2))]
    flows = merge(fwd_parts, rev_parts, band_rows, width)
    before = hop(flows, next_band(1))
    after = hop(flows, next_band(-1))
    return refine(conv_weight, conv_bias, before, flows, after)


def solution(mesh):
    finer = Mesh(mesh.devices.reshape(SIZES), AXES)
    frame, band = AXES[:2], AXES[2:]
    placed = (P(frame, band, None, None), P(frame, None), P(), P())
    return jax.shard_map(
        shards,
        mesh=finer,
        in_specs=placed,
        out_specs=P(frame, None, None, band, None),
        check_vma=False,
    )
```

```python
import functools
import itertools
import math

import jax
import jax.numpy as jnp
from jax import lax
from jax.experimental import pallas as pl
from jax.experimental.pallas import tpu as pltpu
from jax.sharding import Mesh
from jax.sharding import PartitionSpec as P

score_gain = 2.5
AXES = ("fx", "fy", "bh", "bz", "bc")
SIZES = (4, 2, 2, 4, 2)
VMEM = pl.BlockSpec(memory_space=pltpu.VMEM)
SMEM = pl.BlockSpec(memory_space=pltpu.SMEM)
ANY = pl.BlockSpec(memory_space=pl.ANY)


def flat(coords):
    index = 0
    for value, size in zip(coords, SIZES):
        index = index * size + value
    return index


def hop(value, move):
    route = []
    for coords in itertools.product(*(range(size) for size in SIZES)):
        target = move(*coords)
        if target is not None:
            route.append((flat(coords), flat(target)))
    return lax.ppermute(value, AXES, route)


def flip_y(x, y, h, z, c):
    return x, 1 - y, h, z, c


def flip_a(x, y, h, z, c):
    return x ^ 1, y, h, z, c


def flip_b(x, y, h, z, c):
    return 3 - x, y, h, z, c


def flip_h(x, y, h, z, c):
    return x, y, 1 - h, z, c


def flip_c(x, y, h, z, c):
    return x, y, h, z, 1 - c


def flip_hc(x, y, h, z, c):
    return x, y, 1 - h, z, 1 - c


def turn_z(step):
    def move(x, y, h, z, c):
        return x, y, h, (z + step) % SIZES[3], c

    return move


def next_band(step):
    def move(x, y, h, z, c):
        band = (h * SIZES[3] + z) * SIZES[4] + c + step
        if band < 0 or band >= SIZES[2] * SIZES[3] * SIZES[4]:
            return None
        return x, y, band // (SIZES[3] * SIZES[4]), band // SIZES[4] % SIZES[3], band % SIZES[4]

    return move


def gray(x):
    return (x ^ (x >> 1)) & 1, x >> 1


def pick_kernel(table_ref, *refs, variants, sizes):
    pieces = [refs[4 * v : 4 * v + 4] for v in range(variants)]
    outs = refs[4 * variants :]
    me_x, me_y = lax.axis_index("fx"), lax.axis_index("fy")
    me_a, me_b = gray(me_x)
    slots = [(group, n) for group, size in enumerate(sizes) for n in range(size)]
    for slot, (part, n) in enumerate(slots):
        for side in range(2):
            frame = table_ref[slot, side]
            variant, group = frame % variants, frame // variants
            to_a, to_b = gray(group // 2)
            fa, fb, fy = to_a ^ me_a, to_b ^ me_b, (group % 2) ^ me_y
            for v, bits in enumerate(((fy, fa, fb), (fa, fb, fy), (fb, fy, fa))):
                place = bits[0] + 2 * bits[1] + 4 * bits[2]
                for m, (low, count) in enumerate(((0, 1), (1, 1), (2, 2), (4, 4))):

                    @pl.when((variant == v) & (place >= low) & (place < low + count))
                    def _():
                        outs[2 * part + side][n] = pieces[v][m][place - low]


def pick(table, held, sizes):
    block = held[0][0].shape[1:]
    pieces = [piece for have in held for piece in have]
    shapes = [jax.ShapeDtypeStruct((size,) + block, pieces[0].dtype) for size in sizes for _ in range(2)]
    return pl.pallas_call(
        functools.partial(pick_kernel, variants=len(held), sizes=sizes),
        out_shape=shapes,
        in_specs=[SMEM] + [VMEM] * len(pieces),
        out_specs=[VMEM] * len(shapes),
        compiler_params=pltpu.CompilerParams(vmem_limit_bytes=12 << 20),
    )(table, *pieces)


def match_kernel(*refs, nsrc, ntgt, sizes, earlier, span, cells, width):
    groups_of = len(sizes)
    refs = list(refs)
    src = [refs[i * groups_of : (i + 1) * groups_of] for i in range(nsrc)]
    refs = refs[nsrc * groups_of :]
    tgt = [refs[j * groups_of : (j + 1) * groups_of] for j in range(ntgt)]
    refs = refs[ntgt * groups_of :]
    if earlier:
        fwd_in, rev_in = refs[:2]
        refs = refs[2:]
    fwd, rev, rhs, acc, accy, g0, gq, gy, shift_r, shift_c = refs
    if earlier:
        fwd[:, :earlier] = fwd_in[...]
        rev[:, :earlier] = rev_in[...]
    h, z, core = lax.axis_index("bh"), lax.axis_index("bz"), lax.axis_index("bc")
    src_place = [(h, core), (1 - h, core), (h, 1 - core), (1 - h, 1 - core)]
    src_slot = [hh * SIZES[4] + cc for hh, cc in src_place]
    src_band = [(hh * SIZES[3] + z) * SIZES[4] + cc for hh, cc in src_place]
    tgt_slot = [(z + step) % SIZES[3] for step in (0, 3, 1, 2)]
    tgt_band = [(h * SIZES[3] + zz) * SIZES[4] + core for zz in tgt_slot]
    band_rows = cells // width
    chans = src[0][0].shape[-1]
    groups = width // 8
    scale = score_gain / math.sqrt(chans) * math.log2(math.e)
    nt = (((1,), (1,)), ((), ()))
    lane = lax.broadcasted_iota(jnp.int32, (16, width), 1)
    row16 = lax.broadcasted_iota(jnp.int32, (16, width), 0)
    pick = jnp.where(row16 == 0, 1.0, jnp.where(row16 == 1, (2 * lane - (width - 1)).astype(jnp.float32), 0.0)).astype(jnp.bfloat16)
    pick = jnp.concatenate([pick, pick], axis=1)
    sub = lax.broadcasted_iota(jnp.int32, (8, width), 0).astype(jnp.float32)

    def place(band):
        return (band * band_rows).astype(jnp.float32) - 27.5

    def block(jb, p, mode):
        yj = place(functools.reduce(lambda x, j: jnp.where(jb == j, tgt_band[j], x), range(1, ntgt), tgt_band[0]))
        b = rhs[pl.ds(pl.multiple_of(jb * cells, cells), cells), :]
        for lo in range(0, nsrc, span):
            parts = [src[i][p[0]][p[1]] for i in range(lo, lo + span)]
            a = jnp.concatenate(parts, axis=0) if span > 1 else parts[0]
            s = lax.dot_general(jnp.concatenate([a, a], axis=1), b, nt, preferred_element_type=jnp.float32)
            for i in range(span):
                yi = place(src_band[lo + i])
                tt = [None] * band_rows
                uu = [None] * band_rows
                xx = [None] * band_rows
                for q in range(band_rows):
                    ps = [None] * band_rows
                    qs = [None] * band_rows
                    for k in range(groups):
                        r0 = i * cells + q * width + k * 8
                        t = [s[r0:r0 + 8, c * width:(c + 1) * width] for c in range(band_rows)]
                        rsl = slice(lo * cells + r0, lo * cells + r0 + 8)
                        if mode == 0:
                            w = [jnp.exp2(v) for v in t]
                            v = w
                        else:
                            m = shift_r[rsl, :]
                            w = [jnp.exp2(x - m) for x in t]
                            v = [jnp.exp2(x - shift_c[jb, :, c * width:(c + 1) * width]) for c, x in enumerate(t)]
                        a1 = w[0]
                        b1 = w[0]
                        for c in range(1, band_rows):
                            a1 = a1 + w[c]
                            b1 = b1 + a1
                        acc[rsl, :] = acc[rsl, :] + a1
                        accy[rsl, :] = accy[rsl, :] + (yj * a1 - b1)
                        for c in range(band_rows):
                            ps[c] = v[c] if k == 0 else ps[c] + v[c]
                            qs[c] = ps[c] if k == 0 else qs[c] + ps[c]
                    for c in range(band_rows):
                        tt[c] = ps[c] if q == 0 else tt[c] + ps[c]
                        uu[c] = tt[c] if q == 0 else uu[c] + tt[c]
                        xx[c] = qs[c] if q == 0 else xx[c] + qs[c]
                for c in range(band_rows):
                    cs = slice(c * width, (c + 1) * width)
                    if lo + i == 0:
                        g0[jb, :, cs] = tt[c]
                        gy[jb, :, cs] = yi * tt[c] - uu[c]
                        gq[jb, :, cs] = xx[c]
                    else:
                        g0[jb, :, cs] = g0[jb, :, cs] + tt[c]
                        gy[jb, :, cs] = gy[jb, :, cs] + (yi * tt[c] - uu[c])
                        gq[jb, :, cs] = gq[jb, :, cs] + xx[c]

    def sweep(p, mode):
        acc[...] = jnp.zeros_like(acc)
        accy[...] = jnp.zeros_like(accy)
        def body(jb, c):
            block(jb, p, mode)
            return c
        lax.fori_loop(0, ntgt, body, 0)

    def emit(at, shift_f, shift_b):
        ok = None
        for i in range(nsrc):
            sl = slice(i * cells, (i + 1) * cells)
            def lanes(ref):
                x = ref[sl, :]
                hi = x.astype(jnp.bfloat16)
                lo = (x - hi.astype(jnp.float32)).astype(jnp.bfloat16)
                both = jnp.concatenate([hi, lo], axis=1)
                return lax.dot_general(pick, both, nt, preferred_element_type=jnp.float32)
            one = lanes(acc)
            two = lanes(accy)
            tot = one[0:1]
            good = jnp.all((tot > 2.0 ** -90) & (tot < 2.0 ** 110))
            ok = good if ok is None else ok & good
            for r in range(band_rows):
                cs = slice(r * width, (r + 1) * width)
                fwd[src_slot[i], at, band_rows + r:band_rows + r + 1, :] = one[0:1, cs]
                fwd[src_slot[i], at, 2 * band_rows + r:2 * band_rows + r + 1, :] = one[1:2, cs] * (1.0 / width)
                fwd[src_slot[i], at, 3 * band_rows + r:3 * band_rows + r + 1, :] = two[0:1, cs] * (1.0 / 32)
            if shift_f is None:
                fwd[src_slot[i], at, 0:band_rows, :] = jnp.zeros((band_rows, width), jnp.float32)
            else:
                shift_f(i)
        for j in range(ntgt):
            for r in range(band_rows):
                cs = slice(r * width, (r + 1) * width)
                t = g0[j, :, cs]
                x = (129.0 + 2.0 * sub) * t - 16.0 * gq[j, :, cs]
                tot = jnp.sum(t, axis=0, keepdims=True)
                ok = ok & jnp.all((tot > 2.0 ** -90) & (tot < 2.0 ** 110))
                rev[tgt_slot[j], at, band_rows + r:band_rows + r + 1, :] = tot
                rev[tgt_slot[j], at, 2 * band_rows + r:2 * band_rows + r + 1, :] = jnp.sum(x, axis=0, keepdims=True) * (1.0 / width)
                rev[tgt_slot[j], at, 3 * band_rows + r:3 * band_rows + r + 1, :] = jnp.sum(gy[j, :, cs], axis=0, keepdims=True) * (1.0 / 32)
                rev[tgt_slot[j], at, r:r + 1, :] = jnp.zeros((1, width), jnp.float32) if shift_b is None else shift_b[j, 0:1, cs]
        return ok

    def pair(p, at):
        for j in range(ntgt):
            b = tgt[j][p[0]][p[1]].astype(jnp.float32) * scale
            hi = b.astype(jnp.bfloat16)
            lo = (b - hi.astype(jnp.float32)).astype(jnp.bfloat16)
            rhs[j * cells:(j + 1) * cells, :] = jnp.concatenate([hi, lo], axis=1)
        sweep(p, 0)
        ok = emit(at, None, None)

        @pl.when(jnp.logical_not(ok))
        def _():
            shift_r[...] = jnp.full_like(shift_r, -1e30)
            shift_c[...] = jnp.full_like(shift_c, -1e30)
            def tops(jb, c):
                b = rhs[pl.ds(pl.multiple_of(jb * cells, cells), cells), :]
                for i in range(nsrc):
                    def part(q, c2):
                        a = src[i][p[0]][p[1], pl.ds(pl.multiple_of(q * width, width), width), :]
                        s = lax.dot_general(jnp.concatenate([a, a], axis=1), b, nt, preferred_element_type=jnp.float32)
                        sl = pl.ds(pl.multiple_of(i * cells + q * width, width), width)
                        m = shift_r[sl, :]
                        for c3 in range(band_rows):
                            m = jnp.maximum(m, s[:, c3 * width:(c3 + 1) * width])
                        shift_r[sl, :] = m
                        t = shift_c[jb]
                        shift_c[jb] = jnp.maximum(t, jnp.broadcast_to(jnp.max(s, axis=0, keepdims=True), t.shape))
                        return c2
                    lax.fori_loop(0, band_rows, part, 0)
                return c
            lax.fori_loop(0, ntgt, tops, 0)
            def level(n, c):
                sl = pl.ds(pl.multiple_of(n * width, width), width)
                m = shift_r[sl, :]
                shift_r[sl, :] = jnp.broadcast_to(jnp.max(m, axis=1, keepdims=True), m.shape)
                return c
            lax.fori_loop(0, nsrc * (cells // width), level, 0)
            sweep(p, 1)
            def put(i):
                for r in range(band_rows):
                    m = shift_r[i * cells + r * width:i * cells + (r + 1) * width, :]
                    fwd[src_slot[i], at, r:r + 1, :] = jnp.transpose(m)[0:1, :]
            emit(at, put, shift_c)

    at = earlier
    for group, size in enumerate(sizes):
        if size == 1:
            pair((group, 0), at)
        else:
            def step(n, carry):
                pair((group, n), at + n)
                return carry
            lax.fori_loop(0, size, step, 0)
        at += size


def match(src, tgt, earlier=None):
    cells, chans = src[0][0].shape[1:]
    width = 128
    nsrc, ntgt = len(src), len(tgt)
    sizes = tuple(part.shape[0] for part in src[0])
    before = earlier[0].shape[1] if earlier else 0
    kern = functools.partial(
        match_kernel, nsrc=nsrc, ntgt=ntgt, sizes=sizes, earlier=before, span=nsrc, cells=cells, width=width
    )
    stats = jax.ShapeDtypeStruct((nsrc, before + sum(sizes), 4 * cells // width, width), jnp.float32)
    operands = [part for band in (*src, *tgt) for part in band] + list(earlier or ())
    pairs = sum(sizes)
    return pl.pallas_call(
        kern,
        out_shape=[stats, stats],
        in_specs=[VMEM] * len(operands),
        out_specs=[VMEM, VMEM],
        scratch_shapes=[
            pltpu.VMEM((ntgt * cells, 2 * chans), jnp.bfloat16),
            pltpu.VMEM((nsrc * cells, width), jnp.float32),
            pltpu.VMEM((nsrc * cells, width), jnp.float32),
            pltpu.VMEM((ntgt, 8, cells), jnp.float32),
            pltpu.VMEM((ntgt, 8, cells), jnp.float32),
            pltpu.VMEM((ntgt, 8, cells), jnp.float32),
            pltpu.VMEM((nsrc * cells, width), jnp.float32),
            pltpu.VMEM((ntgt, 8, cells), jnp.float32),
        ],
        compiler_params=pltpu.CompilerParams(vmem_limit_bytes=16 << 20),
        cost_estimate=pl.CostEstimate(
            flops=2_000_000_000 * pairs, bytes_accessed=1_300_000 * pairs, transcendentals=4_200_000 * pairs
        ),
    )(*operands)


def merge_kernel(*refs, band_rows, width):
    out = refs[2]
    band = (lax.axis_index("bh") * SIZES[3] + lax.axis_index("bz")) * SIZES[4] + lax.axis_index("bc")
    col = (2 * lax.broadcasted_iota(jnp.int32, (band_rows, width), 1) - (width - 1)).astype(jnp.float32) * (1.0 / width)
    row = lax.broadcasted_iota(jnp.int32, (band_rows, width), 0) + band * band_rows
    row = (2 * row - 63).astype(jnp.float32) * (1.0 / 64)
    for p in range(out.shape[0]):
        for way in range(2):
            part = [refs[way][n, p] for n in range(4)]
            get = [[x[k * band_rows : (k + 1) * band_rows] for x in part] for k in range(4)]
            top = functools.reduce(jnp.maximum, get[0])
            scale = [jnp.exp2(m - top) for m in get[0]]
            total, cols, rows = (sum(v * s for v, s in zip(get[k], scale)) for k in (1, 2, 3))
            out[p, way, 0] = cols / total - col
            out[p, way, 1] = rows / total - row


def merge(fwd, rev, band_rows, width):
    pairs = fwd.shape[1]
    return pl.pallas_call(
        functools.partial(merge_kernel, band_rows=band_rows, width=width),
        out_shape=jax.ShapeDtypeStruct((pairs, 2, 2, band_rows, width), jnp.float32),
        in_specs=[VMEM] * 2,
        out_specs=VMEM,
        compiler_params=pltpu.CompilerParams(vmem_limit_bytes=4 << 20),
    )(fwd, rev)


def refine_kernel(weight, bias, before, own, after, out, *cur, layers):
    pairs, ways, comps, band_rows, width = own.shape
    high = 16
    total = pairs * ways * high
    band = (lax.axis_index("bh") * SIZES[3] + lax.axis_index("bz")) * SIZES[4] + lax.axis_index("bc")
    last = SIZES[2] * SIZES[3] * SIZES[4] - 1
    for i in range(comps):
        for p in range(pairs):
            for d in range(ways):
                base = (p * ways + d) * high
                cur[i][base : base + band_rows] = before[p, d, i]
                cur[i][base + band_rows : base + 2 * band_rows] = own[p, d, i]
                cur[i][base + 2 * band_rows : base + 3 * band_rows] = after[p, d, i]
                cur[i][base + 3 * band_rows : base + high] = jnp.zeros((high - 3 * band_rows, width), jnp.float32)
    row = lax.broadcasted_iota(jnp.int32, (total, width), 0) & (high - 1)
    lane = lax.broadcasted_iota(jnp.int32, (total, width), 1)
    low = jnp.where(band == 0, band_rows, 0)
    top = jnp.where(band == last, 2 * band_rows, 3 * band_rows)
    inside = ((row >= low) & (row < top)).astype(jnp.float32)
    keep_left = (lane > 0).astype(jnp.float32)
    keep_right = (lane < width - 1).astype(jnp.float32)
    for layer in range(layers):
        taps = []
        for i in range(comps):
            act = jnp.tanh(2.0 * cur[i][...]) * inside
            taps.append((pltpu.roll(act, 1, 1) * keep_left, act, pltpu.roll(act, width - 1, 1) * keep_right))
        for o in range(comps):
            lines = []
            for r in range(3):
                line = None
                for i in range(comps):
                    for c in range(3):
                        term = taps[i][c] * weight[(((layer * comps + o) * comps + i) * 3 + r) * 3 + c]
                        line = term if line is None else line + term
                lines.append(line)
            grown = pltpu.roll(lines[0], 1, 0) + lines[1] + pltpu.roll(lines[2], total - 1, 0)
            cur[o][...] = cur[o][...] + (grown + bias[layer * comps + o])
    for i in range(comps):
        for p in range(pairs):
            for d in range(ways):
                base = (p * ways + d) * high + band_rows
                out[p, d, i] = cur[i][base : base + band_rows]


def refine(weight, bias, before, own, after):
    pairs, ways, comps, _, width = own.shape
    return pl.pallas_call(
        functools.partial(refine_kernel, layers=weight.shape[0]),
        out_shape=jax.ShapeDtypeStruct(own.shape, jnp.float32),
        in_specs=[SMEM, SMEM, VMEM, VMEM, VMEM],
        out_specs=VMEM,
        scratch_shapes=[pltpu.VMEM((pairs * ways * 16, width), jnp.float32)] * comps,
        compiler_params=pltpu.CompilerParams(vmem_limit_bytes=4 << 20),
    )(weight.reshape(-1), bias.reshape(-1), before, own, after)


def gather_frames(blocks):
    orders = ((flip_y, flip_a, flip_b), (flip_a, flip_b, flip_y), (flip_b, flip_y, flip_a))
    held = [[block] for block in blocks]
    for stage in range(3):
        send = [have[0] if len(have) == 1 else jnp.concatenate(have, axis=0) for have in held]
        got = [hop(part, order[stage]) for part, order in zip(send, orders)]
        got = lax.optimization_barrier(got)
        for have, piece in zip(held, got):
            have.append(piece)
    return held


def spread(src0, tgt0):
    src1 = hop(src0, flip_h)
    src3 = hop(src0, flip_hc)
    tgt3 = hop(tgt0, turn_z(2))
    tgt1 = hop(tgt0, turn_z(1))
    tgt2 = hop(tgt0, turn_z(-1))
    src2 = hop(src0, flip_c)
    return [[src0], [src1], [src2], [src3]], [[tgt0], [tgt1], [tgt2], [tgt3]]


def shards(features, frame_pairs, conv_weight, conv_bias):
    frames, band_rows, width, chans = features.shape
    pairs = frame_pairs.shape[0]
    cells = band_rows * width
    flat_features = features.reshape(frames, cells, chans)
    held = gather_frames([flat_features[v : v + 1] for v in range(frames)])
    sizes = (1, pairs - 1)
    picked = pick(frame_pairs, held, sizes)
    stats = None
    parts = [spread(picked[2 * n], picked[2 * n + 1]) for n in range(2)]
    for part in parts:
        stats = match(*part, earlier=stats)
    fwd, rev = stats
    fwd = lax.all_to_all(fwd, ("bh", "bc"), 0, 0)
    rev = lax.all_to_all(rev, "bz", 0, 0)
    flows = merge(fwd, rev, band_rows, width)
    before = hop(flows, next_band(1))
    after = hop(flows, next_band(-1))
    return refine(conv_weight, conv_bias, before, flows, after)


def solution(mesh):
    finer = Mesh(mesh.devices.reshape(SIZES), AXES)
    frame, band = AXES[:2], AXES[2:]
    placed = (P(frame, band, None, None), P(frame, None), P(), P())
    return jax.shard_map(
        shards,
        mesh=finer,
        in_specs=placed,
        out_specs=P(frame, None, None, band, None),
        check_vma=False,
    )
```

```python
import functools
import itertools
import math

import jax
import jax.numpy as jnp
from jax import lax
from jax.experimental import pallas as pl
from jax.experimental.pallas import tpu as pltpu
from jax.sharding import Mesh
from jax.sharding import PartitionSpec as P

score_gain = 2.5
AXES = ("fx", "fy", "bh", "bz", "bc")
SIZES = (4, 2, 2, 4, 2)
VMEM = pl.BlockSpec(memory_space=pltpu.VMEM)
SMEM = pl.BlockSpec(memory_space=pltpu.SMEM)
ANY = pl.BlockSpec(memory_space=pl.ANY)


def flat(coords):
    index = 0
    for value, size in zip(coords, SIZES):
        index = index * size + value
    return index


def hop(value, move):
    route = []
    for coords in itertools.product(*(range(size) for size in SIZES)):
        target = move(*coords)
        if target is not None:
            route.append((flat(coords), flat(target)))
    return lax.ppermute(value, AXES, route)


def flip_y(x, y, h, z, c):
    return x, 1 - y, h, z, c


def flip_a(x, y, h, z, c):
    return x ^ 1, y, h, z, c


def flip_b(x, y, h, z, c):
    return 3 - x, y, h, z, c


def flip_h(x, y, h, z, c):
    return x, y, 1 - h, z, c


def flip_c(x, y, h, z, c):
    return x, y, h, z, 1 - c


def flip_za(x, y, h, z, c):
    return x, y, h, z ^ 1, c


def flip_zb(x, y, h, z, c):
    return x, y, h, 3 - z, c


def ring(x, y, h, z, c):
    return x, y, h, (z + 1 - 2 * c) % SIZES[3], c


def back(x, y, h, z, c):
    return x, y, h, (z - 1 + 2 * c) % SIZES[3], c


def by_core(first, second):
    def move(*coords):
        return (second if coords[4] else first)(*coords)

    return move


def next_band(step):
    def move(x, y, h, z, c):
        band = (h * SIZES[3] + z) * SIZES[4] + c + step
        if band < 0 or band >= SIZES[2] * SIZES[3] * SIZES[4]:
            return None
        return x, y, band // (SIZES[3] * SIZES[4]), band // SIZES[4] % SIZES[3], band % SIZES[4]

    return move


def gray(x):
    return (x ^ (x >> 1)) & 1, x >> 1


def pick_kernel(table_ref, *refs, counts):
    pieces = [refs[4 * v : 4 * v + 4] for v in range(len(counts))]
    outs = refs[4 * len(counts) :]
    me_x, me_y, core = lax.axis_index("fx"), lax.axis_index("fy"), lax.axis_index("bc")
    me_a, me_b = gray(me_x)
    frames = sum(counts)
    for slot in range(outs[0].shape[0]):
        for side in range(2):
            frame = table_ref[slot, side]
            which, group = frame % frames, frame // frames
            to_a, to_b = gray(group // 2)
            fa, fb, fy = to_a ^ me_a, to_b ^ me_b, (group % 2) ^ me_y
            other = core == 1
            first = (jnp.where(other, fb, fy), jnp.where(other, fy, fa), jnp.where(other, fa, fb))
            low_frame = 0
            for v, bits in enumerate((first, (fa, fb, fy))):
                count = counts[v]
                place = bits[0] + 2 * bits[1] + 4 * bits[2]
                mine = (which >= low_frame) & (which < low_frame + count)
                for m, (low, span) in enumerate(((0, 1), (1, 1), (2, 2), (4, 4))):

                    @pl.when(mine & (place >= low) & (place < low + span))
                    def _():
                        outs[side][slot] = pieces[v][m][(place - low) * count + which - low_frame]

                low_frame += count


def pick(table, held, counts):
    block = held[0][0].shape[1:]
    pieces = [piece for have in held for piece in have]
    shape = jax.ShapeDtypeStruct((table.shape[0],) + block, pieces[0].dtype)
    return pl.pallas_call(
        functools.partial(pick_kernel, counts=counts),
        out_shape=[shape, shape],
        in_specs=[SMEM] + [VMEM] * len(pieces),
        out_specs=[VMEM, VMEM],
        compiler_params=pltpu.CompilerParams(vmem_limit_bytes=12 << 20),
    )(table, *pieces)


def match_kernel(*refs, nsrc, ntgt, cells, width):
    src, tgt = refs[:nsrc], refs[nsrc : nsrc + ntgt]
    fwd_keep, fwd_send, rev_keep, rev_send, rev, rhs, acc, accy, g0, gq, gy, shift_r, shift_c = refs[nsrc + ntgt :]
    fwd = [(fwd_keep, 0), (fwd_keep, 1), (fwd_send, 0), (fwd_send, 1)]
    h, z, core = lax.axis_index("bh"), lax.axis_index("bz"), lax.axis_index("bc")
    band_rows = cells // width
    pairs = src[0].shape[0]
    span = nsrc
    src_place = [(h, core), (1 - h, core), (h, 1 - core), (1 - h, 1 - core)]
    src_band = [(hh * SIZES[3] + z) * SIZES[4] + cc for hh, cc in src_place]
    step = 1 - 2 * core
    tgt_z = [z, (z - step) % SIZES[3], (z + step) % SIZES[3], (z + 2) % SIZES[3]]
    tgt_band = [(h * SIZES[3] + zz) * SIZES[4] + core for zz in tgt_z]
    tgt_slot = [jnp.where(zz == z, 0, jnp.where(zz == 3 - z, 1, jnp.where(zz == (z ^ 1), 2, 3))) for zz in tgt_z]
    chans = src[0].shape[-1]
    groups = width // 8
    scale = score_gain / math.sqrt(chans) * math.log2(math.e)
    nt = (((1,), (1,)), ((), ()))
    lane = lax.broadcasted_iota(jnp.int32, (16, width), 1)
    row16 = lax.broadcasted_iota(jnp.int32, (16, width), 0)
    pick = jnp.where(row16 == 0, 1.0, jnp.where(row16 == 1, (2 * lane - (width - 1)).astype(jnp.float32), 0.0)).astype(jnp.bfloat16)
    pick = jnp.concatenate([pick, pick], axis=1)
    sub = lax.broadcasted_iota(jnp.int32, (8, width), 0).astype(jnp.float32)

    def place(band):
        return (band * band_rows).astype(jnp.float32) - 27.5

    def block(jb, p, mode):
        yj = place(functools.reduce(lambda x, j: jnp.where(jb == j, tgt_band[j], x), range(1, ntgt), tgt_band[0]))
        b = rhs[pl.ds(pl.multiple_of(jb * cells, cells), cells), :]
        for lo in range(0, nsrc, span):
            parts = [src[i][p] for i in range(lo, lo + span)]
            a = jnp.concatenate(parts, axis=0) if span > 1 else parts[0]
            s = lax.dot_general(jnp.concatenate([a, a], axis=1), b, nt, preferred_element_type=jnp.float32)
            for i in range(span):
                yi = place(src_band[lo + i])
                tt = [None] * band_rows
                uu = [None] * band_rows
                xx = [None] * band_rows
                for q in range(band_rows):
                    ps = [None] * band_rows
                    qs = [None] * band_rows
                    for k in range(groups):
                        r0 = i * cells + q * width + k * 8
                        t = [s[r0:r0 + 8, c * width:(c + 1) * width] for c in range(band_rows)]
                        rsl = slice(lo * cells + r0, lo * cells + r0 + 8)
                        if mode == 0:
                            w = [jnp.exp2(v) for v in t]
                            v = w
                        else:
                            m = shift_r[rsl, :]
                            w = [jnp.exp2(x - m) for x in t]
                            v = [jnp.exp2(x - shift_c[jb, :, c * width:(c + 1) * width]) for c, x in enumerate(t)]
                        a1 = w[0]
                        b1 = w[0]
                        for c in range(1, band_rows):
                            a1 = a1 + w[c]
                            b1 = b1 + a1
                        acc[rsl, :] = acc[rsl, :] + a1
                        accy[rsl, :] = accy[rsl, :] + (yj * a1 - b1)
                        for c in range(band_rows):
                            ps[c] = v[c] if k == 0 else ps[c] + v[c]
                            qs[c] = ps[c] if k == 0 else qs[c] + ps[c]
                    for c in range(band_rows):
                        tt[c] = ps[c] if q == 0 else tt[c] + ps[c]
                        uu[c] = tt[c] if q == 0 else uu[c] + tt[c]
                        xx[c] = qs[c] if q == 0 else xx[c] + qs[c]
                for c in range(band_rows):
                    cs = slice(c * width, (c + 1) * width)
                    if lo + i == 0:
                        g0[jb, :, cs] = tt[c]
                        gy[jb, :, cs] = yi * tt[c] - uu[c]
                        gq[jb, :, cs] = xx[c]
                    else:
                        g0[jb, :, cs] = g0[jb, :, cs] + tt[c]
                        gy[jb, :, cs] = gy[jb, :, cs] + (yi * tt[c] - uu[c])
                        gq[jb, :, cs] = gq[jb, :, cs] + xx[c]

    def sweep(p, mode):
        acc[...] = jnp.zeros_like(acc)
        accy[...] = jnp.zeros_like(accy)
        def body(jb, c):
            block(jb, p, mode)
            return c
        lax.fori_loop(0, ntgt, body, 0)

    def emit(at, shift_f, shift_b):
        ok = None
        for i in range(nsrc):
            sl = slice(i * cells, (i + 1) * cells)
            def lanes(ref):
                x = ref[sl, :]
                hi = x.astype(jnp.bfloat16)
                lo = (x - hi.astype(jnp.float32)).astype(jnp.bfloat16)
                both = jnp.concatenate([hi, lo], axis=1)
                return lax.dot_general(pick, both, nt, preferred_element_type=jnp.float32)
            one = lanes(acc)
            two = lanes(accy)
            tot = one[0:1]
            good = jnp.all((tot > 2.0 ** -90) & (tot < 2.0 ** 110))
            ok = good if ok is None else ok & good
            for r in range(band_rows):
                cs = slice(r * width, (r + 1) * width)
                fwd[i][0][fwd[i][1], at, band_rows + r:band_rows + r + 1, :] = one[0:1, cs]
                fwd[i][0][fwd[i][1], at, 2 * band_rows + r:2 * band_rows + r + 1, :] = one[1:2, cs] * (1.0 / width)
                fwd[i][0][fwd[i][1], at, 3 * band_rows + r:3 * band_rows + r + 1, :] = two[0:1, cs] * (1.0 / 32)
            if shift_f is None:
                fwd[i][0][fwd[i][1], at, 0:band_rows, :] = jnp.zeros((band_rows, width), jnp.float32)
            else:
                shift_f(i)
        for j in range(ntgt):
            for r in range(band_rows):
                cs = slice(r * width, (r + 1) * width)
                t = g0[j, :, cs]
                x = (129.0 + 2.0 * sub) * t - 16.0 * gq[j, :, cs]
                tot = jnp.sum(t, axis=0, keepdims=True)
                ok = ok & jnp.all((tot > 2.0 ** -90) & (tot < 2.0 ** 110))
                rev[tgt_slot[j], at, band_rows + r:band_rows + r + 1, :] = tot
                rev[tgt_slot[j], at, 2 * band_rows + r:2 * band_rows + r + 1, :] = jnp.sum(x, axis=0, keepdims=True) * (1.0 / width)
                rev[tgt_slot[j], at, 3 * band_rows + r:3 * band_rows + r + 1, :] = jnp.sum(gy[j, :, cs], axis=0, keepdims=True) * (1.0 / 32)
                rev[tgt_slot[j], at, r:r + 1, :] = jnp.zeros((1, width), jnp.float32) if shift_b is None else shift_b[j, 0:1, cs]
        return ok

    def pair(p, carry):
        at = p
        for j in range(ntgt):
            b = tgt[j][p].astype(jnp.float32) * scale
            hi = b.astype(jnp.bfloat16)
            lo = (b - hi.astype(jnp.float32)).astype(jnp.bfloat16)
            rhs[j * cells:(j + 1) * cells, :] = jnp.concatenate([hi, lo], axis=1)
        sweep(p, 0)
        ok = emit(at, None, None)

        @pl.when(jnp.logical_not(ok))
        def _():
            shift_r[...] = jnp.full_like(shift_r, -1e30)
            shift_c[...] = jnp.full_like(shift_c, -1e30)
            def tops(jb, c):
                b = rhs[pl.ds(pl.multiple_of(jb * cells, cells), cells), :]
                for i in range(nsrc):
                    def part(q, c2):
                        a = src[i][p, pl.ds(pl.multiple_of(q * width, width), width), :]
                        s = lax.dot_general(jnp.concatenate([a, a], axis=1), b, nt, preferred_element_type=jnp.float32)
                        sl = pl.ds(pl.multiple_of(i * cells + q * width, width), width)
                        m = shift_r[sl, :]
                        for c3 in range(band_rows):
                            m = jnp.maximum(m, s[:, c3 * width:(c3 + 1) * width])
                        shift_r[sl, :] = m
                        t = shift_c[jb]
                        shift_c[jb] = jnp.maximum(t, jnp.broadcast_to(jnp.max(s, axis=0, keepdims=True), t.shape))
                        return c2
                    lax.fori_loop(0, band_rows, part, 0)
                return c
            lax.fori_loop(0, ntgt, tops, 0)
            def level(n, c):
                sl = pl.ds(pl.multiple_of(n * width, width), width)
                m = shift_r[sl, :]
                shift_r[sl, :] = jnp.broadcast_to(jnp.max(m, axis=1, keepdims=True), m.shape)
                return c
            lax.fori_loop(0, nsrc * (cells // width), level, 0)
            sweep(p, 1)
            def put(i):
                for r in range(band_rows):
                    m = shift_r[i * cells + r * width:i * cells + (r + 1) * width, :]
                    fwd[i][0][fwd[i][1], at, r:r + 1, :] = jnp.transpose(m)[0:1, :]
            emit(at, put, shift_c)

        return carry

    lax.fori_loop(0, pairs, pair, 0)
    rev_keep[...] = rev[0:2]
    rev_send[...] = rev[2:4]


def match(src, tgt):
    pairs, cells, chans = src[0].shape
    width = 128
    nsrc, ntgt = len(src), len(tgt)
    stats = jax.ShapeDtypeStruct((2, pairs, 4 * cells // width, width), jnp.float32)
    return pl.pallas_call(
        functools.partial(match_kernel, nsrc=nsrc, ntgt=ntgt, cells=cells, width=width),
        out_shape=[stats] * 4,
        in_specs=[VMEM] * (nsrc + ntgt),
        out_specs=[VMEM] * 4,
        scratch_shapes=[
            pltpu.VMEM((4,) + stats.shape[1:], jnp.float32),
            pltpu.VMEM((ntgt * cells, 2 * chans), jnp.bfloat16),
            pltpu.VMEM((nsrc * cells, width), jnp.float32),
            pltpu.VMEM((nsrc * cells, width), jnp.float32),
            pltpu.VMEM((ntgt, 8, cells), jnp.float32),
            pltpu.VMEM((ntgt, 8, cells), jnp.float32),
            pltpu.VMEM((ntgt, 8, cells), jnp.float32),
            pltpu.VMEM((nsrc * cells, width), jnp.float32),
            pltpu.VMEM((ntgt, 8, cells), jnp.float32),
        ],
        compiler_params=pltpu.CompilerParams(vmem_limit_bytes=20 << 20),
        cost_estimate=pl.CostEstimate(
            flops=2_000_000_000 * pairs, bytes_accessed=1_300_000 * pairs, transcendentals=4_200_000 * pairs
        ),
    )(*src, *tgt)


def joined(left, right, band_rows):
    part = lambda x, k: x[k * band_rows : (k + 1) * band_rows]
    top = jnp.maximum(part(left, 0), part(right, 0))
    scale_l = jnp.exp2(part(left, 0) - top)
    scale_r = jnp.exp2(part(right, 0) - top)
    return [top] + [part(left, k) * scale_l + part(right, k) * scale_r for k in range(1, 4)]


def half_kernel(fwd, fwd_in, rev, rev_in, *outs, band_rows):
    for way, (own, other) in enumerate(((fwd, fwd_in), (rev, rev_in))):
        for side in range(2):
            for p in range(own.shape[1]):
                for k, value in enumerate(joined(own[side, p], other[side, p], band_rows)):
                    outs[2 * way + side][p, k * band_rows : (k + 1) * band_rows] = value


def half(fwd, fwd_in, rev, rev_in, band_rows):
    shape = jax.ShapeDtypeStruct(fwd.shape[1:], jnp.float32)
    return pl.pallas_call(
        functools.partial(half_kernel, band_rows=band_rows),
        out_shape=[shape] * 4,
        in_specs=[VMEM] * 4,
        out_specs=[VMEM] * 4,
        compiler_params=pltpu.CompilerParams(vmem_limit_bytes=4 << 20),
    )(fwd, fwd_in, rev, rev_in)


def merge_kernel(fwd, fwd_in, rev, rev_in, out, *, band_rows, width):
    band = (lax.axis_index("bh") * SIZES[3] + lax.axis_index("bz")) * SIZES[4] + lax.axis_index("bc")
    col = (2 * lax.broadcasted_iota(jnp.int32, (band_rows, width), 1) - (width - 1)).astype(jnp.float32) * (1.0 / width)
    row = lax.broadcasted_iota(jnp.int32, (band_rows, width), 0) + band * band_rows
    row = (2 * row - 63).astype(jnp.float32) * (1.0 / 64)
    for p in range(out.shape[0]):
        for way, (own, other) in enumerate(((fwd, fwd_in), (rev, rev_in))):
            top, total, cols, rows = joined(own[p], other[p], band_rows)
            out[p, way, 0] = cols / total - col
            out[p, way, 1] = rows / total - row


def merge(fwd, fwd_in, rev, rev_in, band_rows, width):
    return pl.pallas_call(
        functools.partial(merge_kernel, band_rows=band_rows, width=width),
        out_shape=jax.ShapeDtypeStruct((fwd.shape[0], 2, 2, band_rows, width), jnp.float32),
        in_specs=[VMEM] * 4,
        out_specs=VMEM,
        compiler_params=pltpu.CompilerParams(vmem_limit_bytes=4 << 20),
    )(fwd, fwd_in, rev, rev_in)


def refine_kernel(weight, bias, before, own, after, out, *cur, layers):
    pairs, ways, comps, band_rows, width = own.shape
    high = 16
    total = pairs * ways * high
    band = (lax.axis_index("bh") * SIZES[3] + lax.axis_index("bz")) * SIZES[4] + lax.axis_index("bc")
    last = SIZES[2] * SIZES[3] * SIZES[4] - 1
    for i in range(comps):
        for p in range(pairs):
            for d in range(ways):
                base = (p * ways + d) * high
                cur[i][base : base + band_rows] = before[p, d, i]
                cur[i][base + band_rows : base + 2 * band_rows] = own[p, d, i]
                cur[i][base + 2 * band_rows : base + 3 * band_rows] = after[p, d, i]
                cur[i][base + 3 * band_rows : base + high] = jnp.zeros((high - 3 * band_rows, width), jnp.float32)
    row = lax.broadcasted_iota(jnp.int32, (total, width), 0) & (high - 1)
    lane = lax.broadcasted_iota(jnp.int32, (total, width), 1)
    low = jnp.where(band == 0, band_rows, 0)
    top = jnp.where(band == last, 2 * band_rows, 3 * band_rows)
    inside = ((row >= low) & (row < top)).astype(jnp.float32)
    keep_left = (lane > 0).astype(jnp.float32)
    keep_right = (lane < width - 1).astype(jnp.float32)
    for layer in range(layers):
        taps = []
        for i in range(comps):
            act = jnp.tanh(2.0 * cur[i][...]) * inside
            taps.append((pltpu.roll(act, 1, 1) * keep_left, act, pltpu.roll(act, width - 1, 1) * keep_right))
        for o in range(comps):
            lines = []
            for r in range(3):
                line = None
                for i in range(comps):
                    for c in range(3):
                        term = taps[i][c] * weight[(((layer * comps + o) * comps + i) * 3 + r) * 3 + c]
                        line = term if line is None else line + term
                lines.append(line)
            grown = pltpu.roll(lines[0], 1, 0) + lines[1] + pltpu.roll(lines[2], total - 1, 0)
            cur[o][...] = cur[o][...] + (grown + bias[layer * comps + o])
    for i in range(comps):
        for p in range(pairs):
            for d in range(ways):
                base = (p * ways + d) * high + band_rows
                out[p, d, i] = cur[i][base : base + band_rows]


def refine(weight, bias, before, own, after):
    pairs, ways, comps, band_rows, width = own.shape
    return pl.pallas_call(
        functools.partial(refine_kernel, layers=weight.shape[0]),
        out_shape=jax.ShapeDtypeStruct(own.shape, jnp.float32),
        in_specs=[SMEM, SMEM, VMEM, VMEM, VMEM],
        out_specs=VMEM,
        scratch_shapes=[pltpu.VMEM((pairs * ways * 16, width), jnp.float32)] * comps,
        compiler_params=pltpu.CompilerParams(vmem_limit_bytes=4 << 20),
    )(weight.reshape(-1), bias.reshape(-1), before, own, after)


def gather_frames(blocks):
    orders = (
        (by_core(flip_y, flip_b), by_core(flip_a, flip_y), by_core(flip_b, flip_a)),
        (flip_a, flip_b, flip_y),
    )
    held = [[block] for block in blocks]
    for stage in range(3):
        send = [have[0] if len(have) == 1 else jnp.concatenate(have, axis=0) for have in held]
        got = [hop(part, order[stage]) for part, order in zip(send, orders)]
        got = lax.optimization_barrier(got)
        for have, piece in zip(held, got):
            have.append(piece)
    return held


def spread(src0, tgt0):
    tgt1 = hop(tgt0, ring)
    tgt2 = hop(tgt0, back)
    src1 = hop(src0, flip_h)
    src2 = hop(src0, flip_c)
    tgt1, tgt2, src1, src2 = lax.optimization_barrier((tgt1, tgt2, src1, src2))
    tgt3 = hop(tgt1, ring)
    src3 = hop(src1, flip_c)
    return (src0, src1, src2, src3), (tgt0, tgt1, tgt2, tgt3)


def shards(features, frame_pairs, conv_weight, conv_bias):
    frames, band_rows, width, chans = features.shape
    pairs = frame_pairs.shape[0]
    cells = band_rows * width
    flat_features = features.reshape(frames, cells, chans)
    counts = (frames - 1, 1)
    held = gather_frames([flat_features[:-1], flat_features[-1:]])
    src0, tgt0 = pick(frame_pairs, held, counts)
    fwd_keep, fwd_send, rev_keep, rev_send = match(*spread(src0, tgt0))
    fwd0, fwd1, rev0, rev1 = half(fwd_keep, hop(fwd_send, flip_c), rev_keep, hop(rev_send, flip_za), band_rows)
    flows = merge(fwd0, hop(fwd1, flip_h), rev0, hop(rev1, flip_zb), band_rows, width)
    before = hop(flows, next_band(1))
    after = hop(flows, next_band(-1))
    return refine(conv_weight, conv_bias, before, flows, after)


def solution(mesh):
    finer = Mesh(mesh.devices.reshape(SIZES), AXES)
    frame, band = AXES[:2], AXES[2:]
    placed = (P(frame, band, None, None), P(frame, None), P(), P())
    return jax.shard_map(
        shards,
        mesh=finer,
        in_specs=placed,
        out_specs=P(frame, None, None, band, None),
        check_vma=False,
    )
```

```python
import functools
import itertools
import math

import jax
import jax.numpy as jnp
from jax import lax
from jax.experimental import pallas as pl
from jax.experimental.pallas import tpu as pltpu
from jax.sharding import Mesh
from jax.sharding import PartitionSpec as P

score_gain = 2.5
AXES = ("fx", "fy", "bh", "bz", "bc")
SIZES = (4, 2, 2, 4, 2)
VMEM = pl.BlockSpec(memory_space=pltpu.VMEM)
SMEM = pl.BlockSpec(memory_space=pltpu.SMEM)
NT = (((1,), (1,)), ((), ()))


def flat(coords):
    index = 0
    for value, size in zip(coords, SIZES):
        index = index * size + value
    return index


def hop(value, move):
    route = []
    for coords in itertools.product(*(range(size) for size in SIZES)):
        target = move(*coords)
        if target is not None:
            route.append((flat(coords), flat(target)))
    return lax.ppermute(value, AXES, route)


def flip_y(x, y, h, z, c):
    return x, 1 - y, h, z, c


def flip_a(x, y, h, z, c):
    return x ^ 1, y, h, z, c


def flip_b(x, y, h, z, c):
    return 3 - x, y, h, z, c


def flip_h(x, y, h, z, c):
    return x, y, 1 - h, z, c


def flip_c(x, y, h, z, c):
    return x, y, h, z, 1 - c


def flip_za(x, y, h, z, c):
    return x, y, h, z ^ 1, c


def flip_zb(x, y, h, z, c):
    return x, y, h, 3 - z, c


def ring(x, y, h, z, c):
    return x, y, h, (z + 1 - 2 * c) % SIZES[3], c


def back(x, y, h, z, c):
    return x, y, h, (z - 1 + 2 * c) % SIZES[3], c


def by_core(first, second):
    def move(*coords):
        return (second if coords[4] else first)(*coords)

    return move


def next_band(step):
    def move(x, y, h, z, c):
        band = (h * SIZES[3] + z) * SIZES[4] + c + step
        return x, y, band // (SIZES[3] * SIZES[4]) % SIZES[2], band // SIZES[4] % SIZES[3], band % SIZES[4]

    return move


def gray(x):
    return (x ^ (x >> 1)) & 1, x >> 1


def pick_kernel(table_ref, *refs, counts):
    pieces = [refs[4 * v : 4 * v + 4] for v in range(len(counts))]
    outs = refs[4 * len(counts) :]
    me_x, me_y, core = lax.axis_index("fx"), lax.axis_index("fy"), lax.axis_index("bc")
    me_a, me_b = gray(me_x)
    frames = sum(counts)
    for slot in range(outs[0].shape[0]):
        for side in range(2):
            frame = table_ref[slot, side]
            which, group = frame % frames, frame // frames
            to_a, to_b = gray(group // 2)
            fa, fb, fy = to_a ^ me_a, to_b ^ me_b, (group % 2) ^ me_y
            other = core == 1
            first = (jnp.where(other, fb, fy), jnp.where(other, fy, fa), jnp.where(other, fa, fb))
            low_frame = 0
            for v, bits in enumerate((first, (fa, fb, fy))):
                count = counts[v]
                place = bits[0] + 2 * bits[1] + 4 * bits[2]
                mine = (which >= low_frame) & (which < low_frame + count)
                for m, (low, span) in enumerate(((0, 1), (1, 1), (2, 2), (4, 4))):

                    @pl.when(mine & (place >= low) & (place < low + span))
                    def _():
                        outs[side][slot] = pieces[v][m][(place - low) * count + which - low_frame]

                low_frame += count


def pick(table, held, counts):
    block = held[0][0].shape[1:]
    pieces = [piece for have in held for piece in have]
    shape = jax.ShapeDtypeStruct((table.shape[0],) + block, pieces[0].dtype)
    return pl.pallas_call(
        functools.partial(pick_kernel, counts=counts),
        out_shape=[shape, shape],
        in_specs=[SMEM] + [VMEM] * len(pieces),
        out_specs=[VMEM, VMEM],
        compiler_params=pltpu.CompilerParams(vmem_limit_bytes=12 << 20),
    )(table, *pieces)


def targets(refs, p, scale, rhs, start, cells):
    for j, ref in enumerate(refs):
        b = ref[p].astype(jnp.float32) * scale
        hi = b.astype(jnp.bfloat16)
        lo = (b - hi.astype(jnp.float32)).astype(jnp.bfloat16)
        rhs[(start + j) * cells : (start + j + 1) * cells, :] = jnp.concatenate([hi, lo], axis=1)


def places(cells, width):
    h, z, core = lax.axis_index("bh"), lax.axis_index("bz"), lax.axis_index("bc")
    src_place = [(h, core), (1 - h, core), (h, 1 - core), (1 - h, 1 - core)]
    src_band = [(hh * SIZES[3] + z) * SIZES[4] + cc for hh, cc in src_place]
    step = 1 - 2 * core
    tgt_z = [z, (z - step) % SIZES[3], (z + step) % SIZES[3], (z + 2) % SIZES[3]]
    tgt_band = [(h * SIZES[3] + zz) * SIZES[4] + core for zz in tgt_z]
    tgt_slot = [jnp.where(zz == z, 0, jnp.where(zz == 3 - z, 1, jnp.where(zz == (z ^ 1), 2, 3))) for zz in tgt_z]
    row = lambda band: (band * (cells // width)).astype(jnp.float32) - 27.5
    return [row(band) for band in src_band], [row(band) for band in tgt_band], tgt_slot


def chosen(values, index):
    return functools.reduce(lambda x, j: jnp.where(index == j, values[j], x), range(1, len(values)), values[0])


def block(sources, b, yj, src_rows, sums, cols, cells, width, shifts=None):
    band_rows = cells // width
    groups = width // 8
    a = jnp.concatenate(sources, axis=0)
    s = lax.dot_general(jnp.concatenate([a, a], axis=1), b, NT, preferred_element_type=jnp.float32)
    put, cols_first = cols
    for i in range(len(sources)):
        tt = [None] * band_rows
        uu = [None] * band_rows
        xx = [None] * band_rows
        for q in range(band_rows):
            ps = [None] * band_rows
            qs = [None] * band_rows
            for k in range(groups):
                r0 = i * cells + q * width + k * 8
                t = [s[r0 : r0 + 8, c * width : (c + 1) * width] for c in range(band_rows)]
                rows = slice(r0, r0 + 8)
                if shifts is None:
                    w = [jnp.exp2(x) for x in t]
                    v = w
                else:
                    m = shifts[0][rows, :]
                    w = [jnp.exp2(x - m) for x in t]
                    v = [jnp.exp2(x - shifts[1](c)) for c, x in enumerate(t)]
                a1 = w[0]
                b1 = w[0]
                for c in range(1, band_rows):
                    a1 = a1 + w[c]
                    b1 = b1 + a1
                sums(rows, a1, yj * a1 - b1)
                for c in range(band_rows):
                    ps[c] = v[c] if k == 0 else ps[c] + v[c]
                    qs[c] = ps[c] if k == 0 else qs[c] + ps[c]
            for c in range(band_rows):
                tt[c] = ps[c] if q == 0 else tt[c] + ps[c]
                uu[c] = tt[c] if q == 0 else uu[c] + tt[c]
                xx[c] = qs[c] if q == 0 else xx[c] + qs[c]
        for c in range(band_rows):
            put(slice(c * width, (c + 1) * width), i == 0 and cols_first, (tt[c], xx[c], src_rows[i] * tt[c] - uu[c]))


def early_kernel(*refs, nsrc, ntgt, cells, width):
    src, tgt = refs[:nsrc], refs[nsrc : nsrc + ntgt]
    acc, accy, g0, gq, gy, rhs = refs[nsrc + ntgt :]
    src_rows, tgt_rows, _ = places(cells, width)
    scale = score_gain / math.sqrt(src[0].shape[-1]) * math.log2(math.e)

    def one(p, jb, first):
        def sums(rows, total, rowed):
            acc[p, rows, :] = total if first else acc[p, rows, :] + total
            accy[p, rows, :] = rowed if first else accy[p, rows, :] + rowed

        def put(lanes, new, values):
            for ref, value in zip((g0, gq, gy), values):
                ref[p, jb, :, lanes] = value if new else ref[p, jb, :, lanes] + value

        b = rhs[pl.ds(pl.multiple_of(jb * cells, cells), cells), :]
        yj = chosen(tgt_rows[:ntgt], jb)
        block([ref[p] for ref in src], b, yj, src_rows, sums, (put, True), cells, width)

    def pair(p, carry):
        targets(tgt, p, scale, rhs, 0, cells)
        one(p, 0, True)

        def more(jb, c):
            one(p, jb, False)
            return c

        return lax.fori_loop(1, ntgt, more, carry)

    lax.fori_loop(0, src[0].shape[0], pair, 0)


def late_kernel(*refs, nsrc, ntgt, cells, width):
    src, tgt = refs[:nsrc], refs[nsrc : nsrc + ntgt]
    acc_in, accy_in, g0_in, gq_in, gy_in, fwd_keep, fwd_send, rev_keep, rev_send, rev, rhs, acc, accy, g0, gq, gy, shift_r, shift_c = refs[
        nsrc + ntgt :
    ]
    fwd = [(fwd_keep, 0), (fwd_keep, 1), (fwd_send, 0), (fwd_send, 1)]
    band_rows = cells // width
    src_rows, tgt_rows, tgt_slot = places(cells, width)
    scale = score_gain / math.sqrt(src[0].shape[-1]) * math.log2(math.e)
    last = ntgt - 1
    lane = lax.broadcasted_iota(jnp.int32, (16, width), 1)
    row16 = lax.broadcasted_iota(jnp.int32, (16, width), 0)
    ramp = (2 * lane - (width - 1)).astype(jnp.float32)
    pick_rows = jnp.where(row16 == 0, 1.0, jnp.where(row16 == 1, ramp, 0.0)).astype(jnp.bfloat16)
    pick_rows = jnp.concatenate([pick_rows, pick_rows], axis=1)
    sub = lax.broadcasted_iota(jnp.int32, (8, width), 0).astype(jnp.float32)

    def safe(x):
        return jnp.all((x > 2.0**-90) & (x < 2.0**110))

    def lanes(ref, sl):
        x = ref[sl, :]
        hi = x.astype(jnp.bfloat16)
        lo = (x - hi.astype(jnp.float32)).astype(jnp.bfloat16)
        return lax.dot_general(pick_rows, jnp.concatenate([hi, lo], axis=1), NT, preferred_element_type=jnp.float32)

    def emit(p, cols_of, tops):
        ok = None
        for i in range(nsrc):
            sl = slice(i * cells, (i + 1) * cells)
            one = lanes(acc, sl)
            two = lanes(accy, sl)
            good = safe(one[0:1])
            ok = good if ok is None else ok & good
            ref, at = fwd[i]
            for r in range(band_rows):
                cs = slice(r * width, (r + 1) * width)
                ref[at, p, band_rows + r : band_rows + r + 1, :] = one[0:1, cs]
                ref[at, p, 2 * band_rows + r : 2 * band_rows + r + 1, :] = one[1:2, cs] * (1.0 / width)
                ref[at, p, 3 * band_rows + r : 3 * band_rows + r + 1, :] = two[0:1, cs] * (1.0 / 32)
                top = jnp.zeros((1, width), jnp.float32)
                if tops:
                    m = shift_r[i * cells + r * width : i * cells + (r + 1) * width, :]
                    top = jnp.transpose(m)[0:1, :]
                ref[at, p, r : r + 1, :] = top
        for j in range(ntgt):
            for r in range(band_rows):
                cs = slice(r * width, (r + 1) * width)
                t, xq, ty = cols_of(j, cs)
                tot = jnp.sum(t, axis=0, keepdims=True)
                ok = ok & safe(tot)
                slot = tgt_slot[j]
                x = (129.0 + 2.0 * sub) * t - 16.0 * xq
                rev[slot, p, band_rows + r : band_rows + r + 1, :] = tot
                rev[slot, p, 2 * band_rows + r : 2 * band_rows + r + 1, :] = jnp.sum(x, axis=0, keepdims=True) * (1.0 / width)
                rev[slot, p, 3 * band_rows + r : 3 * band_rows + r + 1, :] = jnp.sum(ty, axis=0, keepdims=True) * (1.0 / 32)
                rev[slot, p, r : r + 1, :] = shift_c[j, 0:1, cs] if tops else jnp.zeros((1, width), jnp.float32)
        return ok

    def put(jb):
        def inner(lane_slice, new, values):
            for ref, value in zip((g0, gq, gy), values):
                ref[jb, :, lane_slice] = value if new else ref[jb, :, lane_slice] + value

        return inner

    def pair(p, carry):
        targets(tgt[last:], p, scale, rhs, last, cells)

        def sums(rows, total, rowed):
            acc[rows, :] = acc_in[p, rows, :] + total
            accy[rows, :] = accy_in[p, rows, :] + rowed

        sources = [ref[p] for ref in src]
        b = rhs[last * cells : (last + 1) * cells, :]
        block(sources, b, tgt_rows[last], src_rows, sums, (put(last), True), cells, width)

        def cols_of(j, cs):
            if j == last:
                return g0[j, :, cs], gq[j, :, cs], gy[j, :, cs]
            return g0_in[p, j, :, cs], gq_in[p, j, :, cs], gy_in[p, j, :, cs]

        ok = emit(p, cols_of, False)

        @pl.when(jnp.logical_not(ok))
        def _():
            targets(tgt[:last], p, scale, rhs, 0, cells)
            shift_r[...] = jnp.full_like(shift_r, -1e30)
            shift_c[...] = jnp.full_like(shift_c, -1e30)

            def tops(jb, c):
                b = rhs[pl.ds(pl.multiple_of(jb * cells, cells), cells), :]
                for i in range(nsrc):

                    def part(q, c2):
                        a = src[i][p, pl.ds(pl.multiple_of(q * width, width), width), :]
                        s = lax.dot_general(jnp.concatenate([a, a], axis=1), b, NT, preferred_element_type=jnp.float32)
                        sl = pl.ds(pl.multiple_of(i * cells + q * width, width), width)
                        m = shift_r[sl, :]
                        for c3 in range(band_rows):
                            m = jnp.maximum(m, s[:, c3 * width : (c3 + 1) * width])
                        shift_r[sl, :] = m
                        t = shift_c[jb]
                        shift_c[jb] = jnp.maximum(t, jnp.broadcast_to(jnp.max(s, axis=0, keepdims=True), t.shape))
                        return c2

                    lax.fori_loop(0, band_rows, part, 0)
                return c

            lax.fori_loop(0, ntgt, tops, 0)

            def level(n, c):
                sl = pl.ds(pl.multiple_of(n * width, width), width)
                m = shift_r[sl, :]
                shift_r[sl, :] = jnp.broadcast_to(jnp.max(m, axis=1, keepdims=True), m.shape)
                return c

            lax.fori_loop(0, nsrc * band_rows, level, 0)
            acc[...] = jnp.zeros_like(acc)
            accy[...] = jnp.zeros_like(accy)

            def again(jb, c):
                def more(rows, total, rowed):
                    acc[rows, :] = acc[rows, :] + total
                    accy[rows, :] = accy[rows, :] + rowed

                shifts = (shift_r, lambda c4: shift_c[jb, :, c4 * width : (c4 + 1) * width])
                b = rhs[pl.ds(pl.multiple_of(jb * cells, cells), cells), :]
                block(sources, b, chosen(tgt_rows, jb), src_rows, more, (put(jb), True), cells, width, shifts)
                return c

            lax.fori_loop(0, ntgt, again, 0)
            emit(p, lambda j, cs: (g0[j, :, cs], gq[j, :, cs], gy[j, :, cs]), True)

        return carry

    lax.fori_loop(0, src[0].shape[0], pair, 0)
    rev_keep[...] = rev[0:2]
    rev_send[...] = rev[2:4]


def cost(pairs, blocks):
    return pl.CostEstimate(
        flops=134_000_000 * pairs * blocks, bytes_accessed=100_000 * pairs * blocks, transcendentals=262_144 * pairs * blocks
    )


def match_early(src, tgt):
    pairs, cells, chans = src[0].shape
    width = 128
    nsrc, ntgt = len(src), len(tgt)
    rows = jax.ShapeDtypeStruct((pairs, nsrc * cells, width), jnp.float32)
    cols = jax.ShapeDtypeStruct((pairs, ntgt, 8, cells), jnp.float32)
    return pl.pallas_call(
        functools.partial(early_kernel, nsrc=nsrc, ntgt=ntgt, cells=cells, width=width),
        out_shape=[rows, rows, cols, cols, cols],
        in_specs=[VMEM] * (nsrc + ntgt),
        out_specs=[VMEM] * 5,
        scratch_shapes=[pltpu.VMEM((ntgt * cells, 2 * chans), jnp.bfloat16)],
        compiler_params=pltpu.CompilerParams(vmem_limit_bytes=16 << 20),
        cost_estimate=cost(pairs, nsrc * ntgt),
    )(*src, *tgt)


def match_late(src, tgt, early):
    pairs, cells, chans = src[0].shape
    width = 128
    nsrc, ntgt = len(src), len(tgt)
    stats = jax.ShapeDtypeStruct((2, pairs, 4 * cells // width, width), jnp.float32)
    return pl.pallas_call(
        functools.partial(late_kernel, nsrc=nsrc, ntgt=ntgt, cells=cells, width=width),
        out_shape=[stats] * 4,
        in_specs=[VMEM] * (nsrc + ntgt + 5),
        out_specs=[VMEM] * 4,
        scratch_shapes=[
            pltpu.VMEM((4,) + stats.shape[1:], jnp.float32),
            pltpu.VMEM((ntgt * cells, 2 * chans), jnp.bfloat16),
            pltpu.VMEM((nsrc * cells, width), jnp.float32),
            pltpu.VMEM((nsrc * cells, width), jnp.float32),
            pltpu.VMEM((ntgt, 8, cells), jnp.float32),
            pltpu.VMEM((ntgt, 8, cells), jnp.float32),
            pltpu.VMEM((ntgt, 8, cells), jnp.float32),
            pltpu.VMEM((nsrc * cells, width), jnp.float32),
            pltpu.VMEM((ntgt, 8, cells), jnp.float32),
        ],
        compiler_params=pltpu.CompilerParams(vmem_limit_bytes=24 << 20),
        cost_estimate=cost(pairs, nsrc),
    )(*src, *tgt, *early)


def joined(left, right, band_rows):
    part = lambda x, k: x[k * band_rows : (k + 1) * band_rows]
    top = jnp.maximum(part(left, 0), part(right, 0))
    scale_l = jnp.exp2(part(left, 0) - top)
    scale_r = jnp.exp2(part(right, 0) - top)
    return [top] + [part(left, k) * scale_l + part(right, k) * scale_r for k in range(1, 4)]


def half_kernel(fwd, fwd_in, rev, rev_in, *outs, band_rows):
    for way, (own, other) in enumerate(((fwd, fwd_in), (rev, rev_in))):
        for side in range(2):
            for p in range(own.shape[1]):
                for k, value in enumerate(joined(own[side, p], other[side, p], band_rows)):
                    outs[2 * way + side][p, k * band_rows : (k + 1) * band_rows] = value


def half(fwd, fwd_in, rev, rev_in, band_rows):
    shape = jax.ShapeDtypeStruct(fwd.shape[1:], jnp.float32)
    return pl.pallas_call(
        functools.partial(half_kernel, band_rows=band_rows),
        out_shape=[shape] * 4,
        in_specs=[VMEM] * 4,
        out_specs=[VMEM] * 4,
        compiler_params=pltpu.CompilerParams(vmem_limit_bytes=4 << 20),
    )(fwd, fwd_in, rev, rev_in)


def merge_kernel(fwd, fwd_in, rev, rev_in, out, *, band_rows, width):
    band = (lax.axis_index("bh") * SIZES[3] + lax.axis_index("bz")) * SIZES[4] + lax.axis_index("bc")
    col = (2 * lax.broadcasted_iota(jnp.int32, (band_rows, width), 1) - (width - 1)).astype(jnp.float32) * (1.0 / width)
    row = lax.broadcasted_iota(jnp.int32, (band_rows, width), 0) + band * band_rows
    row = (2 * row - 63).astype(jnp.float32) * (1.0 / 64)
    for p in range(out.shape[0]):
        for way, (own, other) in enumerate(((fwd, fwd_in), (rev, rev_in))):
            top, total, cols, rows = joined(own[p], other[p], band_rows)
            out[p, way, 0] = cols / total - col
            out[p, way, 1] = rows / total - row


def merge(fwd, fwd_in, rev, rev_in, band_rows, width):
    return pl.pallas_call(
        functools.partial(merge_kernel, band_rows=band_rows, width=width),
        out_shape=jax.ShapeDtypeStruct((fwd.shape[0], 2, 2, band_rows, width), jnp.float32),
        in_specs=[VMEM] * 4,
        out_specs=VMEM,
        compiler_params=pltpu.CompilerParams(vmem_limit_bytes=4 << 20),
    )(fwd, fwd_in, rev, rev_in)


def refine_kernel(weight, bias, before, own, after, out, *cur, layers):
    pairs, ways, comps, band_rows, width = own.shape
    high = 16
    total = pairs * ways * high
    band = (lax.axis_index("bh") * SIZES[3] + lax.axis_index("bz")) * SIZES[4] + lax.axis_index("bc")
    last = SIZES[2] * SIZES[3] * SIZES[4] - 1
    for i in range(comps):
        for p in range(pairs):
            for d in range(ways):
                base = (p * ways + d) * high
                cur[i][base : base + band_rows] = before[p, d, i]
                cur[i][base + band_rows : base + 2 * band_rows] = own[p, d, i]
                cur[i][base + 2 * band_rows : base + 3 * band_rows] = after[p, d, i]
                cur[i][base + 3 * band_rows : base + high] = jnp.zeros((high - 3 * band_rows, width), jnp.float32)
    row = lax.broadcasted_iota(jnp.int32, (total, width), 0) & (high - 1)
    lane = lax.broadcasted_iota(jnp.int32, (total, width), 1)
    low = jnp.where(band == 0, band_rows, 0)
    top = jnp.where(band == last, 2 * band_rows, 3 * band_rows)
    inside = ((row >= low) & (row < top)).astype(jnp.float32)
    keep_left = (lane > 0).astype(jnp.float32)
    keep_right = (lane < width - 1).astype(jnp.float32)
    for layer in range(layers):
        taps = []
        for i in range(comps):
            act = jnp.tanh(2.0 * cur[i][...]) * inside
            taps.append((pltpu.roll(act, 1, 1) * keep_left, act, pltpu.roll(act, width - 1, 1) * keep_right))
        for o in range(comps):
            lines = []
            for r in range(3):
                line = None
                for i in range(comps):
                    for c in range(3):
                        term = taps[i][c] * weight[(((layer * comps + o) * comps + i) * 3 + r) * 3 + c]
                        line = term if line is None else line + term
                lines.append(line)
            grown = pltpu.roll(lines[0], 1, 0) + lines[1] + pltpu.roll(lines[2], total - 1, 0)
            cur[o][...] = cur[o][...] + (grown + bias[layer * comps + o])
    for i in range(comps):
        for p in range(pairs):
            for d in range(ways):
                base = (p * ways + d) * high + band_rows
                out[p, d, i] = cur[i][base : base + band_rows]


def refine(weight, bias, before, own, after):
    pairs, ways, comps, band_rows, width = own.shape
    return pl.pallas_call(
        functools.partial(refine_kernel, layers=weight.shape[0]),
        out_shape=jax.ShapeDtypeStruct(own.shape, jnp.float32),
        in_specs=[SMEM, SMEM, VMEM, VMEM, VMEM],
        out_specs=VMEM,
        scratch_shapes=[pltpu.VMEM((pairs * ways * 16, width), jnp.float32)] * comps,
        compiler_params=pltpu.CompilerParams(vmem_limit_bytes=4 << 20),
    )(weight.reshape(-1), bias.reshape(-1), before, own, after)


def gather_frames(blocks):
    orders = (
        (by_core(flip_y, flip_b), by_core(flip_a, flip_y), by_core(flip_b, flip_a)),
        (flip_a, flip_b, flip_y),
    )
    held = [[block] for block in blocks]
    for stage in range(3):
        send = [have[0] if len(have) == 1 else jnp.concatenate(have, axis=0) for have in held]
        got = [hop(part, order[stage]) for part, order in zip(send, orders)]
        got = lax.optimization_barrier(got)
        for have, piece in zip(held, got):
            have.append(piece)
    return held


def matched(src0, tgt0):
    tgt1 = hop(tgt0, ring)
    tgt2 = hop(tgt0, back)
    src1 = hop(src0, flip_h)
    src2 = hop(src0, flip_c)
    tgt1, tgt2, src1, src2 = lax.optimization_barrier((tgt1, tgt2, src1, src2))
    tgt3 = hop(tgt1, ring)
    src3 = hop(src1, flip_c)
    src = (src0, src1, src2, src3)
    early = match_early(src, (tgt0, tgt1, tgt2))
    return match_late(src, (tgt0, tgt1, tgt2, tgt3), early)


def shards(features, frame_pairs, conv_weight, conv_bias):
    frames, band_rows, width, chans = features.shape
    pairs = frame_pairs.shape[0]
    cells = band_rows * width
    flat_features = features.reshape(frames, cells, chans)
    counts = (frames - 1, 1)
    held = gather_frames([flat_features[:-1], flat_features[-1:]])
    src0, tgt0 = pick(frame_pairs, held, counts)
    fwd_keep, fwd_send, rev_keep, rev_send = matched(src0, tgt0)
    fwd0, fwd1, rev0, rev1 = half(fwd_keep, hop(fwd_send, flip_c), rev_keep, hop(rev_send, flip_za), band_rows)
    flows = merge(fwd0, hop(fwd1, flip_h), rev0, hop(rev1, flip_zb), band_rows, width)
    before = hop(flows, next_band(1))
    after = hop(flows, next_band(-1))
    return refine(conv_weight, conv_bias, before, flows, after)


def solution(mesh):
    finer = Mesh(mesh.devices.reshape(SIZES), AXES)
    frame, band = AXES[:2], AXES[2:]
    placed = (P(frame, band, None, None), P(frame, None), P(), P())
    return jax.shard_map(
        shards,
        mesh=finer,
        in_specs=placed,
        out_specs=P(frame, None, None, band, None),
        check_vma=False,
    )
```

```python
import functools
import itertools
import math

import jax
import jax.numpy as jnp
from jax import lax
from jax.experimental import pallas as pl
from jax.experimental.pallas import tpu as pltpu
from jax.sharding import Mesh
from jax.sharding import PartitionSpec as P

score_gain = 2.5
AXES = ("fx", "fy", "bh", "bz", "bc")
SIZES = (4, 2, 2, 4, 2)
VMEM = pl.BlockSpec(memory_space=pltpu.VMEM)
SMEM = pl.BlockSpec(memory_space=pltpu.SMEM)
NT = (((1,), (1,)), ((), ()))


def flat(coords):
    index = 0
    for value, size in zip(coords, SIZES):
        index = index * size + value
    return index


def hop(value, move):
    route = []
    for coords in itertools.product(*(range(size) for size in SIZES)):
        target = move(*coords)
        if target is not None:
            route.append((flat(coords), flat(target)))
    return lax.ppermute(value, AXES, route)


def flip_y(x, y, h, z, c):
    return x, 1 - y, h, z, c


def flip_a(x, y, h, z, c):
    return x ^ 1, y, h, z, c


def flip_b(x, y, h, z, c):
    return 3 - x, y, h, z, c


def flip_h(x, y, h, z, c):
    return x, y, 1 - h, z, c


def flip_c(x, y, h, z, c):
    return x, y, h, z, 1 - c


def flip_za(x, y, h, z, c):
    return x, y, h, z ^ 1, c


def flip_zb(x, y, h, z, c):
    return x, y, h, 3 - z, c


def ring(x, y, h, z, c):
    return x, y, h, (z + 1 - 2 * c) % SIZES[3], c


def back(x, y, h, z, c):
    return x, y, h, (z - 1 + 2 * c) % SIZES[3], c


def by_core(first, second):
    def move(*coords):
        return (second if coords[4] else first)(*coords)

    return move


def next_chip(x, y, h, z, c):
    band = (h * SIZES[3] + z) * SIZES[4] + c + 2 * c - 1
    return x, y, band // (SIZES[3] * SIZES[4]) % SIZES[2], band // SIZES[4] % SIZES[3], band % SIZES[4]


def gray(x):
    return (x ^ (x >> 1)) & 1, x >> 1


def pick_kernel(table_ref, *refs, counts):
    pieces = [refs[4 * v : 4 * v + 4] for v in range(len(counts))]
    outs = refs[4 * len(counts) :]
    me_x, me_y, core = lax.axis_index("fx"), lax.axis_index("fy"), lax.axis_index("bc")
    me_a, me_b = gray(me_x)
    frames = sum(counts)
    for slot in range(outs[0].shape[0]):
        for side in range(2):
            frame = table_ref[slot, side]
            which, group = frame % frames, frame // frames
            to_a, to_b = gray(group // 2)
            fa, fb, fy = to_a ^ me_a, to_b ^ me_b, (group % 2) ^ me_y
            other = core == 1
            first = (jnp.where(other, fb, fy), jnp.where(other, fy, fa), jnp.where(other, fa, fb))
            low_frame = 0
            for v, bits in enumerate((first, (fa, fb, fy))):
                count = counts[v]
                place = bits[0] + 2 * bits[1] + 4 * bits[2]
                mine = (which >= low_frame) & (which < low_frame + count)
                for m, (low, span) in enumerate(((0, 1), (1, 1), (2, 2), (4, 4))):

                    @pl.when(mine & (place >= low) & (place < low + span))
                    def _():
                        outs[side][slot] = pieces[v][m][(place - low) * count + which - low_frame]

                low_frame += count


def pick(table, held, counts):
    block = held[0][0].shape[1:]
    pieces = [piece for have in held for piece in have]
    shape = jax.ShapeDtypeStruct((table.shape[0],) + block, pieces[0].dtype)
    return pl.pallas_call(
        functools.partial(pick_kernel, counts=counts),
        out_shape=[shape, shape],
        in_specs=[SMEM] + [VMEM] * len(pieces),
        out_specs=[VMEM, VMEM],
        compiler_params=pltpu.CompilerParams(vmem_limit_bytes=12 << 20),
    )(table, *pieces)


def targets(refs, p, scale, rhs, start, cells):
    for j, ref in enumerate(refs):
        b = ref[p].astype(jnp.float32) * scale
        hi = b.astype(jnp.bfloat16)
        lo = (b - hi.astype(jnp.float32)).astype(jnp.bfloat16)
        rhs[(start + j) * cells : (start + j + 1) * cells, :] = jnp.concatenate([hi, lo], axis=1)


def places(cells, width):
    h, z, core = lax.axis_index("bh"), lax.axis_index("bz"), lax.axis_index("bc")
    src_place = [(h, core), (1 - h, core), (h, 1 - core), (1 - h, 1 - core)]
    src_band = [(hh * SIZES[3] + z) * SIZES[4] + cc for hh, cc in src_place]
    step = 1 - 2 * core
    tgt_z = [z, (z - step) % SIZES[3], (z + step) % SIZES[3], (z + 2) % SIZES[3]]
    tgt_band = [(h * SIZES[3] + zz) * SIZES[4] + core for zz in tgt_z]
    tgt_slot = [jnp.where(zz == z, 0, jnp.where(zz == 3 - z, 1, jnp.where(zz == (z ^ 1), 2, 3))) for zz in tgt_z]
    row = lambda band: (band * (cells // width)).astype(jnp.float32) - 27.5
    return [row(band) for band in src_band], [row(band) for band in tgt_band], tgt_slot


def chosen(values, index):
    return functools.reduce(lambda x, j: jnp.where(index == j, values[j], x), range(1, len(values)), values[0])


def block(sources, b, yj, src_rows, sums, cols, cells, width, shifts=None):
    band_rows = cells // width
    groups = width // 8
    a = jnp.concatenate(sources, axis=0)
    s = lax.dot_general(jnp.concatenate([a, a], axis=1), b, NT, preferred_element_type=jnp.float32)
    put, cols_first = cols
    for i in range(len(sources)):
        tt = [None] * band_rows
        uu = [None] * band_rows
        xx = [None] * band_rows
        for q in range(band_rows):
            ps = [None] * band_rows
            qs = [None] * band_rows
            for k in range(groups):
                r0 = i * cells + q * width + k * 8
                t = [s[r0 : r0 + 8, c * width : (c + 1) * width] for c in range(band_rows)]
                rows = slice(r0, r0 + 8)
                if shifts is None:
                    w = [jnp.exp2(x) for x in t]
                    v = w
                else:
                    m = shifts[0][rows, :]
                    w = [jnp.exp2(x - m) for x in t]
                    v = [jnp.exp2(x - shifts[1](c)) for c, x in enumerate(t)]
                a1 = w[0]
                b1 = w[0]
                for c in range(1, band_rows):
                    a1 = a1 + w[c]
                    b1 = b1 + a1
                sums(rows, a1, yj * a1 - b1)
                for c in range(band_rows):
                    ps[c] = v[c] if k == 0 else ps[c] + v[c]
                    qs[c] = ps[c] if k == 0 else qs[c] + ps[c]
            for c in range(band_rows):
                tt[c] = ps[c] if q == 0 else tt[c] + ps[c]
                uu[c] = tt[c] if q == 0 else uu[c] + tt[c]
                xx[c] = qs[c] if q == 0 else xx[c] + qs[c]
        for c in range(band_rows):
            put(slice(c * width, (c + 1) * width), i == 0 and cols_first, (tt[c], xx[c], src_rows[i] * tt[c] - uu[c]))


def early_kernel(*refs, nsrc, ntgt, cells, width):
    src, tgt = refs[:nsrc], refs[nsrc : nsrc + ntgt]
    acc, accy, g0, gq, gy, rhs = refs[nsrc + ntgt :]
    src_rows, tgt_rows, _ = places(cells, width)
    scale = score_gain / math.sqrt(src[0].shape[-1]) * math.log2(math.e)

    def one(p, jb, first):
        def sums(rows, total, rowed):
            acc[p, rows, :] = total if first else acc[p, rows, :] + total
            accy[p, rows, :] = rowed if first else accy[p, rows, :] + rowed

        def put(lanes, new, values):
            for ref, value in zip((g0, gq, gy), values):
                ref[p, jb, :, lanes] = value if new else ref[p, jb, :, lanes] + value

        b = rhs[jb * cells : (jb + 1) * cells, :]
        block([ref[p] for ref in src], b, tgt_rows[jb], src_rows, sums, (put, True), cells, width)

    def pair(p, carry):
        targets(tgt, p, scale, rhs, 0, cells)
        one(p, 0, True)

        for jb in range(1, ntgt):
            one(p, jb, False)
        return carry

    lax.fori_loop(0, src[0].shape[0], pair, 0)


def late_kernel(*refs, nsrc, ntgt, cells, width):
    src, tgt = refs[:nsrc], refs[nsrc : nsrc + ntgt]
    acc_in, accy_in, g0_in, gq_in, gy_in, fwd_keep, fwd_send, rev_keep, rev_send, rev, rhs, acc, accy, g0, gq, gy, shift_r, shift_c = refs[
        nsrc + ntgt :
    ]
    fwd = [(fwd_keep, 0), (fwd_keep, 1), (fwd_send, 0), (fwd_send, 1)]
    band_rows = cells // width
    src_rows, tgt_rows, tgt_slot = places(cells, width)
    scale = score_gain / math.sqrt(src[0].shape[-1]) * math.log2(math.e)
    early = g0_in.shape[1]
    lane = lax.broadcasted_iota(jnp.int32, (16, width), 1)
    row16 = lax.broadcasted_iota(jnp.int32, (16, width), 0)
    ramp = (2 * lane - (width - 1)).astype(jnp.float32)
    pick_rows = jnp.where(row16 == 0, 1.0, jnp.where(row16 == 1, ramp, 0.0)).astype(jnp.bfloat16)
    pick_rows = jnp.concatenate([pick_rows, pick_rows], axis=1)
    sub = lax.broadcasted_iota(jnp.int32, (8, width), 0).astype(jnp.float32)

    def safe(x):
        return jnp.all((x > 2.0**-90) & (x < 2.0**110))

    def lanes(ref, sl):
        x = ref[sl, :]
        hi = x.astype(jnp.bfloat16)
        lo = (x - hi.astype(jnp.float32)).astype(jnp.bfloat16)
        return lax.dot_general(pick_rows, jnp.concatenate([hi, lo], axis=1), NT, preferred_element_type=jnp.float32)

    def emit(p, cols_of, tops):
        ok = None
        for i in range(nsrc):
            sl = slice(i * cells, (i + 1) * cells)
            one = lanes(acc, sl)
            two = lanes(accy, sl)
            good = safe(one[0:1])
            ok = good if ok is None else ok & good
            ref, at = fwd[i]
            for r in range(band_rows):
                cs = slice(r * width, (r + 1) * width)
                ref[at, p, band_rows + r : band_rows + r + 1, :] = one[0:1, cs]
                ref[at, p, 2 * band_rows + r : 2 * band_rows + r + 1, :] = one[1:2, cs] * (1.0 / width)
                ref[at, p, 3 * band_rows + r : 3 * band_rows + r + 1, :] = two[0:1, cs] * (1.0 / 32)
                top = jnp.zeros((1, width), jnp.float32)
                if tops:
                    m = shift_r[i * cells + r * width : i * cells + (r + 1) * width, :]
                    top = jnp.transpose(m)[0:1, :]
                ref[at, p, r : r + 1, :] = top
        for j in range(ntgt):
            for r in range(band_rows):
                cs = slice(r * width, (r + 1) * width)
                t, xq, ty = cols_of(j, cs)
                tot = jnp.sum(t, axis=0, keepdims=True)
                ok = ok & safe(tot)
                slot = tgt_slot[j]
                x = (129.0 + 2.0 * sub) * t - 16.0 * xq
                rev[slot, p, band_rows + r : band_rows + r + 1, :] = tot
                rev[slot, p, 2 * band_rows + r : 2 * band_rows + r + 1, :] = jnp.sum(x, axis=0, keepdims=True) * (1.0 / width)
                rev[slot, p, 3 * band_rows + r : 3 * band_rows + r + 1, :] = jnp.sum(ty, axis=0, keepdims=True) * (1.0 / 32)
                rev[slot, p, r : r + 1, :] = shift_c[j, 0:1, cs] if tops else jnp.zeros((1, width), jnp.float32)
        return ok

    def put(jb):
        def inner(lane_slice, new, values):
            for ref, value in zip((g0, gq, gy), values):
                ref[jb, :, lane_slice] = value if new else ref[jb, :, lane_slice] + value

        return inner

    def pair(p, carry):
        targets(tgt[early:], p, scale, rhs, early, cells)
        sources = [ref[p] for ref in src]
        for jb in range(early, ntgt):

            def sums(rows, total, rowed):
                acc[rows, :] = (acc_in[p, rows, :] if jb == early else acc[rows, :]) + total
                accy[rows, :] = (accy_in[p, rows, :] if jb == early else accy[rows, :]) + rowed

            b = rhs[jb * cells : (jb + 1) * cells, :]
            block(sources, b, tgt_rows[jb], src_rows, sums, (put(jb), True), cells, width)

        def cols_of(j, cs):
            if j >= early:
                return g0[j, :, cs], gq[j, :, cs], gy[j, :, cs]
            return g0_in[p, j, :, cs], gq_in[p, j, :, cs], gy_in[p, j, :, cs]

        ok = emit(p, cols_of, False)

        @pl.when(jnp.logical_not(ok))
        def _():
            targets(tgt[:early], p, scale, rhs, 0, cells)
            shift_r[...] = jnp.full_like(shift_r, -1e30)
            shift_c[...] = jnp.full_like(shift_c, -1e30)

            def tops(jb, c):
                b = rhs[pl.ds(pl.multiple_of(jb * cells, cells), cells), :]
                for i in range(nsrc):

                    def part(q, c2):
                        a = src[i][p, pl.ds(pl.multiple_of(q * width, width), width), :]
                        s = lax.dot_general(jnp.concatenate([a, a], axis=1), b, NT, preferred_element_type=jnp.float32)
                        sl = pl.ds(pl.multiple_of(i * cells + q * width, width), width)
                        m = shift_r[sl, :]
                        for c3 in range(band_rows):
                            m = jnp.maximum(m, s[:, c3 * width : (c3 + 1) * width])
                        shift_r[sl, :] = m
                        t = shift_c[jb]
                        shift_c[jb] = jnp.maximum(t, jnp.broadcast_to(jnp.max(s, axis=0, keepdims=True), t.shape))
                        return c2

                    lax.fori_loop(0, band_rows, part, 0)
                return c

            lax.fori_loop(0, ntgt, tops, 0)

            def level(n, c):
                sl = pl.ds(pl.multiple_of(n * width, width), width)
                m = shift_r[sl, :]
                shift_r[sl, :] = jnp.broadcast_to(jnp.max(m, axis=1, keepdims=True), m.shape)
                return c

            lax.fori_loop(0, nsrc * band_rows, level, 0)
            acc[...] = jnp.zeros_like(acc)
            accy[...] = jnp.zeros_like(accy)

            def again(jb, c):
                def more(rows, total, rowed):
                    acc[rows, :] = acc[rows, :] + total
                    accy[rows, :] = accy[rows, :] + rowed

                shifts = (shift_r, lambda c4: shift_c[jb, :, c4 * width : (c4 + 1) * width])
                b = rhs[pl.ds(pl.multiple_of(jb * cells, cells), cells), :]
                block(sources, b, chosen(tgt_rows, jb), src_rows, more, (put(jb), True), cells, width, shifts)
                return c

            lax.fori_loop(0, ntgt, again, 0)
            emit(p, lambda j, cs: (g0[j, :, cs], gq[j, :, cs], gy[j, :, cs]), True)

        return carry

    lax.fori_loop(0, src[0].shape[0], pair, 0)
    rev_keep[...] = rev[0:2]
    rev_send[...] = rev[2:4]


def cost(pairs, blocks):
    return pl.CostEstimate(
        flops=134_000_000 * pairs * blocks, bytes_accessed=100_000 * pairs * blocks, transcendentals=262_144 * pairs * blocks
    )


def match_early(src, tgt):
    pairs, cells, chans = src[0].shape
    width = 128
    nsrc, ntgt = len(src), len(tgt)
    rows = jax.ShapeDtypeStruct((pairs, nsrc * cells, width), jnp.float32)
    cols = jax.ShapeDtypeStruct((pairs, ntgt, 8, cells), jnp.float32)
    return pl.pallas_call(
        functools.partial(early_kernel, nsrc=nsrc, ntgt=ntgt, cells=cells, width=width),
        out_shape=[rows, rows, cols, cols, cols],
        in_specs=[VMEM] * (nsrc + ntgt),
        out_specs=[VMEM] * 5,
        scratch_shapes=[pltpu.VMEM((ntgt * cells, 2 * chans), jnp.bfloat16)],
        compiler_params=pltpu.CompilerParams(vmem_limit_bytes=16 << 20),
        cost_estimate=cost(pairs, nsrc * ntgt),
    )(*src, *tgt)


def match_late(src, tgt, early):
    pairs, cells, chans = src[0].shape
    width = 128
    nsrc, ntgt = len(src), len(tgt)
    stats = jax.ShapeDtypeStruct((2, pairs, 4 * cells // width, width), jnp.float32)
    return pl.pallas_call(
        functools.partial(late_kernel, nsrc=nsrc, ntgt=ntgt, cells=cells, width=width),
        out_shape=[stats] * 4,
        in_specs=[VMEM] * (nsrc + ntgt + 5),
        out_specs=[VMEM] * 4,
        scratch_shapes=[
            pltpu.VMEM((4,) + stats.shape[1:], jnp.float32),
            pltpu.VMEM((ntgt * cells, 2 * chans), jnp.bfloat16),
            pltpu.VMEM((nsrc * cells, width), jnp.float32),
            pltpu.VMEM((nsrc * cells, width), jnp.float32),
            pltpu.VMEM((ntgt, 8, cells), jnp.float32),
            pltpu.VMEM((ntgt, 8, cells), jnp.float32),
            pltpu.VMEM((ntgt, 8, cells), jnp.float32),
            pltpu.VMEM((nsrc * cells, width), jnp.float32),
            pltpu.VMEM((ntgt, 8, cells), jnp.float32),
        ],
        compiler_params=pltpu.CompilerParams(vmem_limit_bytes=24 << 20),
        cost_estimate=cost(pairs, 2 * nsrc),
    )(*src, *tgt, *early)


def joined(left, right, band_rows):
    part = lambda x, k: x[k * band_rows : (k + 1) * band_rows]
    top = jnp.maximum(part(left, 0), part(right, 0))
    scale_l = jnp.exp2(part(left, 0) - top)
    scale_r = jnp.exp2(part(right, 0) - top)
    return [top] + [part(left, k) * scale_l + part(right, k) * scale_r for k in range(1, 4)]


def half_kernel(fwd, fwd_in, rev, rev_in, *outs, band_rows):
    for way, (own, other) in enumerate(((fwd, fwd_in), (rev, rev_in))):
        for side in range(2):
            for p in range(own.shape[1]):
                for k, value in enumerate(joined(own[side, p], other[side, p], band_rows)):
                    outs[2 * way + side][p, k * band_rows : (k + 1) * band_rows] = value


def half(fwd, fwd_in, rev, rev_in, band_rows):
    shape = jax.ShapeDtypeStruct(fwd.shape[1:], jnp.float32)
    return pl.pallas_call(
        functools.partial(half_kernel, band_rows=band_rows),
        out_shape=[shape] * 4,
        in_specs=[VMEM] * 4,
        out_specs=[VMEM] * 4,
        compiler_params=pltpu.CompilerParams(vmem_limit_bytes=4 << 20),
    )(fwd, fwd_in, rev, rev_in)


def merge_kernel(fwd, fwd_in, rev, rev_in, out, *, band_rows, width):
    band = (lax.axis_index("bh") * SIZES[3] + lax.axis_index("bz")) * SIZES[4] + lax.axis_index("bc")
    col = (2 * lax.broadcasted_iota(jnp.int32, (band_rows, width), 1) - (width - 1)).astype(jnp.float32) * (1.0 / width)
    row = lax.broadcasted_iota(jnp.int32, (band_rows, width), 0) + band * band_rows
    row = (2 * row - 63).astype(jnp.float32) * (1.0 / 64)
    for p in range(out.shape[0]):
        for way, (own, other) in enumerate(((fwd, fwd_in), (rev, rev_in))):
            _, total, cols, rows = joined(own[p], other[p], band_rows)
            out[p, way, 0] = cols / total - col
            out[p, way, 1] = rows / total - row


def merge(fwd, fwd_in, rev, rev_in, band_rows, width):
    return pl.pallas_call(
        functools.partial(merge_kernel, band_rows=band_rows, width=width),
        out_shape=jax.ShapeDtypeStruct((fwd.shape[0], 2, 2, band_rows, width), jnp.float32),
        in_specs=[VMEM] * 4,
        out_specs=VMEM,
        compiler_params=pltpu.CompilerParams(vmem_limit_bytes=4 << 20),
    )(fwd, fwd_in, rev, rev_in)


def refine_kernel(weight, bias, chip, own, core, out, *cur, layers):
    pairs, ways, comps, band_rows, width = own.shape
    high = 16
    total = pairs * ways * high
    band = (lax.axis_index("bh") * SIZES[3] + lax.axis_index("bz")) * SIZES[4] + lax.axis_index("bc")
    last = SIZES[2] * SIZES[3] * SIZES[4] - 1
    odd = lax.axis_index("bc") == 1
    for i in range(comps):
        for p in range(pairs):
            for d in range(ways):
                base = (p * ways + d) * high
                near, far = core[p, d, i], chip[p, d, i]
                cur[i][base : base + band_rows] = jnp.where(odd, near, far)
                cur[i][base + band_rows : base + 2 * band_rows] = own[p, d, i]
                cur[i][base + 2 * band_rows : base + 3 * band_rows] = jnp.where(odd, far, near)
                cur[i][base + 3 * band_rows : base + high] = jnp.zeros((high - 3 * band_rows, width), jnp.float32)
    row = lax.broadcasted_iota(jnp.int32, (total, width), 0) & (high - 1)
    lane = lax.broadcasted_iota(jnp.int32, (total, width), 1)
    low = jnp.where(band == 0, band_rows, 0)
    top = jnp.where(band == last, 2 * band_rows, 3 * band_rows)
    inside = ((row >= low) & (row < top)).astype(jnp.float32)
    keep_left = (lane > 0).astype(jnp.float32)
    keep_right = (lane < width - 1).astype(jnp.float32)
    for layer in range(layers):
        taps = []
        for i in range(comps):
            act = jnp.tanh(2.0 * cur[i][...]) * inside
            taps.append((pltpu.roll(act, 1, 1) * keep_left, act, pltpu.roll(act, width - 1, 1) * keep_right))
        for o in range(comps):
            lines = []
            for r in range(3):
                line = None
                for i in range(comps):
                    for c in range(3):
                        term = taps[i][c] * weight[(((layer * comps + o) * comps + i) * 3 + r) * 3 + c]
                        line = term if line is None else line + term
                lines.append(line)
            grown = pltpu.roll(lines[0], 1, 0) + lines[1] + pltpu.roll(lines[2], total - 1, 0)
            cur[o][...] = cur[o][...] + (grown + bias[layer * comps + o])
    for i in range(comps):
        for p in range(pairs):
            for d in range(ways):
                base = (p * ways + d) * high + band_rows
                out[p, d, i] = cur[i][base : base + band_rows]


def refine(weight, bias, chip, own, core):
    pairs, ways, comps, _, width = own.shape
    return pl.pallas_call(
        functools.partial(refine_kernel, layers=weight.shape[0]),
        out_shape=jax.ShapeDtypeStruct(own.shape, jnp.float32),
        in_specs=[SMEM, SMEM, VMEM, VMEM, VMEM],
        out_specs=VMEM,
        scratch_shapes=[pltpu.VMEM((pairs * ways * 16, width), jnp.float32)] * comps,
        compiler_params=pltpu.CompilerParams(vmem_limit_bytes=4 << 20),
    )(weight.reshape(-1), bias.reshape(-1), chip, own, core)


def gather_frames(blocks):
    orders = (
        (by_core(flip_y, flip_b), by_core(flip_a, flip_y), by_core(flip_b, flip_a)),
        (flip_a, flip_b, flip_y),
    )
    held = [[block] for block in blocks]
    for stage in range(3):
        send = [have[0] if len(have) == 1 else jnp.concatenate(have, axis=0) for have in held]
        got = [hop(part, order[stage]) for part, order in zip(send, orders)]
        got = lax.optimization_barrier(got)
        for have, piece in zip(held, got):
            have.append(piece)
    return held


def matched(src0, tgt0):
    src1 = hop(src0, flip_h)
    tgt1 = hop(tgt0, ring)
    src2 = hop(src0, flip_c)
    tgt2 = hop(tgt0, back)
    tgt1, src1, src2 = lax.optimization_barrier((tgt1, src1, src2))
    tgt3 = hop(tgt1, ring)
    src3 = hop(src1, flip_c)
    src = (src0, src1, src2, src3)
    early = match_early(src, (tgt0, tgt1))
    return match_late(src, (tgt0, tgt1, tgt2, tgt3), early)


def shards(features, frame_pairs, conv_weight, conv_bias):
    frames, band_rows, width, chans = features.shape
    cells = band_rows * width
    flat_features = features.reshape(frames, cells, chans)
    counts = (frames - 1, 1)
    held = gather_frames([flat_features[:-1], flat_features[-1:]])
    src0, tgt0 = pick(frame_pairs, held, counts)
    fwd_keep, fwd_send, rev_keep, rev_send = matched(src0, tgt0)
    fwd0, fwd1, rev0, rev1 = half(fwd_keep, hop(fwd_send, flip_c), rev_keep, hop(rev_send, flip_za), band_rows)
    flows = merge(fwd0, hop(fwd1, flip_h), rev0, hop(rev1, flip_zb), band_rows, width)
    chip = hop(flows, next_chip)
    core = hop(flows, flip_c)
    return refine(conv_weight, conv_bias, chip, flows, core)


def solution(mesh):
    finer = Mesh(mesh.devices.reshape(SIZES), AXES)
    frame, band = AXES[:2], AXES[2:]
    placed = (P(frame, band, None, None), P(frame, None), P(), P())
    return jax.shard_map(
        shards,
        mesh=finer,
        in_specs=placed,
        out_specs=P(frame, None, None, band, None),
        check_vma=False,
    )
```

```python
import functools
import itertools
import math

import jax
import jax.numpy as jnp
from jax import lax
from jax.experimental import pallas as pl
from jax.experimental.pallas import tpu as pltpu
from jax.sharding import Mesh
from jax.sharding import PartitionSpec as P

score_gain = 2.5
AXES = ("fx", "fy", "bh", "bz", "bc")
SIZES = (4, 2, 2, 4, 2)
VMEM = pl.BlockSpec(memory_space=pltpu.VMEM)
SMEM = pl.BlockSpec(memory_space=pltpu.SMEM)
NT = (((1,), (1,)), ((), ()))


def flat(coords):
    index = 0
    for value, size in zip(coords, SIZES):
        index = index * size + value
    return index


def hop(value, move):
    route = []
    for coords in itertools.product(*(range(size) for size in SIZES)):
        target = move(*coords)
        if target is not None:
            route.append((flat(coords), flat(target)))
    return lax.ppermute(value, AXES, route)


def flip_y(x, y, h, z, c):
    return x, 1 - y, h, z, c


def flip_a(x, y, h, z, c):
    return x ^ 1, y, h, z, c


def flip_b(x, y, h, z, c):
    return 3 - x, y, h, z, c


def flip_h(x, y, h, z, c):
    return x, y, 1 - h, z, c


def flip_c(x, y, h, z, c):
    return x, y, h, z, 1 - c


def flip_za(x, y, h, z, c):
    return x, y, h, z ^ 1, c


def flip_zb(x, y, h, z, c):
    return x, y, h, 3 - z, c


def ring(x, y, h, z, c):
    return x, y, h, (z + 1 - 2 * c) % SIZES[3], c


def back(x, y, h, z, c):
    return x, y, h, (z - 1 + 2 * c) % SIZES[3], c


def by_core(first, second):
    def move(*coords):
        return (second if coords[4] else first)(*coords)

    return move


def next_chip(x, y, h, z, c):
    band = (h * SIZES[3] + z) * SIZES[4] + c + 2 * c - 1
    return x, y, band // (SIZES[3] * SIZES[4]) % SIZES[2], band // SIZES[4] % SIZES[3], band % SIZES[4]


def gray(x):
    return (x ^ (x >> 1)) & 1, x >> 1


def seat(frame, frames):
    me_x, me_y, core = lax.axis_index("fx"), lax.axis_index("fy"), lax.axis_index("bc")
    me_a, me_b = gray(me_x)
    group = frame // frames
    to_a, to_b = gray(group // 2)
    fa, fb, fy = to_a ^ me_a, to_b ^ me_b, (group % 2) ^ me_y
    other = core == 1
    first = (jnp.where(other, fb, fy), jnp.where(other, fy, fa), jnp.where(other, fa, fb))
    return (first, (fa, fb, fy)), frame % frames


def copy_held(pieces, bits, which, frames, take, also=True):
    place = bits[0] + 2 * bits[1]
    for piece, low, span in zip(pieces, (0, 1, 2), (1, 1, 2)):

        @pl.when((place >= low) & (place < low + span) & also)
        def _():
            take(piece[(place - low) * frames + which])


def offer_kernel(*refs, parts):
    tables, pieces, outs = refs[:parts], refs[parts : 4 * parts], refs[4 * parts :]
    frames = pieces[0].shape[0]
    for v in range(parts):
        for slot in range(tables[v].shape[0]):
            for side in range(2):
                seats, which = seat(tables[v][slot, side], frames)

                def take(value):
                    outs[v][2 * slot + side] = value

                copy_held(pieces[3 * v : 3 * v + 3], seats[v], which, frames, take)


def offer(tables, held):
    pieces = [piece for have in held for piece in have]
    slots = 2 * tables[0].shape[0]
    return pl.pallas_call(
        functools.partial(offer_kernel, parts=len(held)),
        out_shape=[jax.ShapeDtypeStruct((slots,) + have[0].shape[1:], have[0].dtype) for have in held],
        in_specs=[SMEM] * len(held) + [VMEM] * len(pieces),
        out_specs=[VMEM] * len(held),
        compiler_params=pltpu.CompilerParams(vmem_limit_bytes=8 << 20),
    )(*tables, *pieces)


def pick_kernel(table, *refs, parts):
    pieces, outs = refs[: 4 * parts], refs[4 * parts :]
    frames = pieces[0].shape[0]
    for slot in range(table.shape[0]):
        for side in range(2):
            seats, which = seat(table[slot, side], frames)
            start = 0
            for v in range(parts):
                count = pieces[4 * v].shape[1]

                def take(value):
                    outs[side][slot, start : start + count] = value

                copy_held(pieces[4 * v : 4 * v + 3], seats[v], which, frames, take, seats[v][2] == 0)

                @pl.when(seats[v][2] == 1)
                def _():
                    take(pieces[4 * v + 3][2 * slot + side])

                start += count


def pick(table, held):
    pieces = [piece for have in held for piece in have]
    cells = sum(have[0].shape[1] for have in held)
    shape = jax.ShapeDtypeStruct((table.shape[0], cells, pieces[0].shape[2]), pieces[0].dtype)
    return pl.pallas_call(
        functools.partial(pick_kernel, parts=len(held)),
        out_shape=[shape, shape],
        in_specs=[SMEM] + [VMEM] * len(pieces),
        out_specs=[VMEM, VMEM],
        compiler_params=pltpu.CompilerParams(vmem_limit_bytes=12 << 20),
    )(table, *pieces)


def targets(refs, p, scale, rhs, start, cells):
    for j, ref in enumerate(refs):
        b = ref[p].astype(jnp.float32) * scale
        hi = b.astype(jnp.bfloat16)
        lo = (b - hi.astype(jnp.float32)).astype(jnp.bfloat16)
        rhs[(start + j) * cells : (start + j + 1) * cells, :] = jnp.concatenate([hi, lo], axis=1)


def places(cells, width):
    h, z, core = lax.axis_index("bh"), lax.axis_index("bz"), lax.axis_index("bc")
    src_place = [(h, core), (1 - h, core), (h, 1 - core), (1 - h, 1 - core)]
    src_band = [(hh * SIZES[3] + z) * SIZES[4] + cc for hh, cc in src_place]
    step = 1 - 2 * core
    tgt_z = [z, (z - step) % SIZES[3], (z + step) % SIZES[3], (z + 2) % SIZES[3]]
    tgt_band = [(h * SIZES[3] + zz) * SIZES[4] + core for zz in tgt_z]
    tgt_slot = [jnp.where(zz == z, 0, jnp.where(zz == 3 - z, 1, jnp.where(zz == (z ^ 1), 2, 3))) for zz in tgt_z]
    row = lambda band: (band * (cells // width)).astype(jnp.float32) - 27.5
    return [row(band) for band in src_band], [row(band) for band in tgt_band], tgt_slot


def chosen(values, index):
    return functools.reduce(lambda x, j: jnp.where(index == j, values[j], x), range(1, len(values)), values[0])


def block(sources, b, yj, src_rows, sums, cols, cells, width, shifts=None):
    band_rows = cells // width
    groups = width // 8
    a = jnp.concatenate(sources, axis=0)
    s = lax.dot_general(jnp.concatenate([a, a], axis=1), b, NT, preferred_element_type=jnp.float32)
    put, cols_first = cols
    for i in range(len(sources)):
        tt = [None] * band_rows
        uu = [None] * band_rows
        xx = [None] * band_rows
        for q in range(band_rows):
            ps = [None] * band_rows
            qs = [None] * band_rows
            for k in range(groups):
                r0 = i * cells + q * width + k * 8
                t = [s[r0 : r0 + 8, c * width : (c + 1) * width] for c in range(band_rows)]
                rows = slice(r0, r0 + 8)
                if shifts is None:
                    w = [jnp.exp2(x) for x in t]
                    v = w
                else:
                    m = shifts[0][rows, :]
                    w = [jnp.exp2(x - m) for x in t]
                    v = [jnp.exp2(x - shifts[1](c)) for c, x in enumerate(t)]
                a1 = w[0]
                b1 = w[0]
                for c in range(1, band_rows):
                    a1 = a1 + w[c]
                    b1 = b1 + a1
                sums(rows, a1, yj * a1 - b1)
                for c in range(band_rows):
                    ps[c] = v[c] if k == 0 else ps[c] + v[c]
                    qs[c] = ps[c] if k == 0 else qs[c] + ps[c]
            for c in range(band_rows):
                tt[c] = ps[c] if q == 0 else tt[c] + ps[c]
                uu[c] = tt[c] if q == 0 else uu[c] + tt[c]
                xx[c] = qs[c] if q == 0 else xx[c] + qs[c]
        for c in range(band_rows):
            put(slice(c * width, (c + 1) * width), i == 0 and cols_first, (tt[c], xx[c], src_rows[i] * tt[c] - uu[c]))


def early_kernel(*refs, nsrc, ntgt, cells, width):
    src, tgt = refs[:nsrc], refs[nsrc : nsrc + ntgt]
    acc, accy, g0, gq, gy, rhs = refs[nsrc + ntgt :]
    src_rows, tgt_rows, _ = places(cells, width)
    scale = score_gain / math.sqrt(src[0].shape[-1]) * math.log2(math.e)

    def one(p, jb, first):
        def sums(rows, total, rowed):
            acc[p, rows, :] = total if first else acc[p, rows, :] + total
            accy[p, rows, :] = rowed if first else accy[p, rows, :] + rowed

        def put(lanes, new, values):
            for ref, value in zip((g0, gq, gy), values):
                ref[p, jb, :, lanes] = value if new else ref[p, jb, :, lanes] + value

        b = rhs[jb * cells : (jb + 1) * cells, :]
        block([ref[p] for ref in src], b, tgt_rows[jb], src_rows, sums, (put, True), cells, width)

    def pair(p, carry):
        targets(tgt, p, scale, rhs, 0, cells)
        one(p, 0, True)

        for jb in range(1, ntgt):
            one(p, jb, False)
        return carry

    lax.fori_loop(0, src[0].shape[0], pair, 0)


def late_kernel(*refs, nsrc, ntgt, cells, width):
    src, tgt = refs[:nsrc], refs[nsrc : nsrc + ntgt]
    acc_in, accy_in, g0_in, gq_in, gy_in, fwd_keep, fwd_send, rev_keep, rev_send, rev, rhs, acc, accy, g0, gq, gy, shift_r, shift_c = refs[
        nsrc + ntgt :
    ]
    fwd = [(fwd_keep, 0), (fwd_keep, 1), (fwd_send, 0), (fwd_send, 1)]
    band_rows = cells // width
    src_rows, tgt_rows, tgt_slot = places(cells, width)
    scale = score_gain / math.sqrt(src[0].shape[-1]) * math.log2(math.e)
    early = g0_in.shape[1]
    lane = lax.broadcasted_iota(jnp.int32, (16, width), 1)
    row16 = lax.broadcasted_iota(jnp.int32, (16, width), 0)
    ramp = (2 * lane - (width - 1)).astype(jnp.float32)
    pick_rows = jnp.where(row16 == 0, 1.0, jnp.where(row16 == 1, ramp, 0.0)).astype(jnp.bfloat16)
    pick_rows = jnp.concatenate([pick_rows, pick_rows], axis=1)
    sub = lax.broadcasted_iota(jnp.int32, (8, width), 0).astype(jnp.float32)

    def safe(x):
        return jnp.all((x > 2.0**-90) & (x < 2.0**110))

    def lanes(ref, sl):
        x = ref[sl, :]
        hi = x.astype(jnp.bfloat16)
        lo = (x - hi.astype(jnp.float32)).astype(jnp.bfloat16)
        return lax.dot_general(pick_rows, jnp.concatenate([hi, lo], axis=1), NT, preferred_element_type=jnp.float32)

    def emit(p, cols_of, tops):
        ok = None
        for i in range(nsrc):
            sl = slice(i * cells, (i + 1) * cells)
            one = lanes(acc, sl)
            two = lanes(accy, sl)
            good = safe(one[0:1])
            ok = good if ok is None else ok & good
            ref, at = fwd[i]
            for r in range(band_rows):
                cs = slice(r * width, (r + 1) * width)
                ref[at, p, band_rows + r : band_rows + r + 1, :] = one[0:1, cs]
                ref[at, p, 2 * band_rows + r : 2 * band_rows + r + 1, :] = one[1:2, cs] * (1.0 / width)
                ref[at, p, 3 * band_rows + r : 3 * band_rows + r + 1, :] = two[0:1, cs] * (1.0 / 32)
                top = jnp.zeros((1, width), jnp.float32)
                if tops:
                    m = shift_r[i * cells + r * width : i * cells + (r + 1) * width, :]
                    top = jnp.transpose(m)[0:1, :]
                ref[at, p, r : r + 1, :] = top
        for j in range(ntgt):
            for r in range(band_rows):
                cs = slice(r * width, (r + 1) * width)
                t, xq, ty = cols_of(j, cs)
                tot = jnp.sum(t, axis=0, keepdims=True)
                ok = ok & safe(tot)
                slot = tgt_slot[j]
                x = (129.0 + 2.0 * sub) * t - 16.0 * xq
                rev[slot, p, band_rows + r : band_rows + r + 1, :] = tot
                rev[slot, p, 2 * band_rows + r : 2 * band_rows + r + 1, :] = jnp.sum(x, axis=0, keepdims=True) * (1.0 / width)
                rev[slot, p, 3 * band_rows + r : 3 * band_rows + r + 1, :] = jnp.sum(ty, axis=0, keepdims=True) * (1.0 / 32)
                rev[slot, p, r : r + 1, :] = shift_c[j, 0:1, cs] if tops else jnp.zeros((1, width), jnp.float32)
        return ok

    def put(jb):
        def inner(lane_slice, new, values):
            for ref, value in zip((g0, gq, gy), values):
                ref[jb, :, lane_slice] = value if new else ref[jb, :, lane_slice] + value

        return inner

    def pair(p, carry):
        targets(tgt[early:], p, scale, rhs, early, cells)
        sources = [ref[p] for ref in src]
        for jb in range(early, ntgt):

            def sums(rows, total, rowed):
                acc[rows, :] = (acc_in[p, rows, :] if jb == early else acc[rows, :]) + total
                accy[rows, :] = (accy_in[p, rows, :] if jb == early else accy[rows, :]) + rowed

            b = rhs[jb * cells : (jb + 1) * cells, :]
            block(sources, b, tgt_rows[jb], src_rows, sums, (put(jb), True), cells, width)

        def cols_of(j, cs):
            if j >= early:
                return g0[j, :, cs], gq[j, :, cs], gy[j, :, cs]
            return g0_in[p, j, :, cs], gq_in[p, j, :, cs], gy_in[p, j, :, cs]

        ok = emit(p, cols_of, False)

        @pl.when(jnp.logical_not(ok))
        def _():
            targets(tgt[:early], p, scale, rhs, 0, cells)
            shift_r[...] = jnp.full_like(shift_r, -1e30)
            shift_c[...] = jnp.full_like(shift_c, -1e30)

            def tops(jb, c):
                b = rhs[pl.ds(pl.multiple_of(jb * cells, cells), cells), :]
                for i in range(nsrc):

                    def part(q, c2):
                        a = src[i][p, pl.ds(pl.multiple_of(q * width, width), width), :]
                        s = lax.dot_general(jnp.concatenate([a, a], axis=1), b, NT, preferred_element_type=jnp.float32)
                        sl = pl.ds(pl.multiple_of(i * cells + q * width, width), width)
                        m = shift_r[sl, :]
                        for c3 in range(band_rows):
                            m = jnp.maximum(m, s[:, c3 * width : (c3 + 1) * width])
                        shift_r[sl, :] = m
                        t = shift_c[jb]
                        shift_c[jb] = jnp.maximum(t, jnp.broadcast_to(jnp.max(s, axis=0, keepdims=True), t.shape))
                        return c2

                    lax.fori_loop(0, band_rows, part, 0)
                return c

            lax.fori_loop(0, ntgt, tops, 0)

            def level(n, c):
                sl = pl.ds(pl.multiple_of(n * width, width), width)
                m = shift_r[sl, :]
                shift_r[sl, :] = jnp.broadcast_to(jnp.max(m, axis=1, keepdims=True), m.shape)
                return c

            lax.fori_loop(0, nsrc * band_rows, level, 0)
            acc[...] = jnp.zeros_like(acc)
            accy[...] = jnp.zeros_like(accy)

            def again(jb, c):
                def more(rows, total, rowed):
                    acc[rows, :] = acc[rows, :] + total
                    accy[rows, :] = accy[rows, :] + rowed

                shifts = (shift_r, lambda c4: shift_c[jb, :, c4 * width : (c4 + 1) * width])
                b = rhs[pl.ds(pl.multiple_of(jb * cells, cells), cells), :]
                block(sources, b, chosen(tgt_rows, jb), src_rows, more, (put(jb), True), cells, width, shifts)
                return c

            lax.fori_loop(0, ntgt, again, 0)
            emit(p, lambda j, cs: (g0[j, :, cs], gq[j, :, cs], gy[j, :, cs]), True)

        return carry

    lax.fori_loop(0, src[0].shape[0], pair, 0)
    rev_keep[...] = rev[0:2]
    rev_send[...] = rev[2:4]


def cost(pairs, blocks):
    return pl.CostEstimate(
        flops=134_000_000 * pairs * blocks, bytes_accessed=100_000 * pairs * blocks, transcendentals=262_144 * pairs * blocks
    )


def match_early(src, tgt):
    pairs, cells, chans = src[0].shape
    width = 128
    nsrc, ntgt = len(src), len(tgt)
    rows = jax.ShapeDtypeStruct((pairs, nsrc * cells, width), jnp.float32)
    cols = jax.ShapeDtypeStruct((pairs, ntgt, 8, cells), jnp.float32)
    return pl.pallas_call(
        functools.partial(early_kernel, nsrc=nsrc, ntgt=ntgt, cells=cells, width=width),
        out_shape=[rows, rows, cols, cols, cols],
        in_specs=[VMEM] * (nsrc + ntgt),
        out_specs=[VMEM] * 5,
        scratch_shapes=[pltpu.VMEM((ntgt * cells, 2 * chans), jnp.bfloat16)],
        compiler_params=pltpu.CompilerParams(vmem_limit_bytes=16 << 20),
        cost_estimate=cost(pairs, nsrc * ntgt),
    )(*src, *tgt)


def match_late(src, tgt, early):
    pairs, cells, chans = src[0].shape
    width = 128
    nsrc, ntgt = len(src), len(tgt)
    stats = jax.ShapeDtypeStruct((2, pairs, 4 * cells // width, width), jnp.float32)
    return pl.pallas_call(
        functools.partial(late_kernel, nsrc=nsrc, ntgt=ntgt, cells=cells, width=width),
        out_shape=[stats] * 4,
        in_specs=[VMEM] * (nsrc + ntgt + 5),
        out_specs=[VMEM] * 4,
        scratch_shapes=[
            pltpu.VMEM((4,) + stats.shape[1:], jnp.float32),
            pltpu.VMEM((ntgt * cells, 2 * chans), jnp.bfloat16),
            pltpu.VMEM((nsrc * cells, width), jnp.float32),
            pltpu.VMEM((nsrc * cells, width), jnp.float32),
            pltpu.VMEM((ntgt, 8, cells), jnp.float32),
            pltpu.VMEM((ntgt, 8, cells), jnp.float32),
            pltpu.VMEM((ntgt, 8, cells), jnp.float32),
            pltpu.VMEM((nsrc * cells, width), jnp.float32),
            pltpu.VMEM((ntgt, 8, cells), jnp.float32),
        ],
        compiler_params=pltpu.CompilerParams(vmem_limit_bytes=24 << 20),
        cost_estimate=cost(pairs, nsrc),
    )(*src, *tgt, *early)


def joined(left, right, band_rows):
    part = lambda x, k: x[k * band_rows : (k + 1) * band_rows]
    top = jnp.maximum(part(left, 0), part(right, 0))
    scale_l = jnp.exp2(part(left, 0) - top)
    scale_r = jnp.exp2(part(right, 0) - top)
    return [top] + [part(left, k) * scale_l + part(right, k) * scale_r for k in range(1, 4)]


def half_kernel(fwd, fwd_in, rev, rev_in, *outs, band_rows):
    for way, (own, other) in enumerate(((fwd, fwd_in), (rev, rev_in))):
        for side in range(2):
            for p in range(own.shape[1]):
                for k, value in enumerate(joined(own[side, p], other[side, p], band_rows)):
                    outs[2 * way + side][p, k * band_rows : (k + 1) * band_rows] = value


def half(fwd, fwd_in, rev, rev_in, band_rows):
    shape = jax.ShapeDtypeStruct(fwd.shape[1:], jnp.float32)
    return pl.pallas_call(
        functools.partial(half_kernel, band_rows=band_rows),
        out_shape=[shape] * 4,
        in_specs=[VMEM] * 4,
        out_specs=[VMEM] * 4,
        compiler_params=pltpu.CompilerParams(vmem_limit_bytes=4 << 20),
    )(fwd, fwd_in, rev, rev_in)


def merge_kernel(fwd, fwd_in, rev, rev_in, out, *, band_rows, width):
    band = (lax.axis_index("bh") * SIZES[3] + lax.axis_index("bz")) * SIZES[4] + lax.axis_index("bc")
    col = (2 * lax.broadcasted_iota(jnp.int32, (band_rows, width), 1) - (width - 1)).astype(jnp.float32) * (1.0 / width)
    row = lax.broadcasted_iota(jnp.int32, (band_rows, width), 0) + band * band_rows
    row = (2 * row - 63).astype(jnp.float32) * (1.0 / 64)
    for p in range(out.shape[0]):
        for way, (own, other) in enumerate(((fwd, fwd_in), (rev, rev_in))):
            _, total, cols, rows = joined(own[p], other[p], band_rows)
            out[p, way, 0] = cols / total - col
            out[p, way, 1] = rows / total - row


def merge(fwd, fwd_in, rev, rev_in, band_rows, width):
    return pl.pallas_call(
        functools.partial(merge_kernel, band_rows=band_rows, width=width),
        out_shape=jax.ShapeDtypeStruct((fwd.shape[0], 2, 2, band_rows, width), jnp.float32),
        in_specs=[VMEM] * 4,
        out_specs=VMEM,
        compiler_params=pltpu.CompilerParams(vmem_limit_bytes=4 << 20),
    )(fwd, fwd_in, rev, rev_in)


def refine_kernel(weight, bias, chip, own, core, out, *cur, layers):
    pairs, ways, comps, band_rows, width = own.shape
    high = 16
    total = pairs * ways * high
    band = (lax.axis_index("bh") * SIZES[3] + lax.axis_index("bz")) * SIZES[4] + lax.axis_index("bc")
    last = SIZES[2] * SIZES[3] * SIZES[4] - 1
    odd = lax.axis_index("bc") == 1
    for i in range(comps):
        for p in range(pairs):
            for d in range(ways):
                base = (p * ways + d) * high
                near, far = core[p, d, i], chip[p, d, i]
                cur[i][base : base + band_rows] = jnp.where(odd, near, far)
                cur[i][base + band_rows : base + 2 * band_rows] = own[p, d, i]
                cur[i][base + 2 * band_rows : base + 3 * band_rows] = jnp.where(odd, far, near)
                cur[i][base + 3 * band_rows : base + high] = jnp.zeros((high - 3 * band_rows, width), jnp.float32)
    row = lax.broadcasted_iota(jnp.int32, (total, width), 0) & (high - 1)
    lane = lax.broadcasted_iota(jnp.int32, (total, width), 1)
    low = jnp.where(band == 0, band_rows, 0)
    top = jnp.where(band == last, 2 * band_rows, 3 * band_rows)
    inside = ((row >= low) & (row < top)).astype(jnp.float32)
    keep_left = (lane > 0).astype(jnp.float32)
    keep_right = (lane < width - 1).astype(jnp.float32)
    for layer in range(layers):
        taps = []
        for i in range(comps):
            act = jnp.tanh(2.0 * cur[i][...]) * inside
            taps.append((pltpu.roll(act, 1, 1) * keep_left, act, pltpu.roll(act, width - 1, 1) * keep_right))
        for o in range(comps):
            lines = []
            for r in range(3):
                line = None
                for i in range(comps):
                    for c in range(3):
                        term = taps[i][c] * weight[(((layer * comps + o) * comps + i) * 3 + r) * 3 + c]
                        line = term if line is None else line + term
                lines.append(line)
            grown = pltpu.roll(lines[0], 1, 0) + lines[1] + pltpu.roll(lines[2], total - 1, 0)
            cur[o][...] = cur[o][...] + (grown + bias[layer * comps + o])
    for i in range(comps):
        for p in range(pairs):
            for d in range(ways):
                base = (p * ways + d) * high + band_rows
                out[p, d, i] = cur[i][base : base + band_rows]


def refine(weight, bias, chip, own, core):
    pairs, ways, comps, _, width = own.shape
    return pl.pallas_call(
        functools.partial(refine_kernel, layers=weight.shape[0]),
        out_shape=jax.ShapeDtypeStruct(own.shape, jnp.float32),
        in_specs=[SMEM, SMEM, VMEM, VMEM, VMEM],
        out_specs=VMEM,
        scratch_shapes=[pltpu.VMEM((pairs * ways * 16, width), jnp.float32)] * comps,
        compiler_params=pltpu.CompilerParams(vmem_limit_bytes=4 << 20),
    )(weight.reshape(-1), bias.reshape(-1), chip, own, core)


def gather_frames(blocks, table):
    orders = (
        (by_core(flip_y, flip_b), by_core(flip_a, flip_y), by_core(flip_b, flip_a)),
        (flip_a, flip_b, flip_y),
    )
    first = lax.optimization_barrier([hop(block, order[0]) for block, order in zip(blocks, orders)])
    held = [[block, piece] for block, piece in zip(blocks, first)]
    send = [jnp.concatenate(have, axis=0) for have in held]
    second = [hop(part, order[1]) for part, order in zip(send, orders)]
    tables = [hop(table, order[2]) for order in orders]
    second, tables = lax.optimization_barrier((second, tables))
    held = [have + [piece] for have, piece in zip(held, second)]
    sent = [hop(part, order[2]) for part, order in zip(offer(tables, held), orders)]
    return pick(table, [have + [piece] for have, piece in zip(held, sent)])


def matched(src0, tgt0):
    src1 = hop(src0, flip_h)
    tgt1 = hop(tgt0, ring)
    src2 = hop(src0, flip_c)
    tgt2 = hop(tgt0, back)
    tgt1, src1, src2, tgt2 = lax.optimization_barrier((tgt1, src1, src2, tgt2))
    tgt3 = hop(tgt1, ring)
    src3 = hop(src1, flip_c)
    src = (src0, src1, src2, src3)
    early = match_early(src, (tgt0, tgt1, tgt2))
    return match_late(src, (tgt0, tgt1, tgt2, tgt3), early)


def shards(features, frame_pairs, conv_weight, conv_bias):
    frames, band_rows, width, chans = features.shape
    cells = band_rows * width
    flat_features = features.reshape(frames, cells, chans)
    cut = cells * 11 // 16
    src0, tgt0 = gather_frames([flat_features[:, :cut], flat_features[:, cut:]], frame_pairs)
    fwd_keep, fwd_send, rev_keep, rev_send = matched(src0, tgt0)
    fwd0, fwd1, rev0, rev1 = half(fwd_keep, hop(fwd_send, flip_c), rev_keep, hop(rev_send, flip_za), band_rows)
    flows = merge(fwd0, hop(fwd1, flip_h), rev0, hop(rev1, flip_zb), band_rows, width)
    chip = hop(flows, next_chip)
    core = hop(flows, flip_c)
    return refine(conv_weight, conv_bias, chip, flows, core)


def solution(mesh):
    finer = Mesh(mesh.devices.reshape(SIZES), AXES)
    frame, band = AXES[:2], AXES[2:]
    placed = (P(frame, band, None, None), P(frame, None), P(), P())
    return jax.shard_map(
        shards,
        mesh=finer,
        in_specs=placed,
        out_specs=P(frame, None, None, band, None),
        check_vma=False,
    )
```

```python
import functools
import itertools
import math

import jax
import jax.numpy as jnp
from jax import lax
from jax.experimental import pallas as pl
from jax.experimental.pallas import tpu as pltpu
from jax.sharding import Mesh
from jax.sharding import PartitionSpec as P

score_gain = 2.5
AXES = ("fx", "fy", "bh", "bz", "bc")
SIZES = (4, 2, 2, 4, 2)
VMEM = pl.BlockSpec(memory_space=pltpu.VMEM)
SMEM = pl.BlockSpec(memory_space=pltpu.SMEM)
NT = (((1,), (1,)), ((), ()))


def flat(coords):
    index = 0
    for value, size in zip(coords, SIZES):
        index = index * size + value
    return index


def hop(value, move):
    route = []
    for coords in itertools.product(*(range(size) for size in SIZES)):
        target = move(*coords)
        if target is not None:
            route.append((flat(coords), flat(target)))
    return lax.ppermute(value, AXES, route)


def flip_y(x, y, h, z, c):
    return x, 1 - y, h, z, c


def flip_a(x, y, h, z, c):
    return x ^ 1, y, h, z, c


def flip_b(x, y, h, z, c):
    return 3 - x, y, h, z, c


def flip_h(x, y, h, z, c):
    return x, y, 1 - h, z, c


def flip_c(x, y, h, z, c):
    return x, y, h, z, 1 - c


def flip_za(x, y, h, z, c):
    return x, y, h, z ^ 1, c


def flip_zb(x, y, h, z, c):
    return x, y, h, 3 - z, c


def ring(x, y, h, z, c):
    return x, y, h, (z + 1 - 2 * c) % SIZES[3], c


def back(x, y, h, z, c):
    return x, y, h, (z - 1 + 2 * c) % SIZES[3], c


def by_core(first, second):
    def move(*coords):
        return (second if coords[4] else first)(*coords)

    return move


def next_chip(x, y, h, z, c):
    band = (h * SIZES[3] + z) * SIZES[4] + c + 2 * c - 1
    if band < 0 or band >= SIZES[2] * SIZES[3] * SIZES[4]:
        return x, y, h, z, c
    return x, y, band // (SIZES[3] * SIZES[4]), band // SIZES[4] % SIZES[3], band % SIZES[4]


def gray(x):
    return (x ^ (x >> 1)) & 1, x >> 1


def seat(frame, frames):
    me_x, me_y, core = lax.axis_index("fx"), lax.axis_index("fy"), lax.axis_index("bc")
    me_a, me_b = gray(me_x)
    group = frame // frames
    to_a, to_b = gray(group // 2)
    fa, fb, fy = to_a ^ me_a, to_b ^ me_b, (group % 2) ^ me_y
    other = core == 1
    first = (jnp.where(other, fb, fy), jnp.where(other, fy, fa), jnp.where(other, fa, fb))
    return (first, (fa, fb, fy)), frame % frames


def copy_held(pieces, bits, which, frames, take, also=True):
    place = bits[0] + 2 * bits[1]
    for piece, low, span in zip(pieces, (0, 1, 2), (1, 1, 2)):

        @pl.when((place >= low) & (place < low + span) & also)
        def _():
            take(piece[(place - low) * frames + which])


def offer_kernel(*refs, parts):
    tables, pieces, outs = refs[:parts], refs[parts : 4 * parts], refs[4 * parts :]
    frames = pieces[0].shape[0]
    for v in range(parts):
        for slot in range(tables[v].shape[0]):
            for side in range(2):
                seats, which = seat(tables[v][slot, side], frames)

                def take(value):
                    outs[v][2 * slot + side] = value

                copy_held(pieces[3 * v : 3 * v + 3], seats[v], which, frames, take)


def offer(tables, held):
    pieces = [piece for have in held for piece in have]
    slots = 2 * tables[0].shape[0]
    return pl.pallas_call(
        functools.partial(offer_kernel, parts=len(held)),
        out_shape=[jax.ShapeDtypeStruct((slots,) + have[0].shape[1:], have[0].dtype) for have in held],
        in_specs=[SMEM] * len(held) + [VMEM] * len(pieces),
        out_specs=[VMEM] * len(held),
        compiler_params=pltpu.CompilerParams(vmem_limit_bytes=8 << 20),
    )(*tables, *pieces)


def pick_kernel(table, *refs, parts):
    pieces, outs = refs[: 4 * parts], refs[4 * parts :]
    frames = pieces[0].shape[0]
    for slot in range(table.shape[0]):
        for side in range(2):
            seats, which = seat(table[slot, side], frames)
            start = 0
            for v in range(parts):
                count = pieces[4 * v].shape[1]

                def take(value):
                    outs[side][slot, start : start + count] = value

                copy_held(pieces[4 * v : 4 * v + 3], seats[v], which, frames, take, seats[v][2] == 0)

                @pl.when(seats[v][2] == 1)
                def _():
                    take(pieces[4 * v + 3][2 * slot + side])

                start += count


def pick(table, held):
    pieces = [piece for have in held for piece in have]
    cells = sum(have[0].shape[1] for have in held)
    shape = jax.ShapeDtypeStruct((table.shape[0], cells, pieces[0].shape[2]), pieces[0].dtype)
    return pl.pallas_call(
        functools.partial(pick_kernel, parts=len(held)),
        out_shape=[shape, shape],
        in_specs=[SMEM] + [VMEM] * len(pieces),
        out_specs=[VMEM, VMEM],
        compiler_params=pltpu.CompilerParams(vmem_limit_bytes=12 << 20),
    )(table, *pieces)


def targets(refs, p, scale, rhs, start, cells):
    for j, ref in enumerate(refs):
        b = ref[p].astype(jnp.float32) * scale
        hi = b.astype(jnp.bfloat16)
        lo = (b - hi.astype(jnp.float32)).astype(jnp.bfloat16)
        rhs[(start + j) * cells : (start + j + 1) * cells, :] = jnp.concatenate([hi, lo], axis=1)


def places(cells, width):
    h, z, core = lax.axis_index("bh"), lax.axis_index("bz"), lax.axis_index("bc")
    src_place = [(h, core), (1 - h, core), (h, 1 - core), (1 - h, 1 - core)]
    src_band = [(hh * SIZES[3] + z) * SIZES[4] + cc for hh, cc in src_place]
    step = 1 - 2 * core
    tgt_z = [z, (z - step) % SIZES[3], (z + step) % SIZES[3], (z + 2) % SIZES[3]]
    tgt_band = [(h * SIZES[3] + zz) * SIZES[4] + core for zz in tgt_z]
    tgt_slot = [jnp.where(zz == z, 0, jnp.where(zz == 3 - z, 1, jnp.where(zz == (z ^ 1), 2, 3))) for zz in tgt_z]
    row = lambda band: (band * (cells // width)).astype(jnp.float32) - 27.5
    return [row(band) for band in src_band], [row(band) for band in tgt_band], tgt_slot


def chosen(values, index):
    return functools.reduce(lambda x, j: jnp.where(index == j, values[j], x), range(1, len(values)), values[0])


def block(sources, b, yj, src_rows, sums, cols, cells, width, shifts=None):
    band_rows = cells // width
    groups = width // 8
    a = jnp.concatenate(sources, axis=0)
    s = lax.dot_general(jnp.concatenate([a, a], axis=1), b, NT, preferred_element_type=jnp.float32)
    put, cols_first = cols
    for i in range(len(sources)):
        tt = [None] * band_rows
        uu = [None] * band_rows
        xx = [None] * band_rows
        for q in range(band_rows):
            ps = [None] * band_rows
            qs = [None] * band_rows
            for k in range(groups):
                r0 = i * cells + q * width + k * 8
                t = [s[r0 : r0 + 8, c * width : (c + 1) * width] for c in range(band_rows)]
                rows = slice(r0, r0 + 8)
                if shifts is None:
                    w = [jnp.exp2(x) for x in t]
                    v = w
                else:
                    m = shifts[0][rows, :]
                    w = [jnp.exp2(x - m) for x in t]
                    v = [jnp.exp2(x - shifts[1](c)) for c, x in enumerate(t)]
                a1 = w[0]
                b1 = w[0]
                for c in range(1, band_rows):
                    a1 = a1 + w[c]
                    b1 = b1 + a1
                sums(rows, a1, yj * a1 - b1)
                for c in range(band_rows):
                    ps[c] = v[c] if k == 0 else ps[c] + v[c]
                    qs[c] = ps[c] if k == 0 else qs[c] + ps[c]
            for c in range(band_rows):
                tt[c] = ps[c] if q == 0 else tt[c] + ps[c]
                uu[c] = tt[c] if q == 0 else uu[c] + tt[c]
                xx[c] = qs[c] if q == 0 else xx[c] + qs[c]
        for c in range(band_rows):
            put(slice(c * width, (c + 1) * width), i == 0 and cols_first, (tt[c], xx[c], src_rows[i] * tt[c] - uu[c]))


def early_kernel(*refs, nsrc, ntgt, cells, width):
    src, tgt = refs[:nsrc], refs[nsrc : nsrc + ntgt]
    acc, accy, g0, gq, gy, rhs = refs[nsrc + ntgt :]
    src_rows, tgt_rows, _ = places(cells, width)
    scale = score_gain / math.sqrt(src[0].shape[-1]) * math.log2(math.e)

    def one(p, jb, first):
        def sums(rows, total, rowed):
            acc[p, rows, :] = total if first else acc[p, rows, :] + total
            accy[p, rows, :] = rowed if first else accy[p, rows, :] + rowed

        def put(lanes, new, values):
            for ref, value in zip((g0, gq, gy), values):
                ref[p, jb, :, lanes] = value if new else ref[p, jb, :, lanes] + value

        b = rhs[jb * cells : (jb + 1) * cells, :]
        block([ref[p] for ref in src], b, tgt_rows[jb], src_rows, sums, (put, True), cells, width)

    def pair(p, carry):
        targets(tgt, p, scale, rhs, 0, cells)
        one(p, 0, True)

        for jb in range(1, ntgt):
            one(p, jb, False)
        return carry

    lax.fori_loop(0, src[0].shape[0], pair, 0)


def late_kernel(*refs, nsrc, ntgt, cells, width):
    src, tgt = refs[:nsrc], refs[nsrc : nsrc + ntgt]
    acc_in, accy_in, g0_in, gq_in, gy_in, fwd_keep, fwd_send, rev_keep, rev_send, rev, rhs, acc, accy, g0, gq, gy, shift_r, shift_c = refs[
        nsrc + ntgt :
    ]
    fwd = [(fwd_keep, 0), (fwd_keep, 1), (fwd_send, 0), (fwd_send, 1)]
    band_rows = cells // width
    src_rows, tgt_rows, tgt_slot = places(cells, width)
    scale = score_gain / math.sqrt(src[0].shape[-1]) * math.log2(math.e)
    early = g0_in.shape[1]
    lane = lax.broadcasted_iota(jnp.int32, (16, width), 1)
    row16 = lax.broadcasted_iota(jnp.int32, (16, width), 0)
    ramp = (2 * lane - (width - 1)).astype(jnp.float32)
    pick_rows = jnp.where(row16 == 0, 1.0, jnp.where(row16 == 1, ramp, 0.0)).astype(jnp.bfloat16)
    pick_rows = jnp.concatenate([pick_rows, pick_rows], axis=1)
    sub = lax.broadcasted_iota(jnp.int32, (8, width), 0).astype(jnp.float32)

    def safe(x):
        return jnp.all((x > 2.0**-90) & (x < 2.0**110))

    def lanes(ref, sl):
        x = ref[sl, :]
        hi = x.astype(jnp.bfloat16)
        lo = (x - hi.astype(jnp.float32)).astype(jnp.bfloat16)
        return lax.dot_general(pick_rows, jnp.concatenate([hi, lo], axis=1), NT, preferred_element_type=jnp.float32)

    def emit(p, cols_of, tops):
        ok = None
        for i in range(nsrc):
            sl = slice(i * cells, (i + 1) * cells)
            one = lanes(acc, sl)
            two = lanes(accy, sl)
            good = safe(one[0:1])
            ok = good if ok is None else ok & good
            ref, at = fwd[i]
            for r in range(band_rows):
                cs = slice(r * width, (r + 1) * width)
                ref[at, p, band_rows + r : band_rows + r + 1, :] = one[0:1, cs]
                ref[at, p, 2 * band_rows + r : 2 * band_rows + r + 1, :] = one[1:2, cs] * (1.0 / width)
                ref[at, p, 3 * band_rows + r : 3 * band_rows + r + 1, :] = two[0:1, cs] * (1.0 / 32)
                top = jnp.zeros((1, width), jnp.float32)
                if tops:
                    m = shift_r[i * cells + r * width : i * cells + (r + 1) * width, :]
                    top = jnp.transpose(m)[0:1, :]
                ref[at, p, r : r + 1, :] = top
        for j in range(ntgt):
            for r in range(band_rows):
                cs = slice(r * width, (r + 1) * width)
                t, xq, ty = cols_of(j, cs)
                tot = jnp.sum(t, axis=0, keepdims=True)
                ok = ok & safe(tot)
                slot = tgt_slot[j]
                x = (129.0 + 2.0 * sub) * t - 16.0 * xq
                rev[slot, p, band_rows + r : band_rows + r + 1, :] = tot
                rev[slot, p, 2 * band_rows + r : 2 * band_rows + r + 1, :] = jnp.sum(x, axis=0, keepdims=True) * (1.0 / width)
                rev[slot, p, 3 * band_rows + r : 3 * band_rows + r + 1, :] = jnp.sum(ty, axis=0, keepdims=True) * (1.0 / 32)
                rev[slot, p, r : r + 1, :] = shift_c[j, 0:1, cs] if tops else jnp.zeros((1, width), jnp.float32)
        return ok

    def put(jb):
        def inner(lane_slice, new, values):
            for ref, value in zip((g0, gq, gy), values):
                ref[jb, :, lane_slice] = value if new else ref[jb, :, lane_slice] + value

        return inner

    def pair(p, carry):
        targets(tgt[early:], p, scale, rhs, early, cells)
        sources = [ref[p] for ref in src]
        for jb in range(early, ntgt):

            def sums(rows, total, rowed):
                acc[rows, :] = (acc_in[p, rows, :] if jb == early else acc[rows, :]) + total
                accy[rows, :] = (accy_in[p, rows, :] if jb == early else accy[rows, :]) + rowed

            b = rhs[jb * cells : (jb + 1) * cells, :]
            block(sources, b, tgt_rows[jb], src_rows, sums, (put(jb), True), cells, width)

        def cols_of(j, cs):
            if j >= early:
                return g0[j, :, cs], gq[j, :, cs], gy[j, :, cs]
            return g0_in[p, j, :, cs], gq_in[p, j, :, cs], gy_in[p, j, :, cs]

        ok = emit(p, cols_of, False)

        @pl.when(jnp.logical_not(ok))
        def _():
            targets(tgt[:early], p, scale, rhs, 0, cells)
            shift_r[...] = jnp.full_like(shift_r, -1e30)
            shift_c[...] = jnp.full_like(shift_c, -1e30)

            def tops(jb, c):
                b = rhs[pl.ds(pl.multiple_of(jb * cells, cells), cells), :]
                for i in range(nsrc):

                    def part(q, c2):
                        a = src[i][p, pl.ds(pl.multiple_of(q * width, width), width), :]
                        s = lax.dot_general(jnp.concatenate([a, a], axis=1), b, NT, preferred_element_type=jnp.float32)
                        sl = pl.ds(pl.multiple_of(i * cells + q * width, width), width)
                        m = shift_r[sl, :]
                        for c3 in range(band_rows):
                            m = jnp.maximum(m, s[:, c3 * width : (c3 + 1) * width])
                        shift_r[sl, :] = m
                        t = shift_c[jb]
                        shift_c[jb] = jnp.maximum(t, jnp.broadcast_to(jnp.max(s, axis=0, keepdims=True), t.shape))
                        return c2

                    lax.fori_loop(0, band_rows, part, 0)
                return c

            lax.fori_loop(0, ntgt, tops, 0)

            def level(n, c):
                sl = pl.ds(pl.multiple_of(n * width, width), width)
                m = shift_r[sl, :]
                shift_r[sl, :] = jnp.broadcast_to(jnp.max(m, axis=1, keepdims=True), m.shape)
                return c

            lax.fori_loop(0, nsrc * band_rows, level, 0)
            acc[...] = jnp.zeros_like(acc)
            accy[...] = jnp.zeros_like(accy)

            def again(jb, c):
                def more(rows, total, rowed):
                    acc[rows, :] = acc[rows, :] + total
                    accy[rows, :] = accy[rows, :] + rowed

                shifts = (shift_r, lambda c4: shift_c[jb, :, c4 * width : (c4 + 1) * width])
                b = rhs[pl.ds(pl.multiple_of(jb * cells, cells), cells), :]
                block(sources, b, chosen(tgt_rows, jb), src_rows, more, (put(jb), True), cells, width, shifts)
                return c

            lax.fori_loop(0, ntgt, again, 0)
            emit(p, lambda j, cs: (g0[j, :, cs], gq[j, :, cs], gy[j, :, cs]), True)

        return carry

    lax.fori_loop(0, src[0].shape[0], pair, 0)
    rev_keep[...] = rev[0:2]
    rev_send[...] = rev[2:4]


def cost(pairs, blocks):
    return pl.CostEstimate(
        flops=134_000_000 * pairs * blocks, bytes_accessed=100_000 * pairs * blocks, transcendentals=262_144 * pairs * blocks
    )


def match_early(src, tgt):
    pairs, cells, chans = src[0].shape
    width = 128
    nsrc, ntgt = len(src), len(tgt)
    rows = jax.ShapeDtypeStruct((pairs, nsrc * cells, width), jnp.float32)
    cols = jax.ShapeDtypeStruct((pairs, ntgt, 8, cells), jnp.float32)
    return pl.pallas_call(
        functools.partial(early_kernel, nsrc=nsrc, ntgt=ntgt, cells=cells, width=width),
        out_shape=[rows, rows, cols, cols, cols],
        in_specs=[VMEM] * (nsrc + ntgt),
        out_specs=[VMEM] * 5,
        scratch_shapes=[pltpu.VMEM((ntgt * cells, 2 * chans), jnp.bfloat16)],
        compiler_params=pltpu.CompilerParams(vmem_limit_bytes=16 << 20),
        cost_estimate=cost(pairs, nsrc * ntgt),
    )(*src, *tgt)


def match_late(src, tgt, early):
    pairs, cells, chans = src[0].shape
    width = 128
    nsrc, ntgt = len(src), len(tgt)
    stats = jax.ShapeDtypeStruct((2, pairs, 4 * cells // width, width), jnp.float32)
    return pl.pallas_call(
        functools.partial(late_kernel, nsrc=nsrc, ntgt=ntgt, cells=cells, width=width),
        out_shape=[stats] * 4,
        in_specs=[VMEM] * (nsrc + ntgt + 5),
        out_specs=[VMEM] * 4,
        scratch_shapes=[
            pltpu.VMEM((4,) + stats.shape[1:], jnp.float32),
            pltpu.VMEM((ntgt * cells, 2 * chans), jnp.bfloat16),
            pltpu.VMEM((nsrc * cells, width), jnp.float32),
            pltpu.VMEM((nsrc * cells, width), jnp.float32),
            pltpu.VMEM((ntgt, 8, cells), jnp.float32),
            pltpu.VMEM((ntgt, 8, cells), jnp.float32),
            pltpu.VMEM((ntgt, 8, cells), jnp.float32),
            pltpu.VMEM((nsrc * cells, width), jnp.float32),
            pltpu.VMEM((ntgt, 8, cells), jnp.float32),
        ],
        compiler_params=pltpu.CompilerParams(vmem_limit_bytes=24 << 20),
        cost_estimate=cost(pairs, nsrc),
    )(*src, *tgt, *early)


def joined(left, right, band_rows):
    part = lambda x, k: x[k * band_rows : (k + 1) * band_rows]
    top = jnp.maximum(part(left, 0), part(right, 0))
    scale_l = jnp.exp2(part(left, 0) - top)
    scale_r = jnp.exp2(part(right, 0) - top)
    return [top] + [part(left, k) * scale_l + part(right, k) * scale_r for k in range(1, 4)]


def half_kernel(fwd, fwd_in, rev, rev_in, *outs, band_rows):
    for way, (own, other) in enumerate(((fwd, fwd_in), (rev, rev_in))):
        for side in range(2):
            for p in range(own.shape[1]):
                for k, value in enumerate(joined(own[side, p], other[side, p], band_rows)):
                    outs[2 * way + side][p, k * band_rows : (k + 1) * band_rows] = value


def half(fwd, fwd_in, rev, rev_in, band_rows):
    shape = jax.ShapeDtypeStruct(fwd.shape[1:], jnp.float32)
    return pl.pallas_call(
        functools.partial(half_kernel, band_rows=band_rows),
        out_shape=[shape] * 4,
        in_specs=[VMEM] * 4,
        out_specs=[VMEM] * 4,
        compiler_params=pltpu.CompilerParams(vmem_limit_bytes=4 << 20),
    )(fwd, fwd_in, rev, rev_in)


def merge_kernel(fwd, fwd_in, rev, rev_in, out, *, band_rows, width):
    band = (lax.axis_index("bh") * SIZES[3] + lax.axis_index("bz")) * SIZES[4] + lax.axis_index("bc")
    col = (2 * lax.broadcasted_iota(jnp.int32, (band_rows, width), 1) - (width - 1)).astype(jnp.float32) * (1.0 / width)
    row = lax.broadcasted_iota(jnp.int32, (band_rows, width), 0) + band * band_rows
    row = (2 * row - 63).astype(jnp.float32) * (1.0 / 64)
    for p in range(out.shape[0]):
        for way, (own, other) in enumerate(((fwd, fwd_in), (rev, rev_in))):
            _, total, cols, rows = joined(own[p], other[p], band_rows)
            out[p, way, 0] = cols / total - col
            out[p, way, 1] = rows / total - row


def merge(fwd, fwd_in, rev, rev_in, band_rows, width):
    return pl.pallas_call(
        functools.partial(merge_kernel, band_rows=band_rows, width=width),
        out_shape=jax.ShapeDtypeStruct((fwd.shape[0], 2, 2, band_rows, width), jnp.float32),
        in_specs=[VMEM] * 4,
        out_specs=VMEM,
        compiler_params=pltpu.CompilerParams(vmem_limit_bytes=4 << 20),
    )(fwd, fwd_in, rev, rev_in)


def refine_kernel(weight, bias, chip, own, core, out, *cur, layers):
    pairs, ways, comps, band_rows, width = own.shape
    high = 16
    total = pairs * ways * high
    band = (lax.axis_index("bh") * SIZES[3] + lax.axis_index("bz")) * SIZES[4] + lax.axis_index("bc")
    last = SIZES[2] * SIZES[3] * SIZES[4] - 1
    odd = lax.axis_index("bc") == 1
    for i in range(comps):
        for p in range(pairs):
            for d in range(ways):
                base = (p * ways + d) * high
                near, far = core[p, d, i], chip[p, d, i]
                cur[i][base : base + band_rows] = jnp.where(odd, near, far)
                cur[i][base + band_rows : base + 2 * band_rows] = own[p, d, i]
                cur[i][base + 2 * band_rows : base + 3 * band_rows] = jnp.where(odd, far, near)
                cur[i][base + 3 * band_rows : base + high] = jnp.zeros((high - 3 * band_rows, width), jnp.float32)
    row = lax.broadcasted_iota(jnp.int32, (total, width), 0) & (high - 1)
    lane = lax.broadcasted_iota(jnp.int32, (total, width), 1)
    low = jnp.where(band == 0, band_rows, 0)
    top = jnp.where(band == last, 2 * band_rows, 3 * band_rows)
    inside = ((row >= low) & (row < top)).astype(jnp.float32)
    keep_left = (lane > 0).astype(jnp.float32)
    keep_right = (lane < width - 1).astype(jnp.float32)
    for layer in range(layers):
        taps = []
        for i in range(comps):
            act = jnp.tanh(2.0 * cur[i][...]) * inside
            taps.append((pltpu.roll(act, 1, 1) * keep_left, act, pltpu.roll(act, width - 1, 1) * keep_right))
        for o in range(comps):
            lines = []
            for r in range(3):
                line = None
                for i in range(comps):
                    for c in range(3):
                        term = taps[i][c] * weight[(((layer * comps + o) * comps + i) * 3 + r) * 3 + c]
                        line = term if line is None else line + term
                lines.append(line)
            grown = pltpu.roll(lines[0], 1, 0) + lines[1] + pltpu.roll(lines[2], total - 1, 0)
            cur[o][...] = cur[o][...] + (grown + bias[layer * comps + o])
    for i in range(comps):
        for p in range(pairs):
            for d in range(ways):
                base = (p * ways + d) * high + band_rows
                out[p, d, i] = cur[i][base : base + band_rows]


def refine(weight, bias, chip, own, core):
    pairs, ways, comps, _, width = own.shape
    return pl.pallas_call(
        functools.partial(refine_kernel, layers=weight.shape[0]),
        out_shape=jax.ShapeDtypeStruct(own.shape, jnp.float32),
        in_specs=[SMEM, SMEM, VMEM, VMEM, VMEM],
        out_specs=VMEM,
        scratch_shapes=[pltpu.VMEM((pairs * ways * 16, width), jnp.float32)] * comps,
        compiler_params=pltpu.CompilerParams(vmem_limit_bytes=4 << 20),
    )(weight.reshape(-1), bias.reshape(-1), chip, own, core)


def gather_frames(blocks, table):
    orders = (
        (by_core(flip_y, flip_b), by_core(flip_a, flip_y), by_core(flip_b, flip_a)),
        (flip_a, flip_b, flip_y),
    )
    first = [hop(block, order[0]) for block, order in zip(blocks, orders)]
    tables = [hop(table, order[2]) for order in orders]
    first, tables = lax.optimization_barrier((first, tables))
    held = [[block, piece] for block, piece in zip(blocks, first)]
    send = [jnp.concatenate(have, axis=0) for have in held]
    second = lax.optimization_barrier([hop(part, order[1]) for part, order in zip(send, orders)])
    held = [have + [piece] for have, piece in zip(held, second)]
    sent = [hop(part, order[2]) for part, order in zip(offer(tables, held), orders)]
    return pick(table, [have + [piece] for have, piece in zip(held, sent)])


def matched(src0, tgt0):
    tgt1 = hop(tgt0, ring)
    tgt2 = hop(tgt0, back)
    src1 = hop(src0, flip_h)
    src2 = hop(src0, flip_c)
    tgt1, src1, src2, tgt2 = lax.optimization_barrier((tgt1, src1, src2, tgt2))
    tgt3 = hop(tgt1, ring)
    src3 = hop(src1, flip_c)
    src = (src0, src1, src2, src3)
    early = match_early(src, (tgt0, tgt1, tgt2))
    return match_late(src, (tgt0, tgt1, tgt2, tgt3), early)


def shards(features, frame_pairs, conv_weight, conv_bias):
    frames, band_rows, width, chans = features.shape
    cells = band_rows * width
    flat_features = features.reshape(frames, cells, chans)
    cut = cells * 11 // 16
    src0, tgt0 = gather_frames([flat_features[:, :cut], flat_features[:, cut:]], frame_pairs)
    fwd_keep, fwd_send, rev_keep, rev_send = matched(src0, tgt0)
    fwd0, fwd1, rev0, rev1 = half(fwd_keep, hop(fwd_send, flip_c), rev_keep, hop(rev_send, flip_za), band_rows)
    flows = merge(fwd0, hop(fwd1, flip_h), rev0, hop(rev1, flip_zb), band_rows, width)
    chip = hop(flows, next_chip)
    core = hop(flows, flip_c)
    return refine(conv_weight, conv_bias, chip, flows, core)


def solution(mesh):
    finer = Mesh(mesh.devices.reshape(SIZES), AXES)
    frame, band = AXES[:2], AXES[2:]
    placed = (P(frame, band, None, None), P(frame, None), P(), P())
    return jax.shard_map(
        shards,
        mesh=finer,
        in_specs=placed,
        out_specs=P(frame, None, None, band, None),
        check_vma=False,
    )
```

```python
import functools
import itertools
import math

import jax
import jax.numpy as jnp
from jax import lax
from jax.experimental import pallas as pl
from jax.experimental.pallas import tpu as pltpu
from jax.sharding import Mesh
from jax.sharding import PartitionSpec as P

score_gain = 2.5
AXES = ("fx", "fy", "bh", "bz", "bc")
SIZES = (4, 2, 2, 4, 2)
VMEM = pl.BlockSpec(memory_space=pltpu.VMEM)
SMEM = pl.BlockSpec(memory_space=pltpu.SMEM)
NT = (((1,), (1,)), ((), ()))


def flat(coords):
    index = 0
    for value, size in zip(coords, SIZES):
        index = index * size + value
    return index


def hop(value, move):
    route = []
    for coords in itertools.product(*(range(size) for size in SIZES)):
        target = move(*coords)
        if target is not None:
            route.append((flat(coords), flat(target)))
    return lax.ppermute(value, AXES, route)


def flip_y(x, y, h, z, c):
    return x, 1 - y, h, z, c


def flip_a(x, y, h, z, c):
    return x ^ 1, y, h, z, c


def flip_b(x, y, h, z, c):
    return 3 - x, y, h, z, c


def flip_h(x, y, h, z, c):
    return x, y, 1 - h, z, c


def flip_c(x, y, h, z, c):
    return x, y, h, z, 1 - c


def flip_za(x, y, h, z, c):
    return x, y, h, z ^ 1, c


def flip_zb(x, y, h, z, c):
    return x, y, h, 3 - z, c


def ring(x, y, h, z, c):
    return x, y, h, (z + 1 - 2 * c) % SIZES[3], c


def back(x, y, h, z, c):
    return x, y, h, (z - 1 + 2 * c) % SIZES[3], c


def by_core(first, second):
    def move(*coords):
        return (second if coords[4] else first)(*coords)

    return move


def next_chip(x, y, h, z, c):
    band = (h * SIZES[3] + z) * SIZES[4] + c + 2 * c - 1
    if band < 0 or band >= SIZES[2] * SIZES[3] * SIZES[4]:
        return x, y, h, z, c
    return x, y, band // (SIZES[3] * SIZES[4]), band // SIZES[4] % SIZES[3], band % SIZES[4]


def gray(x):
    return (x ^ (x >> 1)) & 1, x >> 1


def seat(frame, frames):
    me_x, me_y, core = lax.axis_index("fx"), lax.axis_index("fy"), lax.axis_index("bc")
    me_a, me_b = gray(me_x)
    group = frame // frames
    to_a, to_b = gray(group // 2)
    fa, fb, fy = to_a ^ me_a, to_b ^ me_b, (group % 2) ^ me_y
    other = core == 1
    first = (jnp.where(other, fb, fy), jnp.where(other, fy, fa), jnp.where(other, fa, fb))
    return (first, (fa, fb, fy)), frame % frames


def copy_held(pieces, bits, which, frames, take, also=True):
    place = bits[0] + 2 * bits[1]
    for piece, low, span in zip(pieces, (0, 1, 2), (1, 1, 2)):

        @pl.when((place >= low) & (place < low + span) & also)
        def _():
            take(piece[(place - low) * frames + which])


def offer_kernel(*refs, parts):
    tables, pieces, outs = refs[:parts], refs[parts : 4 * parts], refs[4 * parts :]
    frames = pieces[0].shape[0]
    for v in range(parts):
        for slot in range(tables[v].shape[0]):
            for side in range(2):
                seats, which = seat(tables[v][slot, side], frames)

                def take(value):
                    outs[v][2 * slot + side] = value

                copy_held(pieces[3 * v : 3 * v + 3], seats[v], which, frames, take)


def offer(tables, held):
    pieces = [piece for have in held for piece in have]
    slots = 2 * tables[0].shape[0]
    return pl.pallas_call(
        functools.partial(offer_kernel, parts=len(held)),
        out_shape=[jax.ShapeDtypeStruct((slots,) + have[0].shape[1:], have[0].dtype) for have in held],
        in_specs=[SMEM] * len(held) + [VMEM] * len(pieces),
        out_specs=[VMEM] * len(held),
        compiler_params=pltpu.CompilerParams(vmem_limit_bytes=8 << 20),
    )(*tables, *pieces)


def pick_kernel(table, *refs, parts):
    pieces, outs = refs[: 4 * parts], refs[4 * parts :]
    frames = pieces[0].shape[0]
    for slot in range(table.shape[0]):
        for side in range(2):
            seats, which = seat(table[slot, side], frames)
            start = 0
            for v in range(parts):
                count = pieces[4 * v].shape[1]

                def take(value):
                    outs[side][slot, start : start + count] = value

                copy_held(pieces[4 * v : 4 * v + 3], seats[v], which, frames, take, seats[v][2] == 0)

                @pl.when(seats[v][2] == 1)
                def _():
                    take(pieces[4 * v + 3][2 * slot + side])

                start += count


def pick(table, held):
    pieces = [piece for have in held for piece in have]
    cells = sum(have[0].shape[1] for have in held)
    shape = jax.ShapeDtypeStruct((table.shape[0], cells, pieces[0].shape[2]), pieces[0].dtype)
    return pl.pallas_call(
        functools.partial(pick_kernel, parts=len(held)),
        out_shape=[shape, shape],
        in_specs=[SMEM] + [VMEM] * len(pieces),
        out_specs=[VMEM, VMEM],
        compiler_params=pltpu.CompilerParams(vmem_limit_bytes=12 << 20),
    )(table, *pieces)


def targets(refs, p, scale, rhs, start, cells):
    for j, ref in enumerate(refs):
        b = ref[p].astype(jnp.float32) * scale
        hi = b.astype(jnp.bfloat16)
        lo = (b - hi.astype(jnp.float32)).astype(jnp.bfloat16)
        rhs[(start + j) * cells : (start + j + 1) * cells, :] = jnp.concatenate([hi, lo], axis=1)


def places(cells, width):
    h, z, core = lax.axis_index("bh"), lax.axis_index("bz"), lax.axis_index("bc")
    src_place = [(h, core), (1 - h, core), (h, 1 - core), (1 - h, 1 - core)]
    src_band = [(hh * SIZES[3] + z) * SIZES[4] + cc for hh, cc in src_place]
    step = 1 - 2 * core
    tgt_z = [z, (z - step) % SIZES[3], (z + step) % SIZES[3], (z + 2) % SIZES[3]]
    tgt_band = [(h * SIZES[3] + zz) * SIZES[4] + core for zz in tgt_z]
    tgt_slot = [jnp.where(zz == z, 0, jnp.where(zz == 3 - z, 1, jnp.where(zz == (z ^ 1), 2, 3))) for zz in tgt_z]
    row = lambda band: (band * (cells // width)).astype(jnp.float32) - 27.5
    return [row(band) for band in src_band], [row(band) for band in tgt_band], tgt_slot


def chosen(values, index):
    return functools.reduce(lambda x, j: jnp.where(index == j, values[j], x), range(1, len(values)), values[0])


def block(sources, b, yj, src_rows, sums, cols, cells, width, shifts=None):
    band_rows = cells // width
    groups = width // 8
    a = jnp.concatenate(sources, axis=0)
    s = lax.dot_general(jnp.concatenate([a, a], axis=1), b, NT, preferred_element_type=jnp.float32)
    put, cols_first = cols
    for i in range(len(sources)):
        tt = [None] * band_rows
        uu = [None] * band_rows
        xx = [None] * band_rows
        for q in range(band_rows):
            ps = [None] * band_rows
            qs = [None] * band_rows
            for k in range(groups):
                r0 = i * cells + q * width + k * 8
                t = [s[r0 : r0 + 8, c * width : (c + 1) * width] for c in range(band_rows)]
                rows = slice(r0, r0 + 8)
                if shifts is None:
                    w = [jnp.exp2(x) for x in t]
                    v = w
                else:
                    m = shifts[0][rows, :]
                    w = [jnp.exp2(x - m) for x in t]
                    v = [jnp.exp2(x - shifts[1](c)) for c, x in enumerate(t)]
                a1 = w[0]
                b1 = w[0]
                for c in range(1, band_rows):
                    a1 = a1 + w[c]
                    b1 = b1 + a1
                sums(rows, a1, yj * a1 - b1)
                for c in range(band_rows):
                    ps[c] = v[c] if k == 0 else ps[c] + v[c]
                    qs[c] = ps[c] if k == 0 else qs[c] + ps[c]
            for c in range(band_rows):
                tt[c] = ps[c] if q == 0 else tt[c] + ps[c]
                uu[c] = tt[c] if q == 0 else uu[c] + tt[c]
                xx[c] = qs[c] if q == 0 else xx[c] + qs[c]
        for c in range(band_rows):
            put(slice(c * width, (c + 1) * width), i == 0 and cols_first, (tt[c], xx[c], src_rows[i] * tt[c] - uu[c]))


def early_kernel(*refs, which, ntgt, cells, width, ready):
    nsrc = len(which)
    src, refs = refs[:nsrc], refs[nsrc:]
    if ready:
        rhs, acc, accy, g0, gq, gy = refs
    else:
        tgt, refs = refs[:ntgt], refs[ntgt:]
        acc, accy, g0, gq, gy, rhs = refs
    src_rows, tgt_rows, _ = places(cells, width)
    src_rows = [src_rows[i] for i in which]
    scale = score_gain / math.sqrt(src[0].shape[-1]) * math.log2(math.e)

    def one(p, jb, first):
        def sums(rows, total, rowed):
            acc[p, rows, :] = total if first else acc[p, rows, :] + total
            accy[p, rows, :] = rowed if first else accy[p, rows, :] + rowed

        def put(lanes, new, values):
            for ref, value in zip((g0, gq, gy), values):
                ref[p, jb, :, lanes] = value if new else ref[p, jb, :, lanes] + value

        b = rhs[p, jb * cells : (jb + 1) * cells, :]
        block([ref[p] for ref in src], b, tgt_rows[jb], src_rows, sums, (put, True), cells, width)

    def pair(p, carry):
        if not ready:
            targets(tgt, p, scale, rhs.at[p], 0, cells)
        for jb in range(ntgt):
            one(p, jb, jb == 0)
        return carry

    lax.fori_loop(0, src[0].shape[0], pair, 0)


def late_kernel(*refs, nsrc, ntgt, cells, width):
    src, tgt = refs[:nsrc], refs[nsrc : nsrc + ntgt]
    before = (refs[nsrc + ntgt : nsrc + ntgt + 5], refs[nsrc + ntgt + 5 : nsrc + ntgt + 10])
    fwd_keep, fwd_send, rev_keep, rev_send, rev, rhs, acc, accy, g0, gq, gy, shift_r, shift_c = refs[nsrc + ntgt + 10 :]
    fwd = [(fwd_keep, 0), (fwd_keep, 1), (fwd_send, 0), (fwd_send, 1)]
    band_rows = cells // width
    src_rows, tgt_rows, tgt_slot = places(cells, width)
    scale = score_gain / math.sqrt(src[0].shape[-1]) * math.log2(math.e)
    early = before[0][2].shape[1]
    lane = lax.broadcasted_iota(jnp.int32, (16, width), 1)
    row16 = lax.broadcasted_iota(jnp.int32, (16, width), 0)
    ramp = (2 * lane - (width - 1)).astype(jnp.float32)
    pick_rows = jnp.where(row16 == 0, 1.0, jnp.where(row16 == 1, ramp, 0.0)).astype(jnp.bfloat16)
    pick_rows = jnp.concatenate([pick_rows, pick_rows], axis=1)
    sub = lax.broadcasted_iota(jnp.int32, (8, width), 0).astype(jnp.float32)

    def safe(x):
        return jnp.all((x > 2.0**-90) & (x < 2.0**110))

    def lanes(ref, sl):
        x = ref[sl, :]
        hi = x.astype(jnp.bfloat16)
        lo = (x - hi.astype(jnp.float32)).astype(jnp.bfloat16)
        return lax.dot_general(pick_rows, jnp.concatenate([hi, lo], axis=1), NT, preferred_element_type=jnp.float32)

    def emit(p, cols_of, tops):
        ok = None
        for i in range(nsrc):
            sl = slice(i * cells, (i + 1) * cells)
            one = lanes(acc, sl)
            two = lanes(accy, sl)
            good = safe(one[0:1])
            ok = good if ok is None else ok & good
            ref, at = fwd[i]
            for r in range(band_rows):
                cs = slice(r * width, (r + 1) * width)
                ref[at, p, band_rows + r : band_rows + r + 1, :] = one[0:1, cs]
                ref[at, p, 2 * band_rows + r : 2 * band_rows + r + 1, :] = one[1:2, cs] * (1.0 / width)
                ref[at, p, 3 * band_rows + r : 3 * band_rows + r + 1, :] = two[0:1, cs] * (1.0 / 32)
                top = jnp.zeros((1, width), jnp.float32)
                if tops:
                    m = shift_r[i * cells + r * width : i * cells + (r + 1) * width, :]
                    top = jnp.transpose(m)[0:1, :]
                ref[at, p, r : r + 1, :] = top
        for j in range(ntgt):
            for r in range(band_rows):
                cs = slice(r * width, (r + 1) * width)
                t, xq, ty = cols_of(j, cs)
                tot = jnp.sum(t, axis=0, keepdims=True)
                ok = ok & safe(tot)
                slot = tgt_slot[j]
                x = (129.0 + 2.0 * sub) * t - 16.0 * xq
                rev[slot, p, band_rows + r : band_rows + r + 1, :] = tot
                rev[slot, p, 2 * band_rows + r : 2 * band_rows + r + 1, :] = jnp.sum(x, axis=0, keepdims=True) * (1.0 / width)
                rev[slot, p, 3 * band_rows + r : 3 * band_rows + r + 1, :] = jnp.sum(ty, axis=0, keepdims=True) * (1.0 / 32)
                rev[slot, p, r : r + 1, :] = shift_c[j, 0:1, cs] if tops else jnp.zeros((1, width), jnp.float32)
        return ok

    def put(jb):
        def inner(lane_slice, new, values):
            for ref, value in zip((g0, gq, gy), values):
                ref[jb, :, lane_slice] = value if new else ref[jb, :, lane_slice] + value

        return inner

    def pair(p, carry):
        targets(tgt[early:], p, scale, rhs, early, cells)
        sources = [ref[p] for ref in src]
        for jb in range(early, ntgt):

            def sums(rows, total, rowed):
                i, r0 = divmod(rows.start, cells)
                r0 += i // 2 * cells
                old = before[i % 2]
                acc[rows, :] = (old[0][p, r0 : r0 + 8, :] if jb == early else acc[rows, :]) + total
                accy[rows, :] = (old[1][p, r0 : r0 + 8, :] if jb == early else accy[rows, :]) + rowed

            b = rhs[jb * cells : (jb + 1) * cells, :]
            block(sources, b, tgt_rows[jb], src_rows, sums, (put(jb), True), cells, width)

        def cols_of(j, cs):
            if j >= early:
                return g0[j, :, cs], gq[j, :, cs], gy[j, :, cs]
            return [before[0][n][p, j, :, cs] + before[1][n][p, j, :, cs] for n in (2, 3, 4)]

        ok = emit(p, cols_of, False)

        @pl.when(jnp.logical_not(ok))
        def _():
            targets(tgt[:early], p, scale, rhs, 0, cells)
            shift_r[...] = jnp.full_like(shift_r, -1e30)
            shift_c[...] = jnp.full_like(shift_c, -1e30)

            def tops(jb, c):
                b = rhs[pl.ds(pl.multiple_of(jb * cells, cells), cells), :]
                for i in range(nsrc):

                    def part(q, c2):
                        a = src[i][p, pl.ds(pl.multiple_of(q * width, width), width), :]
                        s = lax.dot_general(jnp.concatenate([a, a], axis=1), b, NT, preferred_element_type=jnp.float32)
                        sl = pl.ds(pl.multiple_of(i * cells + q * width, width), width)
                        m = shift_r[sl, :]
                        for c3 in range(band_rows):
                            m = jnp.maximum(m, s[:, c3 * width : (c3 + 1) * width])
                        shift_r[sl, :] = m
                        t = shift_c[jb]
                        shift_c[jb] = jnp.maximum(t, jnp.broadcast_to(jnp.max(s, axis=0, keepdims=True), t.shape))
                        return c2

                    lax.fori_loop(0, band_rows, part, 0)
                return c

            lax.fori_loop(0, ntgt, tops, 0)

            def level(n, c):
                sl = pl.ds(pl.multiple_of(n * width, width), width)
                m = shift_r[sl, :]
                shift_r[sl, :] = jnp.broadcast_to(jnp.max(m, axis=1, keepdims=True), m.shape)
                return c

            lax.fori_loop(0, nsrc * band_rows, level, 0)
            acc[...] = jnp.zeros_like(acc)
            accy[...] = jnp.zeros_like(accy)

            def again(jb, c):
                def more(rows, total, rowed):
                    acc[rows, :] = acc[rows, :] + total
                    accy[rows, :] = accy[rows, :] + rowed

                shifts = (shift_r, lambda c4: shift_c[jb, :, c4 * width : (c4 + 1) * width])
                b = rhs[pl.ds(pl.multiple_of(jb * cells, cells), cells), :]
                block(sources, b, chosen(tgt_rows, jb), src_rows, more, (put(jb), True), cells, width, shifts)
                return c

            lax.fori_loop(0, ntgt, again, 0)
            emit(p, lambda j, cs: (g0[j, :, cs], gq[j, :, cs], gy[j, :, cs]), True)

        return carry

    lax.fori_loop(0, src[0].shape[0], pair, 0)
    rev_keep[...] = rev[0:2]
    rev_send[...] = rev[2:4]


def cost(pairs, blocks):
    return pl.CostEstimate(
        flops=134_000_000 * pairs * blocks, bytes_accessed=100_000 * pairs * blocks, transcendentals=262_144 * pairs * blocks
    )


def match_early(src, which, tgt=None, scaled=None):
    pairs, cells, chans = src[0].shape
    width = 128
    nsrc = len(src)
    ntgt = len(tgt) if tgt else scaled.shape[1] // cells
    rows = jax.ShapeDtypeStruct((pairs, nsrc * cells, width), jnp.float32)
    cols = jax.ShapeDtypeStruct((pairs, ntgt, 8, cells), jnp.float32)
    shapes = [rows, rows, cols, cols, cols]
    if tgt:
        shapes.append(jax.ShapeDtypeStruct((pairs, ntgt * cells, 2 * chans), jnp.bfloat16))
    operands = (*src, *tgt) if tgt else (*src, scaled)
    return pl.pallas_call(
        functools.partial(early_kernel, which=which, ntgt=ntgt, cells=cells, width=width, ready=not tgt),
        out_shape=shapes,
        in_specs=[VMEM] * len(operands),
        out_specs=[VMEM] * len(shapes),
        compiler_params=pltpu.CompilerParams(vmem_limit_bytes=14 << 20),
        cost_estimate=cost(pairs, nsrc * ntgt),
    )(*operands)


def match_late(src, tgt, early):
    pairs, cells, chans = src[0].shape
    width = 128
    nsrc, ntgt = len(src), len(tgt)
    stats = jax.ShapeDtypeStruct((2, pairs, 4 * cells // width, width), jnp.float32)
    return pl.pallas_call(
        functools.partial(late_kernel, nsrc=nsrc, ntgt=ntgt, cells=cells, width=width),
        out_shape=[stats] * 4,
        in_specs=[VMEM] * (nsrc + ntgt + 10),
        out_specs=[VMEM] * 4,
        scratch_shapes=[
            pltpu.VMEM((4,) + stats.shape[1:], jnp.float32),
            pltpu.VMEM((ntgt * cells, 2 * chans), jnp.bfloat16),
            pltpu.VMEM((nsrc * cells, width), jnp.float32),
            pltpu.VMEM((nsrc * cells, width), jnp.float32),
            pltpu.VMEM((ntgt, 8, cells), jnp.float32),
            pltpu.VMEM((ntgt, 8, cells), jnp.float32),
            pltpu.VMEM((ntgt, 8, cells), jnp.float32),
            pltpu.VMEM((nsrc * cells, width), jnp.float32),
            pltpu.VMEM((ntgt, 8, cells), jnp.float32),
        ],
        compiler_params=pltpu.CompilerParams(vmem_limit_bytes=24 << 20),
        cost_estimate=cost(pairs, nsrc),
    )(*src, *tgt, *early)


def joined(left, right, band_rows):
    part = lambda x, k: x[k * band_rows : (k + 1) * band_rows]
    top = jnp.maximum(part(left, 0), part(right, 0))
    scale_l = jnp.exp2(part(left, 0) - top)
    scale_r = jnp.exp2(part(right, 0) - top)
    return [top] + [part(left, k) * scale_l + part(right, k) * scale_r for k in range(1, 4)]


def half_kernel(fwd, fwd_in, rev, rev_in, *outs, band_rows):
    for way, (own, other) in enumerate(((fwd, fwd_in), (rev, rev_in))):
        for side in range(2):
            for p in range(own.shape[1]):
                for k, value in enumerate(joined(own[side, p], other[side, p], band_rows)):
                    outs[2 * way + side][p, k * band_rows : (k + 1) * band_rows] = value


def half(fwd, fwd_in, rev, rev_in, band_rows):
    shape = jax.ShapeDtypeStruct(fwd.shape[1:], jnp.float32)
    return pl.pallas_call(
        functools.partial(half_kernel, band_rows=band_rows),
        out_shape=[shape] * 4,
        in_specs=[VMEM] * 4,
        out_specs=[VMEM] * 4,
        compiler_params=pltpu.CompilerParams(vmem_limit_bytes=4 << 20),
    )(fwd, fwd_in, rev, rev_in)


def merge_kernel(fwd, fwd_in, rev, rev_in, out, *, band_rows, width):
    band = (lax.axis_index("bh") * SIZES[3] + lax.axis_index("bz")) * SIZES[4] + lax.axis_index("bc")
    col = (2 * lax.broadcasted_iota(jnp.int32, (band_rows, width), 1) - (width - 1)).astype(jnp.float32) * (1.0 / width)
    row = lax.broadcasted_iota(jnp.int32, (band_rows, width), 0) + band * band_rows
    row = (2 * row - 63).astype(jnp.float32) * (1.0 / 64)
    for p in range(out.shape[0]):
        for way, (own, other) in enumerate(((fwd, fwd_in), (rev, rev_in))):
            _, total, cols, rows = joined(own[p], other[p], band_rows)
            out[p, way, 0] = cols / total - col
            out[p, way, 1] = rows / total - row


def merge(fwd, fwd_in, rev, rev_in, band_rows, width):
    return pl.pallas_call(
        functools.partial(merge_kernel, band_rows=band_rows, width=width),
        out_shape=jax.ShapeDtypeStruct((fwd.shape[0], 2, 2, band_rows, width), jnp.float32),
        in_specs=[VMEM] * 4,
        out_specs=VMEM,
        compiler_params=pltpu.CompilerParams(vmem_limit_bytes=4 << 20),
    )(fwd, fwd_in, rev, rev_in)


def refine_kernel(weight, bias, chip, own, core, out, *cur, layers):
    pairs, ways, comps, band_rows, width = own.shape
    high = 16
    total = pairs * ways * high
    band = (lax.axis_index("bh") * SIZES[3] + lax.axis_index("bz")) * SIZES[4] + lax.axis_index("bc")
    last = SIZES[2] * SIZES[3] * SIZES[4] - 1
    odd = lax.axis_index("bc") == 1
    for i in range(comps):
        for p in range(pairs):
            for d in range(ways):
                base = (p * ways + d) * high
                near, far = core[p, d, i], chip[p, d, i]
                cur[i][base : base + band_rows] = jnp.where(odd, near, far)
                cur[i][base + band_rows : base + 2 * band_rows] = own[p, d, i]
                cur[i][base + 2 * band_rows : base + 3 * band_rows] = jnp.where(odd, far, near)
                cur[i][base + 3 * band_rows : base + high] = jnp.zeros((high - 3 * band_rows, width), jnp.float32)
    row = lax.broadcasted_iota(jnp.int32, (total, width), 0) & (high - 1)
    lane = lax.broadcasted_iota(jnp.int32, (total, width), 1)
    low = jnp.where(band == 0, band_rows, 0)
    top = jnp.where(band == last, 2 * band_rows, 3 * band_rows)
    inside = ((row >= low) & (row < top)).astype(jnp.float32)
    keep_left = (lane > 0).astype(jnp.float32)
    keep_right = (lane < width - 1).astype(jnp.float32)
    for layer in range(layers):
        taps = []
        for i in range(comps):
            act = jnp.tanh(2.0 * cur[i][...]) * inside
            taps.append((pltpu.roll(act, 1, 1) * keep_left, act, pltpu.roll(act, width - 1, 1) * keep_right))
        for o in range(comps):
            lines = []
            for r in range(3):
                line = None
                for i in range(comps):
                    for c in range(3):
                        term = taps[i][c] * weight[(((layer * comps + o) * comps + i) * 3 + r) * 3 + c]
                        line = term if line is None else line + term
                lines.append(line)
            grown = pltpu.roll(lines[0], 1, 0) + lines[1] + pltpu.roll(lines[2], total - 1, 0)
            cur[o][...] = cur[o][...] + (grown + bias[layer * comps + o])
    for i in range(comps):
        for p in range(pairs):
            for d in range(ways):
                base = (p * ways + d) * high + band_rows
                out[p, d, i] = cur[i][base : base + band_rows]


def refine(weight, bias, chip, own, core):
    pairs, ways, comps, _, width = own.shape
    return pl.pallas_call(
        functools.partial(refine_kernel, layers=weight.shape[0]),
        out_shape=jax.ShapeDtypeStruct(own.shape, jnp.float32),
        in_specs=[SMEM, SMEM, VMEM, VMEM, VMEM],
        out_specs=VMEM,
        scratch_shapes=[pltpu.VMEM((pairs * ways * 16, width), jnp.float32)] * comps,
        compiler_params=pltpu.CompilerParams(vmem_limit_bytes=4 << 20),
    )(weight.reshape(-1), bias.reshape(-1), chip, own, core)


def gather_frames(blocks, table):
    orders = (
        (by_core(flip_y, flip_b), by_core(flip_a, flip_y), by_core(flip_b, flip_a)),
        (flip_a, flip_b, flip_y),
    )
    first = lax.optimization_barrier([hop(block, order[0]) for block, order in zip(blocks, orders)])
    held = [[block, piece] for block, piece in zip(blocks, first)]
    send = [jnp.concatenate(have, axis=0) for have in held]
    second = [hop(part, order[1]) for part, order in zip(send, orders)]
    tables = [hop(table, order[2]) for order in orders]
    second, tables = lax.optimization_barrier((second, tables))
    held = [have + [piece] for have, piece in zip(held, second)]
    sent = [hop(part, order[2]) for part, order in zip(offer(tables, held), orders)]
    return pick(table, [have + [piece] for have, piece in zip(held, sent)])


def matched(src0, tgt0):
    tgt1 = hop(tgt0, ring)
    tgt2 = hop(tgt0, back)
    src1 = hop(src0, flip_h)
    src2 = hop(src0, flip_c)
    tgt1, tgt2, src2 = lax.optimization_barrier((tgt1, tgt2, src2))
    tgt3 = hop(tgt1, ring)
    *own, scaled = match_early((src0, src2), (0, 2), tgt=(tgt0, tgt1, tgt2))
    src3 = hop(src1, flip_c)
    other = match_early((src1, src3), (1, 3), scaled=scaled)
    return match_late((src0, src1, src2, src3), (tgt0, tgt1, tgt2, tgt3), (*own, *other))


def shards(features, frame_pairs, conv_weight, conv_bias):
    frames, band_rows, width, chans = features.shape
    cells = band_rows * width
    flat_features = features.reshape(frames, cells, chans)
    cut = cells * 11 // 16
    src0, tgt0 = gather_frames([flat_features[:, :cut], flat_features[:, cut:]], frame_pairs)
    fwd_keep, fwd_send, rev_keep, rev_send = matched(src0, tgt0)
    fwd0, fwd1, rev0, rev1 = half(fwd_keep, hop(fwd_send, flip_c), rev_keep, hop(rev_send, flip_za), band_rows)
    flows = merge(fwd0, hop(fwd1, flip_h), rev0, hop(rev1, flip_zb), band_rows, width)
    chip = hop(flows, next_chip)
    core = hop(flows, flip_c)
    return refine(conv_weight, conv_bias, chip, flows, core)


def solution(mesh):
    finer = Mesh(mesh.devices.reshape(SIZES), AXES)
    frame, band = AXES[:2], AXES[2:]
    placed = (P(frame, band, None, None), P(frame, None), P(), P())
    return jax.shard_map(
        shards,
        mesh=finer,
        in_specs=placed,
        out_specs=P(frame, None, None, band, None),
        check_vma=False,
    )
```

```python
import functools
import itertools
import math

import jax
import jax.numpy as jnp
from jax import lax
from jax.experimental import pallas as pl
from jax.experimental.pallas import tpu as pltpu
from jax.sharding import Mesh
from jax.sharding import PartitionSpec as P

score_gain = 2.5
AXES = ("fx", "fy", "bh", "bz", "bc")
SIZES = (4, 2, 2, 4, 2)
VMEM = pl.BlockSpec(memory_space=pltpu.VMEM)
SMEM = pl.BlockSpec(memory_space=pltpu.SMEM)
NT = (((1,), (1,)), ((), ()))


def flat(coords):
    index = 0
    for value, size in zip(coords, SIZES):
        index = index * size + value
    return index


def hop(value, move):
    route = []
    for coords in itertools.product(*(range(size) for size in SIZES)):
        target = move(*coords)
        if target is not None:
            route.append((flat(coords), flat(target)))
    return lax.ppermute(value, AXES, route)


def flip_y(x, y, h, z, c):
    return x, 1 - y, h, z, c


def flip_a(x, y, h, z, c):
    return x ^ 1, y, h, z, c


def flip_b(x, y, h, z, c):
    return 3 - x, y, h, z, c


def flip_h(x, y, h, z, c):
    return x, y, 1 - h, z, c


def flip_c(x, y, h, z, c):
    return x, y, h, z, 1 - c


def flip_za(x, y, h, z, c):
    return x, y, h, z ^ 1, c


def flip_zb(x, y, h, z, c):
    return x, y, h, 3 - z, c


def ring(x, y, h, z, c):
    return x, y, h, (z + 1 - 2 * c) % SIZES[3], c


def back(x, y, h, z, c):
    return x, y, h, (z - 1 + 2 * c) % SIZES[3], c


def by_core(first, second):
    def move(*coords):
        return (second if coords[4] else first)(*coords)

    return move


def next_chip(x, y, h, z, c):
    band = (h * SIZES[3] + z) * SIZES[4] + c + 2 * c - 1
    if band < 0 or band >= SIZES[2] * SIZES[3] * SIZES[4]:
        return x, y, h, z, c
    return x, y, band // (SIZES[3] * SIZES[4]), band // SIZES[4] % SIZES[3], band % SIZES[4]


def gray(x):
    return (x ^ (x >> 1)) & 1, x >> 1


def seat(frame, frames):
    me_x, me_y, core = lax.axis_index("fx"), lax.axis_index("fy"), lax.axis_index("bc")
    me_a, me_b = gray(me_x)
    group = frame // frames
    to_a, to_b = gray(group // 2)
    fa, fb, fy = to_a ^ me_a, to_b ^ me_b, (group % 2) ^ me_y
    other = core == 1
    first = (jnp.where(other, fb, fy), jnp.where(other, fy, fa), jnp.where(other, fa, fb))
    return (first, (fa, fb, fy)), frame % frames


def copy_held(pieces, bits, which, frames, take, also=True):
    place = bits[0] + 2 * bits[1]
    for piece, low, span in zip(pieces, (0, 1, 2), (1, 1, 2)):

        @pl.when((place >= low) & (place < low + span) & also)
        def _():
            take(piece[(place - low) * frames + which])


def offer_kernel(*refs, parts):
    tables, pieces, outs = refs[:parts], refs[parts : 4 * parts], refs[4 * parts :]
    frames = pieces[0].shape[0]
    for v in range(parts):
        for slot in range(tables[v].shape[0]):
            for side in range(2):
                seats, which = seat(tables[v][slot, side], frames)

                def take(value):
                    outs[v][2 * slot + side] = value

                copy_held(pieces[3 * v : 3 * v + 3], seats[v], which, frames, take)


def offer(tables, held):
    pieces = [piece for have in held for piece in have]
    slots = 2 * tables[0].shape[0]
    return pl.pallas_call(
        functools.partial(offer_kernel, parts=len(held)),
        out_shape=[jax.ShapeDtypeStruct((slots,) + have[0].shape[1:], have[0].dtype) for have in held],
        in_specs=[SMEM] * len(held) + [VMEM] * len(pieces),
        out_specs=[VMEM] * len(held),
        compiler_params=pltpu.CompilerParams(vmem_limit_bytes=8 << 20),
    )(*tables, *pieces)


def pick_kernel(table, *refs, parts):
    pieces, outs = refs[: 4 * parts], refs[4 * parts :]
    frames = pieces[0].shape[0]
    for slot in range(table.shape[0]):
        for side in range(2):
            seats, which = seat(table[slot, side], frames)
            start = 0
            for v in range(parts):
                count = pieces[4 * v].shape[1]

                def take(value):
                    outs[side][slot, start : start + count] = value

                copy_held(pieces[4 * v : 4 * v + 3], seats[v], which, frames, take, seats[v][2] == 0)

                @pl.when(seats[v][2] == 1)
                def _():
                    take(pieces[4 * v + 3][2 * slot + side])

                start += count


def pick(table, held):
    pieces = [piece for have in held for piece in have]
    cells = sum(have[0].shape[1] for have in held)
    shape = jax.ShapeDtypeStruct((table.shape[0], cells, pieces[0].shape[2]), pieces[0].dtype)
    return pl.pallas_call(
        functools.partial(pick_kernel, parts=len(held)),
        out_shape=[shape, shape],
        in_specs=[SMEM] + [VMEM] * len(pieces),
        out_specs=[VMEM, VMEM],
        compiler_params=pltpu.CompilerParams(vmem_limit_bytes=12 << 20),
    )(table, *pieces)


def targets(refs, p, scale, rhs, start, cells):
    for j, ref in enumerate(refs):
        b = ref[p].astype(jnp.float32) * scale
        hi = b.astype(jnp.bfloat16)
        lo = (b - hi.astype(jnp.float32)).astype(jnp.bfloat16)
        rhs[(start + j) * cells : (start + j + 1) * cells, :] = jnp.concatenate([hi, lo], axis=1)


def places(cells, width):
    h, z, core = lax.axis_index("bh"), lax.axis_index("bz"), lax.axis_index("bc")
    src_place = [(h, core), (1 - h, core), (h, 1 - core), (1 - h, 1 - core)]
    src_band = [(hh * SIZES[3] + z) * SIZES[4] + cc for hh, cc in src_place]
    step = 1 - 2 * core
    tgt_z = [z, (z - step) % SIZES[3], (z + step) % SIZES[3], (z + 2) % SIZES[3]]
    tgt_band = [(h * SIZES[3] + zz) * SIZES[4] + core for zz in tgt_z]
    tgt_slot = [jnp.where(zz == z, 0, jnp.where(zz == 3 - z, 1, jnp.where(zz == (z ^ 1), 2, 3))) for zz in tgt_z]
    row = lambda band: (band * (cells // width)).astype(jnp.float32) - 27.5
    return [row(band) for band in src_band], [row(band) for band in tgt_band], tgt_slot


def chosen(values, index):
    return functools.reduce(lambda x, j: jnp.where(index == j, values[j], x), range(1, len(values)), values[0])


def block(sources, b, yj, src_rows, sums, cols, cells, width, shifts=None):
    band_rows = cells // width
    groups = width // 8
    a = jnp.concatenate(sources, axis=0)
    s = lax.dot_general(jnp.concatenate([a, a], axis=1), b, NT, preferred_element_type=jnp.float32)
    put, cols_first = cols
    for i in range(len(sources)):
        tt = [None] * band_rows
        uu = [None] * band_rows
        xx = [None] * band_rows
        for q in range(band_rows):
            ps = [None] * band_rows
            qs = [None] * band_rows
            for k in range(groups):
                r0 = i * cells + q * width + k * 8
                t = [s[r0 : r0 + 8, c * width : (c + 1) * width] for c in range(band_rows)]
                rows = slice(r0, r0 + 8)
                if shifts is None:
                    w = [jnp.exp2(x) for x in t]
                    v = w
                else:
                    m = shifts[0][rows, :]
                    w = [jnp.exp2(x - m) for x in t]
                    v = [jnp.exp2(x - shifts[1](c)) for c, x in enumerate(t)]
                a1 = w[0]
                b1 = w[0]
                for c in range(1, band_rows):
                    a1 = a1 + w[c]
                    b1 = b1 + a1
                sums(rows, a1, yj * a1 - b1)
                for c in range(band_rows):
                    ps[c] = v[c] if k == 0 else ps[c] + v[c]
                    qs[c] = ps[c] if k == 0 else qs[c] + ps[c]
            for c in range(band_rows):
                tt[c] = ps[c] if q == 0 else tt[c] + ps[c]
                uu[c] = tt[c] if q == 0 else uu[c] + tt[c]
                xx[c] = qs[c] if q == 0 else xx[c] + qs[c]
        for c in range(band_rows):
            put(slice(c * width, (c + 1) * width), i == 0 and cols_first, (tt[c], xx[c], src_rows[i] * tt[c] - uu[c]))


def early_kernel(*refs, which, bands, cells, width, given):
    nsrc, ntgt = len(which), len(bands)
    handed = bool(given)
    src, refs = refs[:nsrc], refs[nsrc:]
    if given:
        scaled, (acc, accy, g0, gq, gy) = refs[: len(given)], refs[len(given) :]
    else:
        tgt, (acc, accy, g0, gq, gy, rhs) = refs[:ntgt], refs[ntgt:]
        scaled, given = (rhs,), (ntgt,)
    seats = [(ref, n * cells) for ref, count in zip(scaled, given) for n in range(count)]
    src_rows, tgt_rows, _ = places(cells, width)
    src_rows = [src_rows[i] for i in which]
    scale = score_gain / math.sqrt(src[0].shape[-1]) * math.log2(math.e)

    def one(p, n, first):
        def sums(rows, total, rowed):
            acc[p, rows, :] = total if first else acc[p, rows, :] + total
            accy[p, rows, :] = rowed if first else accy[p, rows, :] + rowed

        def put(lanes, new, values):
            for ref, value in zip((g0, gq, gy), values):
                ref[p, n, :, lanes] = value if new else ref[p, n, :, lanes] + value

        ref, start = seats[n]
        b = ref[p, start : start + cells, :]
        block([ref[p] for ref in src], b, tgt_rows[bands[n]], src_rows, sums, (put, True), cells, width)

    def pair(p, carry):
        if not handed:
            targets(tgt, p, scale, scaled[0].at[p], 0, cells)
        for n in range(ntgt):
            one(p, n, n == 0)
        return carry

    lax.fori_loop(0, src[0].shape[0], pair, 0)


def late_kernel(*refs, nsrc, ntgt, cells, width, calls):
    src, tgt = refs[:nsrc], refs[nsrc : nsrc + ntgt]
    base = nsrc + ntgt
    before = [(*call, refs[base + 5 * n : base + 5 * n + 5]) for n, call in enumerate(calls)]
    fwd_keep, fwd_send, rev_keep, rev_send, rev, rhs, acc, accy, g0, gq, gy, shift_r, shift_c = refs[base + 5 * len(calls) :]
    fwd = [(fwd_keep, 0), (fwd_keep, 1), (fwd_send, 0), (fwd_send, 1)]
    band_rows = cells // width
    src_rows, tgt_rows, tgt_slot = places(cells, width)
    scale = score_gain / math.sqrt(src[0].shape[-1]) * math.log2(math.e)
    early = ntgt - 1
    lane = lax.broadcasted_iota(jnp.int32, (16, width), 1)
    row16 = lax.broadcasted_iota(jnp.int32, (16, width), 0)
    ramp = (2 * lane - (width - 1)).astype(jnp.float32)
    pick_rows = jnp.where(row16 == 0, 1.0, jnp.where(row16 == 1, ramp, 0.0)).astype(jnp.bfloat16)
    pick_rows = jnp.concatenate([pick_rows, pick_rows], axis=1)
    sub = lax.broadcasted_iota(jnp.int32, (8, width), 0).astype(jnp.float32)

    def safe(x):
        return jnp.all((x > 2.0**-90) & (x < 2.0**110))

    def lanes(ref, sl):
        x = ref[sl, :]
        hi = x.astype(jnp.bfloat16)
        lo = (x - hi.astype(jnp.float32)).astype(jnp.bfloat16)
        return lax.dot_general(pick_rows, jnp.concatenate([hi, lo], axis=1), NT, preferred_element_type=jnp.float32)

    def emit(p, cols_of, tops):
        ok = None
        for i in range(nsrc):
            sl = slice(i * cells, (i + 1) * cells)
            one = lanes(acc, sl)
            two = lanes(accy, sl)
            good = safe(one[0:1])
            ok = good if ok is None else ok & good
            ref, at = fwd[i]
            for r in range(band_rows):
                cs = slice(r * width, (r + 1) * width)
                ref[at, p, band_rows + r : band_rows + r + 1, :] = one[0:1, cs]
                ref[at, p, 2 * band_rows + r : 2 * band_rows + r + 1, :] = one[1:2, cs] * (1.0 / width)
                ref[at, p, 3 * band_rows + r : 3 * band_rows + r + 1, :] = two[0:1, cs] * (1.0 / 32)
                top = jnp.zeros((1, width), jnp.float32)
                if tops:
                    m = shift_r[i * cells + r * width : i * cells + (r + 1) * width, :]
                    top = jnp.transpose(m)[0:1, :]
                ref[at, p, r : r + 1, :] = top
        for j in range(ntgt):
            for r in range(band_rows):
                cs = slice(r * width, (r + 1) * width)
                t, xq, ty = cols_of(j, cs)
                tot = jnp.sum(t, axis=0, keepdims=True)
                ok = ok & safe(tot)
                slot = tgt_slot[j]
                x = (129.0 + 2.0 * sub) * t - 16.0 * xq
                rev[slot, p, band_rows + r : band_rows + r + 1, :] = tot
                rev[slot, p, 2 * band_rows + r : 2 * band_rows + r + 1, :] = jnp.sum(x, axis=0, keepdims=True) * (1.0 / width)
                rev[slot, p, 3 * band_rows + r : 3 * band_rows + r + 1, :] = jnp.sum(ty, axis=0, keepdims=True) * (1.0 / 32)
                rev[slot, p, r : r + 1, :] = shift_c[j, 0:1, cs] if tops else jnp.zeros((1, width), jnp.float32)
        return ok

    def put(jb):
        def inner(lane_slice, new, values):
            for ref, value in zip((g0, gq, gy), values):
                ref[jb, :, lane_slice] = value if new else ref[jb, :, lane_slice] + value

        return inner

    def pair(p, carry):
        targets(tgt[early:], p, scale, rhs, early, cells)
        sources = [ref[p] for ref in src]
        for jb in range(early, ntgt):

            def sums(rows, total, rowed):
                i, r0 = divmod(rows.start, cells)
                for which, _, old in before:
                    if i in which:
                        at = which.index(i) * cells + r0
                        total = total + old[0][p, at : at + 8, :]
                        rowed = rowed + old[1][p, at : at + 8, :]
                acc[rows, :] = total
                accy[rows, :] = rowed

            b = rhs[jb * cells : (jb + 1) * cells, :]
            block(sources, b, tgt_rows[jb], src_rows, sums, (put(jb), True), cells, width)

        def cols_of(j, cs):
            if j >= early:
                return g0[j, :, cs], gq[j, :, cs], gy[j, :, cs]
            olds = [(old, bands.index(j)) for _, bands, old in before if j in bands]
            return [functools.reduce(jnp.add, [old[n][p, at, :, cs] for old, at in olds]) for n in (2, 3, 4)]

        ok = emit(p, cols_of, False)

        @pl.when(jnp.logical_not(ok))
        def _():
            targets(tgt[:early], p, scale, rhs, 0, cells)
            shift_r[...] = jnp.full_like(shift_r, -1e30)
            shift_c[...] = jnp.full_like(shift_c, -1e30)

            def tops(jb, c):
                b = rhs[pl.ds(pl.multiple_of(jb * cells, cells), cells), :]
                for i in range(nsrc):

                    def part(q, c2):
                        a = src[i][p, pl.ds(pl.multiple_of(q * width, width), width), :]
                        s = lax.dot_general(jnp.concatenate([a, a], axis=1), b, NT, preferred_element_type=jnp.float32)
                        sl = pl.ds(pl.multiple_of(i * cells + q * width, width), width)
                        m = shift_r[sl, :]
                        for c3 in range(band_rows):
                            m = jnp.maximum(m, s[:, c3 * width : (c3 + 1) * width])
                        shift_r[sl, :] = m
                        t = shift_c[jb]
                        shift_c[jb] = jnp.maximum(t, jnp.broadcast_to(jnp.max(s, axis=0, keepdims=True), t.shape))
                        return c2

                    lax.fori_loop(0, band_rows, part, 0)
                return c

            lax.fori_loop(0, ntgt, tops, 0)

            def level(n, c):
                sl = pl.ds(pl.multiple_of(n * width, width), width)
                m = shift_r[sl, :]
                shift_r[sl, :] = jnp.broadcast_to(jnp.max(m, axis=1, keepdims=True), m.shape)
                return c

            lax.fori_loop(0, nsrc * band_rows, level, 0)
            acc[...] = jnp.zeros_like(acc)
            accy[...] = jnp.zeros_like(accy)

            def again(jb, c):
                def more(rows, total, rowed):
                    acc[rows, :] = acc[rows, :] + total
                    accy[rows, :] = accy[rows, :] + rowed

                shifts = (shift_r, lambda c4: shift_c[jb, :, c4 * width : (c4 + 1) * width])
                b = rhs[pl.ds(pl.multiple_of(jb * cells, cells), cells), :]
                block(sources, b, chosen(tgt_rows, jb), src_rows, more, (put(jb), True), cells, width, shifts)
                return c

            lax.fori_loop(0, ntgt, again, 0)
            emit(p, lambda j, cs: (g0[j, :, cs], gq[j, :, cs], gy[j, :, cs]), True)

        return carry

    lax.fori_loop(0, src[0].shape[0], pair, 0)
    rev_keep[...] = rev[0:2]
    rev_send[...] = rev[2:4]


def cost(pairs, blocks):
    return pl.CostEstimate(
        flops=134_000_000 * pairs * blocks, bytes_accessed=100_000 * pairs * blocks, transcendentals=262_144 * pairs * blocks
    )


def match_early(src, which, bands, tgt=None, scaled=()):
    pairs, cells, chans = src[0].shape
    width = 128
    nsrc, ntgt = len(src), len(bands)
    rows = jax.ShapeDtypeStruct((pairs, nsrc * cells, width), jnp.float32)
    cols = jax.ShapeDtypeStruct((pairs, ntgt, 8, cells), jnp.float32)
    shapes = [rows, rows, cols, cols, cols]
    if tgt:
        shapes.append(jax.ShapeDtypeStruct((pairs, ntgt * cells, 2 * chans), jnp.bfloat16))
    operands = (*src, *tgt) if tgt else (*src, *scaled)
    given = tuple(part.shape[1] // cells for part in scaled)
    return pl.pallas_call(
        functools.partial(early_kernel, which=which, bands=bands, cells=cells, width=width, given=given),
        out_shape=shapes,
        in_specs=[VMEM] * len(operands),
        out_specs=[VMEM] * len(shapes),
        compiler_params=pltpu.CompilerParams(vmem_limit_bytes=14 << 20),
        cost_estimate=cost(pairs, nsrc * ntgt),
    )(*operands)


def match_late(src, tgt, early, calls):
    pairs, cells, chans = src[0].shape
    width = 128
    nsrc, ntgt = len(src), len(tgt)
    stats = jax.ShapeDtypeStruct((2, pairs, 4 * cells // width, width), jnp.float32)
    return pl.pallas_call(
        functools.partial(late_kernel, nsrc=nsrc, ntgt=ntgt, cells=cells, width=width, calls=calls),
        out_shape=[stats] * 4,
        in_specs=[VMEM] * (nsrc + ntgt + len(early)),
        out_specs=[VMEM] * 4,
        scratch_shapes=[
            pltpu.VMEM((4,) + stats.shape[1:], jnp.float32),
            pltpu.VMEM((ntgt * cells, 2 * chans), jnp.bfloat16),
            pltpu.VMEM((nsrc * cells, width), jnp.float32),
            pltpu.VMEM((nsrc * cells, width), jnp.float32),
            pltpu.VMEM((ntgt, 8, cells), jnp.float32),
            pltpu.VMEM((ntgt, 8, cells), jnp.float32),
            pltpu.VMEM((ntgt, 8, cells), jnp.float32),
            pltpu.VMEM((nsrc * cells, width), jnp.float32),
            pltpu.VMEM((ntgt, 8, cells), jnp.float32),
        ],
        compiler_params=pltpu.CompilerParams(vmem_limit_bytes=24 << 20),
        cost_estimate=cost(pairs, nsrc),
    )(*src, *tgt, *early)


def joined(left, right, band_rows):
    part = lambda x, k: x[k * band_rows : (k + 1) * band_rows]
    top = jnp.maximum(part(left, 0), part(right, 0))
    scale_l = jnp.exp2(part(left, 0) - top)
    scale_r = jnp.exp2(part(right, 0) - top)
    return [top] + [part(left, k) * scale_l + part(right, k) * scale_r for k in range(1, 4)]


def half_kernel(fwd, fwd_in, rev, rev_in, *outs, band_rows):
    for way, (own, other) in enumerate(((fwd, fwd_in), (rev, rev_in))):
        for side in range(2):
            for p in range(own.shape[1]):
                for k, value in enumerate(joined(own[side, p], other[side, p], band_rows)):
                    outs[2 * way + side][p, k * band_rows : (k + 1) * band_rows] = value


def half(fwd, fwd_in, rev, rev_in, band_rows):
    shape = jax.ShapeDtypeStruct(fwd.shape[1:], jnp.float32)
    return pl.pallas_call(
        functools.partial(half_kernel, band_rows=band_rows),
        out_shape=[shape] * 4,
        in_specs=[VMEM] * 4,
        out_specs=[VMEM] * 4,
        compiler_params=pltpu.CompilerParams(vmem_limit_bytes=4 << 20),
    )(fwd, fwd_in, rev, rev_in)


def merge_kernel(fwd, fwd_in, rev, rev_in, out, *, band_rows, width):
    band = (lax.axis_index("bh") * SIZES[3] + lax.axis_index("bz")) * SIZES[4] + lax.axis_index("bc")
    col = (2 * lax.broadcasted_iota(jnp.int32, (band_rows, width), 1) - (width - 1)).astype(jnp.float32) * (1.0 / width)
    row = lax.broadcasted_iota(jnp.int32, (band_rows, width), 0) + band * band_rows
    row = (2 * row - 63).astype(jnp.float32) * (1.0 / 64)
    for p in range(out.shape[0]):
        for way, (own, other) in enumerate(((fwd, fwd_in), (rev, rev_in))):
            _, total, cols, rows = joined(own[p], other[p], band_rows)
            out[p, way, 0] = cols / total - col
            out[p, way, 1] = rows / total - row


def merge(fwd, fwd_in, rev, rev_in, band_rows, width):
    return pl.pallas_call(
        functools.partial(merge_kernel, band_rows=band_rows, width=width),
        out_shape=jax.ShapeDtypeStruct((fwd.shape[0], 2, 2, band_rows, width), jnp.float32),
        in_specs=[VMEM] * 4,
        out_specs=VMEM,
        compiler_params=pltpu.CompilerParams(vmem_limit_bytes=4 << 20),
    )(fwd, fwd_in, rev, rev_in)


def refine_kernel(weight, bias, chip, own, core, out, mask, *cur, layers):
    pairs, ways, comps, band_rows, width = own.shape
    high = 3 * band_rows
    total = pairs * ways * high
    band = (lax.axis_index("bh") * SIZES[3] + lax.axis_index("bz")) * SIZES[4] + lax.axis_index("bc")
    last = SIZES[2] * SIZES[3] * SIZES[4] - 1
    odd = lax.axis_index("bc") == 1
    full = lambda value: jnp.full((band_rows, width), value, jnp.float32)
    for p in range(pairs):
        for d in range(ways):
            base = (p * ways + d) * high
            mask[base : base + band_rows] = full(jnp.where(band == 0, 0.0, 1.0))
            mask[base + band_rows : base + 2 * band_rows] = full(1.0)
            mask[base + 2 * band_rows : base + high] = full(jnp.where(band == last, 0.0, 1.0))
            for i in range(comps):
                near, far = core[p, d, i], chip[p, d, i]
                cur[i][base : base + band_rows] = jnp.where(odd, near, far)
                cur[i][base + band_rows : base + 2 * band_rows] = own[p, d, i]
                cur[i][base + 2 * band_rows : base + high] = jnp.where(odd, far, near)
    inside = mask[...]
    lane = lax.broadcasted_iota(jnp.int32, (total, width), 1)
    keep_left = (lane > 0).astype(jnp.float32)
    keep_right = (lane < width - 1).astype(jnp.float32)
    for layer in range(layers):
        taps = []
        for i in range(comps):
            act = jnp.tanh(2.0 * cur[i][...]) * inside
            taps.append((pltpu.roll(act, 1, 1) * keep_left, act, pltpu.roll(act, width - 1, 1) * keep_right))
        for o in range(comps):
            lines = []
            for r in range(3):
                line = None
                for i in range(comps):
                    for c in range(3):
                        term = taps[i][c] * weight[(((layer * comps + o) * comps + i) * 3 + r) * 3 + c]
                        line = term if line is None else line + term
                lines.append(line)
            grown = pltpu.roll(lines[0], 1, 0) + lines[1] + pltpu.roll(lines[2], total - 1, 0)
            cur[o][...] = cur[o][...] + (grown + bias[layer * comps + o])
    for i in range(comps):
        for p in range(pairs):
            for d in range(ways):
                base = (p * ways + d) * high + band_rows
                out[p, d, i] = cur[i][base : base + band_rows]


def refine(weight, bias, chip, own, core):
    pairs, ways, comps, band_rows, width = own.shape
    return pl.pallas_call(
        functools.partial(refine_kernel, layers=weight.shape[0]),
        out_shape=jax.ShapeDtypeStruct(own.shape, jnp.float32),
        in_specs=[SMEM, SMEM, VMEM, VMEM, VMEM],
        out_specs=VMEM,
        scratch_shapes=[pltpu.VMEM((pairs * ways * 3 * band_rows, width), jnp.float32)] * (comps + 1),
        compiler_params=pltpu.CompilerParams(vmem_limit_bytes=4 << 20),
    )(weight.reshape(-1), bias.reshape(-1), chip, own, core)


def gather_frames(blocks, table):
    orders = (
        (by_core(flip_y, flip_b), by_core(flip_a, flip_y), by_core(flip_b, flip_a)),
        (flip_a, flip_b, flip_y),
    )
    first = lax.optimization_barrier([hop(block, order[0]) for block, order in zip(blocks, orders)])
    held = [[block, piece] for block, piece in zip(blocks, first)]
    send = [jnp.concatenate(have, axis=0) for have in held]
    second = [hop(part, order[1]) for part, order in zip(send, orders)]
    tables = [hop(table, order[2]) for order in orders]
    second, tables = lax.optimization_barrier((second, tables))
    held = [have + [piece] for have, piece in zip(held, second)]
    sent = [hop(part, order[2]) for part, order in zip(offer(tables, held), orders)]
    return pick(table, [have + [piece] for have, piece in zip(held, sent)])


def matched(src0, tgt0):
    tgt1 = hop(tgt0, ring)
    tgt2 = hop(tgt0, back)
    src1 = hop(src0, flip_h)
    src2 = hop(src0, flip_c)
    *own, scaled0 = match_early((src0, src2), (0, 2), (0,), tgt=(tgt0,))
    tgt3 = hop(tgt1, ring)
    *near, scaled1 = match_early((src0, src2), (0, 2), (1, 2), tgt=(tgt1, tgt2))
    src3 = hop(src1, flip_c)
    other = match_early((src1, src3), (1, 3), (0, 1, 2), scaled=(scaled0, scaled1))
    calls = (((0, 2), (0,)), ((0, 2), (1, 2)), ((1, 3), (0, 1, 2)))
    return match_late((src0, src1, src2, src3), (tgt0, tgt1, tgt2, tgt3), (*own, *near, *other), calls)


def shards(features, frame_pairs, conv_weight, conv_bias):
    frames, band_rows, width, chans = features.shape
    cells = band_rows * width
    flat_features = features.reshape(frames, cells, chans)
    cut = cells * 11 // 16
    src0, tgt0 = gather_frames([flat_features[:, :cut], flat_features[:, cut:]], frame_pairs)
    fwd_keep, fwd_send, rev_keep, rev_send = matched(src0, tgt0)
    fwd0, fwd1, rev0, rev1 = half(fwd_keep, hop(fwd_send, flip_c), rev_keep, hop(rev_send, flip_za), band_rows)
    flows = merge(fwd0, hop(fwd1, flip_h), rev0, hop(rev1, flip_zb), band_rows, width)
    chip = hop(flows, next_chip)
    core = hop(flows, flip_c)
    return refine(conv_weight, conv_bias, chip, flows, core)


def solution(mesh):
    finer = Mesh(mesh.devices.reshape(SIZES), AXES)
    frame, band = AXES[:2], AXES[2:]
    placed = (P(frame, band, None, None), P(frame, None), P(), P())
    return jax.shard_map(
        shards,
        mesh=finer,
        in_specs=placed,
        out_specs=P(frame, None, None, band, None),
        check_vma=False,
    )
```

```python
import functools
import itertools
import math

import jax
import jax.numpy as jnp
from jax import lax
from jax.experimental import pallas as pl
from jax.experimental.pallas import tpu as pltpu
from jax.sharding import Mesh
from jax.sharding import PartitionSpec as P

score_gain = 2.5
AXES = ("fx", "fy", "bh", "bz", "bc")
SIZES = (4, 2, 2, 4, 2)
VMEM = pl.BlockSpec(memory_space=pltpu.VMEM)
SMEM = pl.BlockSpec(memory_space=pltpu.SMEM)
NT = (((1,), (1,)), ((), ()))


def flat(coords):
    index = 0
    for value, size in zip(coords, SIZES):
        index = index * size + value
    return index


def hop(value, move):
    route = []
    for coords in itertools.product(*(range(size) for size in SIZES)):
        target = move(*coords)
        if target is not None:
            route.append((flat(coords), flat(target)))
    return lax.ppermute(value, AXES, route)


def flip_y(x, y, h, z, c):
    return x, 1 - y, h, z, c


def flip_a(x, y, h, z, c):
    return x ^ 1, y, h, z, c


def flip_b(x, y, h, z, c):
    return 3 - x, y, h, z, c


def flip_h(x, y, h, z, c):
    return x, y, 1 - h, z, c


def flip_c(x, y, h, z, c):
    return x, y, h, z, 1 - c


def flip_za(x, y, h, z, c):
    return x, y, h, z ^ 1, c


def flip_zb(x, y, h, z, c):
    return x, y, h, 3 - z, c


def ring(x, y, h, z, c):
    return x, y, h, (z + 1 - 2 * c) % SIZES[3], c


def back(x, y, h, z, c):
    return x, y, h, (z - 1 + 2 * c) % SIZES[3], c


def by_core(first, second):
    def move(*coords):
        return (second if coords[4] else first)(*coords)

    return move


def next_chip(x, y, h, z, c):
    band = (h * SIZES[3] + z) * SIZES[4] + c + 2 * c - 1
    if band < 0 or band >= SIZES[2] * SIZES[3] * SIZES[4]:
        return x, y, h, z, c
    return x, y, band // (SIZES[3] * SIZES[4]), band // SIZES[4] % SIZES[3], band % SIZES[4]


def gray(x):
    return (x ^ (x >> 1)) & 1, x >> 1


def seat(frame, frames):
    me_x, me_y, core = lax.axis_index("fx"), lax.axis_index("fy"), lax.axis_index("bc")
    me_a, me_b = gray(me_x)
    group = frame // frames
    to_a, to_b = gray(group // 2)
    fa, fb, fy = to_a ^ me_a, to_b ^ me_b, (group % 2) ^ me_y
    other = core == 1
    first = (jnp.where(other, fb, fy), jnp.where(other, fy, fa), jnp.where(other, fa, fb))
    return (first, (fa, fb, fy)), frame % frames


def copy_held(pieces, bits, which, frames, take, also=True):
    place = bits[0] + 2 * bits[1]
    for piece, low, span in zip(pieces, (0, 1, 2), (1, 1, 2)):

        @pl.when((place >= low) & (place < low + span) & also)
        def _():
            take(piece[(place - low) * frames + which])


def offer_kernel(*refs, parts):
    tables, pieces, outs = refs[:parts], refs[parts : 4 * parts], refs[4 * parts :]
    frames = pieces[0].shape[0]
    for v in range(parts):
        for slot in range(tables[v].shape[0]):
            for side in range(2):
                seats, which = seat(tables[v][slot, side], frames)

                def take(value):
                    outs[v][2 * slot + side] = value

                copy_held(pieces[3 * v : 3 * v + 3], seats[v], which, frames, take)


def offer(tables, held):
    pieces = [piece for have in held for piece in have]
    slots = 2 * tables[0].shape[0]
    return pl.pallas_call(
        functools.partial(offer_kernel, parts=len(held)),
        out_shape=[jax.ShapeDtypeStruct((slots,) + have[0].shape[1:], have[0].dtype) for have in held],
        in_specs=[SMEM] * len(held) + [VMEM] * len(pieces),
        out_specs=[VMEM] * len(held),
        compiler_params=pltpu.CompilerParams(vmem_limit_bytes=8 << 20),
    )(*tables, *pieces)


def pick_kernel(table, *refs, parts):
    pieces, outs = refs[: 4 * parts], refs[4 * parts :]
    frames = pieces[0].shape[0]
    for slot in range(table.shape[0]):
        for side in range(2):
            seats, which = seat(table[slot, side], frames)
            start = 0
            for v in range(parts):
                count = pieces[4 * v].shape[1]

                def take(value):
                    outs[side][slot, start : start + count] = value

                copy_held(pieces[4 * v : 4 * v + 3], seats[v], which, frames, take, seats[v][2] == 0)

                @pl.when(seats[v][2] == 1)
                def _():
                    take(pieces[4 * v + 3][2 * slot + side])

                start += count


def pick(table, held):
    pieces = [piece for have in held for piece in have]
    cells = sum(have[0].shape[1] for have in held)
    shape = jax.ShapeDtypeStruct((table.shape[0], cells, pieces[0].shape[2]), pieces[0].dtype)
    return pl.pallas_call(
        functools.partial(pick_kernel, parts=len(held)),
        out_shape=[shape, shape],
        in_specs=[SMEM] + [VMEM] * len(pieces),
        out_specs=[VMEM, VMEM],
        compiler_params=pltpu.CompilerParams(vmem_limit_bytes=12 << 20),
    )(table, *pieces)


def targets(refs, p, scale, rhs, start, cells):
    for j, ref in enumerate(refs):
        b = ref[p].astype(jnp.float32) * scale
        hi = b.astype(jnp.bfloat16)
        lo = (b - hi.astype(jnp.float32)).astype(jnp.bfloat16)
        rhs[(start + j) * cells : (start + j + 1) * cells, :] = jnp.concatenate([hi, lo], axis=1)


def places(cells, width):
    h, z, core = lax.axis_index("bh"), lax.axis_index("bz"), lax.axis_index("bc")
    src_place = [(h, core), (1 - h, core), (h, 1 - core), (1 - h, 1 - core)]
    src_band = [(hh * SIZES[3] + z) * SIZES[4] + cc for hh, cc in src_place]
    step = 1 - 2 * core
    tgt_z = [z, (z - step) % SIZES[3], (z + step) % SIZES[3], (z + 2) % SIZES[3]]
    tgt_band = [(h * SIZES[3] + zz) * SIZES[4] + core for zz in tgt_z]
    tgt_slot = [jnp.where(zz == z, 0, jnp.where(zz == 3 - z, 1, jnp.where(zz == (z ^ 1), 2, 3))) for zz in tgt_z]
    row = lambda band: (band * (cells // width)).astype(jnp.float32) - 27.5
    return [row(band) for band in src_band], [row(band) for band in tgt_band], tgt_slot


def chosen(values, index):
    return functools.reduce(lambda x, j: jnp.where(index == j, values[j], x), range(1, len(values)), values[0])


def block(sources, b, yj, src_rows, sums, cols, cells, width, shifts=None):
    band_rows = cells // width
    groups = width // 8
    a = jnp.concatenate(sources, axis=0)
    s = lax.dot_general(jnp.concatenate([a, a], axis=1), b, NT, preferred_element_type=jnp.float32)
    put, cols_first = cols
    for i in range(len(sources)):
        tt = [None] * band_rows
        uu = [None] * band_rows
        xx = [None] * band_rows
        for q in range(band_rows):
            ps = [None] * band_rows
            qs = [None] * band_rows
            for k in range(groups):
                r0 = i * cells + q * width + k * 8
                t = [s[r0 : r0 + 8, c * width : (c + 1) * width] for c in range(band_rows)]
                rows = slice(r0, r0 + 8)
                if shifts is None:
                    w = [jnp.exp2(x) for x in t]
                    v = w
                else:
                    m = shifts[0][rows, :]
                    w = [jnp.exp2(x - m) for x in t]
                    v = [jnp.exp2(x - shifts[1](c)) for c, x in enumerate(t)]
                a1 = w[0]
                b1 = w[0]
                for c in range(1, band_rows):
                    a1 = a1 + w[c]
                    b1 = b1 + a1
                sums(rows, a1, yj * a1 - b1)
                for c in range(band_rows):
                    ps[c] = v[c] if k == 0 else ps[c] + v[c]
                    qs[c] = ps[c] if k == 0 else qs[c] + ps[c]
            for c in range(band_rows):
                tt[c] = ps[c] if q == 0 else tt[c] + ps[c]
                uu[c] = tt[c] if q == 0 else uu[c] + tt[c]
                xx[c] = qs[c] if q == 0 else xx[c] + qs[c]
        for c in range(band_rows):
            put(slice(c * width, (c + 1) * width), i == 0 and cols_first, (tt[c], xx[c], src_rows[i] * tt[c] - uu[c]))


def early_kernel(*refs, which, bands, cells, width, given):
    nsrc, ntgt = len(which), len(bands)
    handed = bool(given)
    src, refs = refs[:nsrc], refs[nsrc:]
    if given:
        scaled, (acc, accy, g0, gq, gy) = refs[: len(given)], refs[len(given) :]
    else:
        tgt, (acc, accy, g0, gq, gy, rhs) = refs[:ntgt], refs[ntgt:]
        scaled, given = (rhs,), (ntgt,)
    seats = [(ref, n * cells) for ref, count in zip(scaled, given) for n in range(count)]
    src_rows, tgt_rows, _ = places(cells, width)
    src_rows = [src_rows[i] for i in which]
    scale = score_gain / math.sqrt(src[0].shape[-1]) * math.log2(math.e)

    def one(p, n, first):
        def sums(rows, total, rowed):
            acc[p, rows, :] = total if first else acc[p, rows, :] + total
            accy[p, rows, :] = rowed if first else accy[p, rows, :] + rowed

        def put(lanes, new, values):
            for ref, value in zip((g0, gq, gy), values):
                ref[p, n, :, lanes] = value if new else ref[p, n, :, lanes] + value

        ref, start = seats[n]
        b = ref[p, start : start + cells, :]
        block([ref[p] for ref in src], b, tgt_rows[bands[n]], src_rows, sums, (put, True), cells, width)

    def pair(p, carry):
        if not handed:
            targets(tgt, p, scale, scaled[0].at[p], 0, cells)
        for n in range(ntgt):
            one(p, n, n == 0)
        return carry

    lax.fori_loop(0, src[0].shape[0], pair, 0)


def late_kernel(*refs, nsrc, ntgt, cells, width, calls):
    src, tgt = refs[:nsrc], refs[nsrc : nsrc + ntgt]
    base = nsrc + ntgt
    before = [(*call, refs[base + 5 * n : base + 5 * n + 5]) for n, call in enumerate(calls)]
    fwd_keep, fwd_send, rev_keep, rev_send, rev, rhs, acc, accy, g0, gq, gy, shift_r, shift_c = refs[base + 5 * len(calls) :]
    fwd = [(fwd_keep, 0), (fwd_keep, 1), (fwd_send, 0), (fwd_send, 1)]
    band_rows = cells // width
    src_rows, tgt_rows, tgt_slot = places(cells, width)
    scale = score_gain / math.sqrt(src[0].shape[-1]) * math.log2(math.e)
    early = ntgt - 1
    lane = lax.broadcasted_iota(jnp.int32, (16, width), 1)
    row16 = lax.broadcasted_iota(jnp.int32, (16, width), 0)
    ramp = (2 * lane - (width - 1)).astype(jnp.float32)
    pick_rows = jnp.where(row16 == 0, 1.0, jnp.where(row16 == 1, ramp, 0.0)).astype(jnp.bfloat16)
    pick_rows = jnp.concatenate([pick_rows, pick_rows], axis=1)
    sub = lax.broadcasted_iota(jnp.int32, (8, width), 0).astype(jnp.float32)

    def safe(x):
        return jnp.all((x > 2.0**-90) & (x < 2.0**110))

    def lanes(ref, sl):
        x = ref[sl, :]
        hi = x.astype(jnp.bfloat16)
        lo = (x - hi.astype(jnp.float32)).astype(jnp.bfloat16)
        return lax.dot_general(pick_rows, jnp.concatenate([hi, lo], axis=1), NT, preferred_element_type=jnp.float32)

    def emit(p, cols_of, tops):
        ok = None
        for i in range(nsrc):
            sl = slice(i * cells, (i + 1) * cells)
            one = lanes(acc, sl)
            two = lanes(accy, sl)
            good = safe(one[0:1])
            ok = good if ok is None else ok & good
            ref, at = fwd[i]
            for r in range(band_rows):
                cs = slice(r * width, (r + 1) * width)
                ref[at, p, band_rows + r : band_rows + r + 1, :] = one[0:1, cs]
                ref[at, p, 2 * band_rows + r : 2 * band_rows + r + 1, :] = one[1:2, cs] * (1.0 / width)
                ref[at, p, 3 * band_rows + r : 3 * band_rows + r + 1, :] = two[0:1, cs] * (1.0 / 32)
                top = jnp.zeros((1, width), jnp.float32)
                if tops:
                    m = shift_r[i * cells + r * width : i * cells + (r + 1) * width, :]
                    top = jnp.transpose(m)[0:1, :]
                ref[at, p, r : r + 1, :] = top
        for j in range(ntgt):
            for r in range(band_rows):
                cs = slice(r * width, (r + 1) * width)
                t, xq, ty = cols_of(j, cs)
                tot = jnp.sum(t, axis=0, keepdims=True)
                ok = ok & safe(tot)
                slot = tgt_slot[j]
                x = (129.0 + 2.0 * sub) * t - 16.0 * xq
                rev[slot, p, band_rows + r : band_rows + r + 1, :] = tot
                rev[slot, p, 2 * band_rows + r : 2 * band_rows + r + 1, :] = jnp.sum(x, axis=0, keepdims=True) * (1.0 / width)
                rev[slot, p, 3 * band_rows + r : 3 * band_rows + r + 1, :] = jnp.sum(ty, axis=0, keepdims=True) * (1.0 / 32)
                rev[slot, p, r : r + 1, :] = shift_c[j, 0:1, cs] if tops else jnp.zeros((1, width), jnp.float32)
        return ok

    def put(jb):
        def inner(lane_slice, new, values):
            for ref, value in zip((g0, gq, gy), values):
                ref[jb, :, lane_slice] = value if new else ref[jb, :, lane_slice] + value

        return inner

    def pair(p, carry):
        targets(tgt[early:], p, scale, rhs, early, cells)
        sources = [ref[p] for ref in src]
        for jb in range(early, ntgt):

            def sums(rows, total, rowed):
                i, r0 = divmod(rows.start, cells)
                for which, _, old in before:
                    if i in which:
                        at = which.index(i) * cells + r0
                        total = total + old[0][p, at : at + 8, :]
                        rowed = rowed + old[1][p, at : at + 8, :]
                acc[rows, :] = total
                accy[rows, :] = rowed

            b = rhs[jb * cells : (jb + 1) * cells, :]
            block(sources, b, tgt_rows[jb], src_rows, sums, (put(jb), True), cells, width)

        def cols_of(j, cs):
            if j >= early:
                return g0[j, :, cs], gq[j, :, cs], gy[j, :, cs]
            olds = [(old, bands.index(j)) for _, bands, old in before if j in bands]
            return [functools.reduce(jnp.add, [old[n][p, at, :, cs] for old, at in olds]) for n in (2, 3, 4)]

        ok = emit(p, cols_of, False)

        @pl.when(jnp.logical_not(ok))
        def _():
            targets(tgt[:early], p, scale, rhs, 0, cells)
            shift_r[...] = jnp.full_like(shift_r, -1e30)
            shift_c[...] = jnp.full_like(shift_c, -1e30)

            def tops(jb, c):
                b = rhs[pl.ds(pl.multiple_of(jb * cells, cells), cells), :]
                for i in range(nsrc):

                    def part(q, c2):
                        a = src[i][p, pl.ds(pl.multiple_of(q * width, width), width), :]
                        s = lax.dot_general(jnp.concatenate([a, a], axis=1), b, NT, preferred_element_type=jnp.float32)
                        sl = pl.ds(pl.multiple_of(i * cells + q * width, width), width)
                        m = shift_r[sl, :]
                        for c3 in range(band_rows):
                            m = jnp.maximum(m, s[:, c3 * width : (c3 + 1) * width])
                        shift_r[sl, :] = m
                        t = shift_c[jb]
                        shift_c[jb] = jnp.maximum(t, jnp.broadcast_to(jnp.max(s, axis=0, keepdims=True), t.shape))
                        return c2

                    lax.fori_loop(0, band_rows, part, 0)
                return c

            lax.fori_loop(0, ntgt, tops, 0)

            def level(n, c):
                sl = pl.ds(pl.multiple_of(n * width, width), width)
                m = shift_r[sl, :]
                shift_r[sl, :] = jnp.broadcast_to(jnp.max(m, axis=1, keepdims=True), m.shape)
                return c

            lax.fori_loop(0, nsrc * band_rows, level, 0)
            acc[...] = jnp.zeros_like(acc)
            accy[...] = jnp.zeros_like(accy)

            def again(jb, c):
                def more(rows, total, rowed):
                    acc[rows, :] = acc[rows, :] + total
                    accy[rows, :] = accy[rows, :] + rowed

                shifts = (shift_r, lambda c4: shift_c[jb, :, c4 * width : (c4 + 1) * width])
                b = rhs[pl.ds(pl.multiple_of(jb * cells, cells), cells), :]
                block(sources, b, chosen(tgt_rows, jb), src_rows, more, (put(jb), True), cells, width, shifts)
                return c

            lax.fori_loop(0, ntgt, again, 0)
            emit(p, lambda j, cs: (g0[j, :, cs], gq[j, :, cs], gy[j, :, cs]), True)

        return carry

    lax.fori_loop(0, src[0].shape[0], pair, 0)
    rev_keep[...] = rev[0:2]
    rev_send[...] = rev[2:4]


def cost(pairs, blocks):
    return pl.CostEstimate(
        flops=134_000_000 * pairs * blocks, bytes_accessed=100_000 * pairs * blocks, transcendentals=262_144 * pairs * blocks
    )


def match_early(src, which, bands, tgt=None, scaled=()):
    pairs, cells, chans = src[0].shape
    width = 128
    nsrc, ntgt = len(src), len(bands)
    rows = jax.ShapeDtypeStruct((pairs, nsrc * cells, width), jnp.float32)
    cols = jax.ShapeDtypeStruct((pairs, ntgt, 8, cells), jnp.float32)
    shapes = [rows, rows, cols, cols, cols]
    if tgt:
        shapes.append(jax.ShapeDtypeStruct((pairs, ntgt * cells, 2 * chans), jnp.bfloat16))
    operands = (*src, *tgt) if tgt else (*src, *scaled)
    given = tuple(part.shape[1] // cells for part in scaled)
    return pl.pallas_call(
        functools.partial(early_kernel, which=which, bands=bands, cells=cells, width=width, given=given),
        out_shape=shapes,
        in_specs=[VMEM] * len(operands),
        out_specs=[VMEM] * len(shapes),
        compiler_params=pltpu.CompilerParams(vmem_limit_bytes=14 << 20),
        cost_estimate=cost(pairs, nsrc * ntgt),
    )(*operands)


def match_late(src, tgt, early, calls):
    pairs, cells, chans = src[0].shape
    width = 128
    nsrc, ntgt = len(src), len(tgt)
    stats = jax.ShapeDtypeStruct((2, pairs, 4 * cells // width, width), jnp.float32)
    return pl.pallas_call(
        functools.partial(late_kernel, nsrc=nsrc, ntgt=ntgt, cells=cells, width=width, calls=calls),
        out_shape=[stats] * 4,
        in_specs=[VMEM] * (nsrc + ntgt + len(early)),
        out_specs=[VMEM] * 4,
        scratch_shapes=[
            pltpu.VMEM((4,) + stats.shape[1:], jnp.float32),
            pltpu.VMEM((ntgt * cells, 2 * chans), jnp.bfloat16),
            pltpu.VMEM((nsrc * cells, width), jnp.float32),
            pltpu.VMEM((nsrc * cells, width), jnp.float32),
            pltpu.VMEM((ntgt, 8, cells), jnp.float32),
            pltpu.VMEM((ntgt, 8, cells), jnp.float32),
            pltpu.VMEM((ntgt, 8, cells), jnp.float32),
            pltpu.VMEM((nsrc * cells, width), jnp.float32),
            pltpu.VMEM((ntgt, 8, cells), jnp.float32),
        ],
        compiler_params=pltpu.CompilerParams(vmem_limit_bytes=24 << 20),
        cost_estimate=cost(pairs, nsrc),
    )(*src, *tgt, *early)


def joined(left, right, band_rows):
    part = lambda x, k: x[k * band_rows : (k + 1) * band_rows]
    top = jnp.maximum(part(left, 0), part(right, 0))
    scale_l = jnp.exp2(part(left, 0) - top)
    scale_r = jnp.exp2(part(right, 0) - top)
    return [top] + [part(left, k) * scale_l + part(right, k) * scale_r for k in range(1, 4)]


def half_kernel(fwd, fwd_in, rev, rev_in, *outs, band_rows):
    for way, (own, other) in enumerate(((fwd, fwd_in), (rev, rev_in))):
        for side in range(2):
            for p in range(own.shape[1]):
                for k, value in enumerate(joined(own[side, p], other[side, p], band_rows)):
                    outs[2 * way + side][p, k * band_rows : (k + 1) * band_rows] = value


def half(fwd, fwd_in, rev, rev_in, band_rows):
    shape = jax.ShapeDtypeStruct(fwd.shape[1:], jnp.float32)
    return pl.pallas_call(
        functools.partial(half_kernel, band_rows=band_rows),
        out_shape=[shape] * 4,
        in_specs=[VMEM] * 4,
        out_specs=[VMEM] * 4,
        compiler_params=pltpu.CompilerParams(vmem_limit_bytes=4 << 20),
    )(fwd, fwd_in, rev, rev_in)


def merge_kernel(fwd, fwd_in, rev, rev_in, out, *, band_rows, width):
    band = (lax.axis_index("bh") * SIZES[3] + lax.axis_index("bz")) * SIZES[4] + lax.axis_index("bc")
    col = (2 * lax.broadcasted_iota(jnp.int32, (band_rows, width), 1) - (width - 1)).astype(jnp.float32) * (1.0 / width)
    row = lax.broadcasted_iota(jnp.int32, (band_rows, width), 0) + band * band_rows
    row = (2 * row - 63).astype(jnp.float32) * (1.0 / 64)
    for p in range(out.shape[0]):
        for way, (own, other) in enumerate(((fwd, fwd_in), (rev, rev_in))):
            _, total, cols, rows = joined(own[p], other[p], band_rows)
            out[p, way, 0] = cols / total - col
            out[p, way, 1] = rows / total - row


def merge(fwd, fwd_in, rev, rev_in, band_rows, width):
    return pl.pallas_call(
        functools.partial(merge_kernel, band_rows=band_rows, width=width),
        out_shape=jax.ShapeDtypeStruct((fwd.shape[0], 2, 2, band_rows, width), jnp.float32),
        in_specs=[VMEM] * 4,
        out_specs=VMEM,
        compiler_params=pltpu.CompilerParams(vmem_limit_bytes=4 << 20),
    )(fwd, fwd_in, rev, rev_in)


def refine_kernel(weight, bias, chip, own, core, out, mask, *cur, layers):
    pairs, ways, comps, band_rows, width = own.shape
    high = 3 * band_rows
    total = pairs * ways * high
    band = (lax.axis_index("bh") * SIZES[3] + lax.axis_index("bz")) * SIZES[4] + lax.axis_index("bc")
    last = SIZES[2] * SIZES[3] * SIZES[4] - 1
    odd = lax.axis_index("bc") == 1
    full = lambda value: jnp.full((band_rows, width), value, jnp.float32)
    for p in range(pairs):
        for d in range(ways):
            base = (p * ways + d) * high
            mask[base : base + band_rows] = full(jnp.where(band == 0, 0.0, 1.0))
            mask[base + band_rows : base + 2 * band_rows] = full(1.0)
            mask[base + 2 * band_rows : base + high] = full(jnp.where(band == last, 0.0, 1.0))
            for i in range(comps):
                near, far = core[p, d, i], chip[p, d, i]
                cur[i][base : base + band_rows] = jnp.where(odd, near, far)
                cur[i][base + band_rows : base + 2 * band_rows] = own[p, d, i]
                cur[i][base + 2 * band_rows : base + high] = jnp.where(odd, far, near)
    inside = mask[...]
    lane = lax.broadcasted_iota(jnp.int32, (total, width), 1)
    keep_left = (lane > 0).astype(jnp.float32)
    keep_right = (lane < width - 1).astype(jnp.float32)
    for layer in range(layers):
        taps = []
        for i in range(comps):
            act = jnp.tanh(2.0 * cur[i][...]) * inside
            taps.append((pltpu.roll(act, 1, 1) * keep_left, act, pltpu.roll(act, width - 1, 1) * keep_right))
        for o in range(comps):
            lines = []
            for r in range(3):
                line = None
                for i in range(comps):
                    for c in range(3):
                        term = taps[i][c] * weight[(((layer * comps + o) * comps + i) * 3 + r) * 3 + c]
                        line = term if line is None else line + term
                lines.append(line)
            grown = pltpu.roll(lines[0], 1, 0) + lines[1] + pltpu.roll(lines[2], total - 1, 0)
            cur[o][...] = cur[o][...] + (grown + bias[layer * comps + o])
    for i in range(comps):
        for p in range(pairs):
            for d in range(ways):
                base = (p * ways + d) * high + band_rows
                out[p, d, i] = cur[i][base : base + band_rows]


def refine(weight, bias, chip, own, core):
    pairs, ways, comps, band_rows, width = own.shape
    return pl.pallas_call(
        functools.partial(refine_kernel, layers=weight.shape[0]),
        out_shape=jax.ShapeDtypeStruct(own.shape, jnp.float32),
        in_specs=[SMEM, SMEM, VMEM, VMEM, VMEM],
        out_specs=VMEM,
        scratch_shapes=[pltpu.VMEM((pairs * ways * 3 * band_rows, width), jnp.float32)] * (comps + 1),
        compiler_params=pltpu.CompilerParams(vmem_limit_bytes=4 << 20),
    )(weight.reshape(-1), bias.reshape(-1), chip, own, core)


def split_kernel(whole, first, second):
    cut = first.shape[1]
    first[...] = whole[:, :cut]
    second[...] = whole[:, cut:]


def split(whole, cut):
    frames, cells, chans = whole.shape
    return pl.pallas_call(
        split_kernel,
        out_shape=[jax.ShapeDtypeStruct((frames, size, chans), whole.dtype) for size in (cut, cells - cut)],
        in_specs=[VMEM],
        out_specs=[VMEM, VMEM],
        compiler_params=pltpu.CompilerParams(vmem_limit_bytes=4 << 20),
    )(whole)


def gather_frames(blocks, table):
    orders = (
        (by_core(flip_y, flip_b), by_core(flip_a, flip_y), by_core(flip_b, flip_a)),
        (flip_a, flip_b, flip_y),
    )
    first = lax.optimization_barrier([hop(block, order[0]) for block, order in zip(blocks, orders)])
    held = [[block, piece] for block, piece in zip(blocks, first)]
    send = [jnp.concatenate(have, axis=0) for have in held]
    second = [hop(part, order[1]) for part, order in zip(send, orders)]
    tables = [hop(table, order[2]) for order in orders]
    second, tables = lax.optimization_barrier((second, tables))
    held = [have + [piece] for have, piece in zip(held, second)]
    sent = [hop(part, order[2]) for part, order in zip(offer(tables, held), orders)]
    return pick(table, [have + [piece] for have, piece in zip(held, sent)])


def matched(src0, tgt0):
    tgt1 = hop(tgt0, ring)
    tgt2 = hop(tgt0, back)
    src1 = hop(src0, flip_h)
    src2 = hop(src0, flip_c)
    *own, scaled0 = match_early((src0, src2), (0, 2), (0,), tgt=(tgt0,))
    tgt3 = hop(tgt1, ring)
    *near, scaled1 = match_early((src0, src2), (0, 2), (1, 2), tgt=(tgt1, tgt2))
    src3 = hop(src1, flip_c)
    other = match_early((src1, src3), (1, 3), (0, 1, 2), scaled=(scaled0, scaled1))
    calls = (((0, 2), (0,)), ((0, 2), (1, 2)), ((1, 3), (0, 1, 2)))
    return match_late((src0, src1, src2, src3), (tgt0, tgt1, tgt2, tgt3), (*own, *near, *other), calls)


def shards(features, frame_pairs, conv_weight, conv_bias):
    frames, band_rows, width, chans = features.shape
    cells = band_rows * width
    flat_features = features.reshape(frames, cells, chans)
    src0, tgt0 = gather_frames(split(flat_features, cells * 19 // 32), frame_pairs)
    fwd_keep, fwd_send, rev_keep, rev_send = matched(src0, tgt0)
    fwd0, fwd1, rev0, rev1 = half(fwd_keep, hop(fwd_send, flip_c), rev_keep, hop(rev_send, flip_za), band_rows)
    flows = merge(fwd0, hop(fwd1, flip_h), rev0, hop(rev1, flip_zb), band_rows, width)
    chip = hop(flows, next_chip)
    core = hop(flows, flip_c)
    return refine(conv_weight, conv_bias, chip, flows, core)


def solution(mesh):
    finer = Mesh(mesh.devices.reshape(SIZES), AXES)
    frame, band = AXES[:2], AXES[2:]
    placed = (P(frame, band, None, None), P(frame, None), P(), P())
    return jax.shard_map(
        shards,
        mesh=finer,
        in_specs=placed,
        out_specs=P(frame, None, None, band, None),
        check_vma=False,
    )
```

```python
import functools
import itertools
import math

import jax
import jax.numpy as jnp
from jax import lax
from jax.experimental import pallas as pl
from jax.experimental.pallas import tpu as pltpu
from jax.sharding import Mesh
from jax.sharding import PartitionSpec as P

score_gain = 2.5
AXES = ("fx", "fy", "bh", "bz", "bc")
SIZES = (4, 2, 2, 4, 2)
VMEM = pl.BlockSpec(memory_space=pltpu.VMEM)
SMEM = pl.BlockSpec(memory_space=pltpu.SMEM)
NT = (((1,), (1,)), ((), ()))


def flat(coords):
    index = 0
    for value, size in zip(coords, SIZES):
        index = index * size + value
    return index


def hop(value, move):
    route = []
    for coords in itertools.product(*(range(size) for size in SIZES)):
        target = move(*coords)
        if target is not None:
            route.append((flat(coords), flat(target)))
    return lax.ppermute(value, AXES, route)


def flip_y(x, y, h, z, c):
    return x, 1 - y, h, z, c


def flip_a(x, y, h, z, c):
    return x ^ 1, y, h, z, c


def flip_b(x, y, h, z, c):
    return 3 - x, y, h, z, c


def flip_h(x, y, h, z, c):
    return x, y, 1 - h, z, c


def flip_c(x, y, h, z, c):
    return x, y, h, z, 1 - c


def flip_za(x, y, h, z, c):
    return x, y, h, z ^ 1, c


def flip_zb(x, y, h, z, c):
    return x, y, h, 3 - z, c


def ring(x, y, h, z, c):
    return x, y, h, (z + 1 - 2 * c) % SIZES[3], c


def back(x, y, h, z, c):
    return x, y, h, (z - 1 + 2 * c) % SIZES[3], c


def by_core(first, second):
    def move(*coords):
        return (second if coords[4] else first)(*coords)

    return move


def next_chip(x, y, h, z, c):
    band = (h * SIZES[3] + z) * SIZES[4] + c + 2 * c - 1
    if band < 0 or band >= SIZES[2] * SIZES[3] * SIZES[4]:
        return x, y, h, z, c
    return x, y, band // (SIZES[3] * SIZES[4]), band // SIZES[4] % SIZES[3], band % SIZES[4]


def gray(x):
    return (x ^ (x >> 1)) & 1, x >> 1


def seat(frame, frames):
    me_x, me_y, core = lax.axis_index("fx"), lax.axis_index("fy"), lax.axis_index("bc")
    me_a, me_b = gray(me_x)
    group = frame // frames
    to_a, to_b = gray(group // 2)
    fa, fb, fy = to_a ^ me_a, to_b ^ me_b, (group % 2) ^ me_y
    other = core == 1
    first = (jnp.where(other, fb, fy), jnp.where(other, fy, fa), jnp.where(other, fa, fb))
    return (first, (fa, fb, fy)), frame % frames


def copy_held(pieces, bits, which, frames, take, also=True):
    for side, piece in enumerate(pieces):

        @pl.when((bits[1] == side) & also)
        def _():
            take(piece[bits[0] * frames + which])


def offer_kernel(*refs, parts):
    tables, pieces, outs = refs[:parts], refs[parts : 3 * parts], refs[3 * parts :]
    frames = pieces[0].shape[0] // 2
    for v in range(parts):
        for slot in range(tables[v].shape[0]):
            for side in range(2):
                seats, which = seat(tables[v][slot, side], frames)

                def take(value):
                    outs[v][2 * slot + side] = value

                copy_held(pieces[2 * v : 2 * v + 2], seats[v], which, frames, take)


def offer(tables, held):
    pieces = [piece for have in held for piece in have]
    slots = 2 * tables[0].shape[0]
    return pl.pallas_call(
        functools.partial(offer_kernel, parts=len(held)),
        out_shape=[jax.ShapeDtypeStruct((slots,) + have[0].shape[1:], have[0].dtype) for have in held],
        in_specs=[SMEM] * len(held) + [VMEM] * len(pieces),
        out_specs=[VMEM] * len(held),
        compiler_params=pltpu.CompilerParams(vmem_limit_bytes=8 << 20),
    )(*tables, *pieces)


def pick_kernel(table, *refs, parts):
    pieces, outs = refs[: 3 * parts], refs[3 * parts :]
    frames = pieces[0].shape[0] // 2
    for slot in range(table.shape[0]):
        for side in range(2):
            seats, which = seat(table[slot, side], frames)
            start = 0
            for v in range(parts):
                count = pieces[3 * v].shape[1]

                def take(value):
                    outs[side][slot, start : start + count] = value

                copy_held(pieces[3 * v : 3 * v + 2], seats[v], which, frames, take, seats[v][2] == 0)

                @pl.when(seats[v][2] == 1)
                def _():
                    take(pieces[3 * v + 2][2 * slot + side])

                start += count


def pick(table, held):
    pieces = [piece for have in held for piece in have]
    cells = sum(have[0].shape[1] for have in held)
    shape = jax.ShapeDtypeStruct((table.shape[0], cells, pieces[0].shape[2]), pieces[0].dtype)
    return pl.pallas_call(
        functools.partial(pick_kernel, parts=len(held)),
        out_shape=[shape, shape],
        in_specs=[SMEM] + [VMEM] * len(pieces),
        out_specs=[VMEM, VMEM],
        compiler_params=pltpu.CompilerParams(vmem_limit_bytes=12 << 20),
    )(table, *pieces)


def targets(refs, p, scale, rhs, start, cells):
    for j, ref in enumerate(refs):
        b = ref[p].astype(jnp.float32) * scale
        hi = b.astype(jnp.bfloat16)
        lo = (b - hi.astype(jnp.float32)).astype(jnp.bfloat16)
        rhs[(start + j) * cells : (start + j + 1) * cells, :] = jnp.concatenate([hi, lo], axis=1)


def places(cells, width):
    h, z, core = lax.axis_index("bh"), lax.axis_index("bz"), lax.axis_index("bc")
    src_place = [(h, core), (1 - h, core), (h, 1 - core), (1 - h, 1 - core)]
    src_band = [(hh * SIZES[3] + z) * SIZES[4] + cc for hh, cc in src_place]
    step = 1 - 2 * core
    tgt_z = [z, (z - step) % SIZES[3], (z + step) % SIZES[3], (z + 2) % SIZES[3]]
    tgt_band = [(h * SIZES[3] + zz) * SIZES[4] + core for zz in tgt_z]
    tgt_slot = [jnp.where(zz == z, 0, jnp.where(zz == 3 - z, 1, jnp.where(zz == (z ^ 1), 2, 3))) for zz in tgt_z]
    row = lambda band: (band * (cells // width)).astype(jnp.float32) - 27.5
    return [row(band) for band in src_band], [row(band) for band in tgt_band], tgt_slot


def chosen(values, index):
    return functools.reduce(lambda x, j: jnp.where(index == j, values[j], x), range(1, len(values)), values[0])


def block(sources, b, yj, src_rows, sums, cols, cells, width, shifts=None):
    band_rows = cells // width
    groups = width // 8
    a = jnp.concatenate(sources, axis=0)
    s = lax.dot_general(jnp.concatenate([a, a], axis=1), b, NT, preferred_element_type=jnp.float32)
    put, cols_first = cols
    for i in range(len(sources)):
        tt = [None] * band_rows
        uu = [None] * band_rows
        xx = [None] * band_rows
        for q in range(band_rows):
            ps = [None] * band_rows
            qs = [None] * band_rows
            for k in range(groups):
                r0 = i * cells + q * width + k * 8
                t = [s[r0 : r0 + 8, c * width : (c + 1) * width] for c in range(band_rows)]
                rows = slice(r0, r0 + 8)
                if shifts is None:
                    w = [jnp.exp2(x) for x in t]
                    v = w
                else:
                    m = shifts[0][rows, :]
                    w = [jnp.exp2(x - m) for x in t]
                    v = [jnp.exp2(x - shifts[1](c)) for c, x in enumerate(t)]
                a1 = w[0]
                b1 = w[0]
                for c in range(1, band_rows):
                    a1 = a1 + w[c]
                    b1 = b1 + a1
                sums(rows, a1, yj * a1 - b1)
                for c in range(band_rows):
                    ps[c] = v[c] if k == 0 else ps[c] + v[c]
                    qs[c] = ps[c] if k == 0 else qs[c] + ps[c]
            for c in range(band_rows):
                tt[c] = ps[c] if q == 0 else tt[c] + ps[c]
                uu[c] = tt[c] if q == 0 else uu[c] + tt[c]
                xx[c] = qs[c] if q == 0 else xx[c] + qs[c]
        for c in range(band_rows):
            put(slice(c * width, (c + 1) * width), i == 0 and cols_first, (tt[c], xx[c], src_rows[i] * tt[c] - uu[c]))


def early_kernel(*refs, which, bands, cells, width, given):
    nsrc, ntgt = len(which), len(bands)
    handed = bool(given)
    src, refs = refs[:nsrc], refs[nsrc:]
    if given:
        scaled, (acc, accy, g0, gq, gy) = refs[: len(given)], refs[len(given) :]
    else:
        tgt, (acc, accy, g0, gq, gy, rhs) = refs[:ntgt], refs[ntgt:]
        scaled, given = (rhs,), (ntgt,)
    seats = [(ref, n * cells) for ref, count in zip(scaled, given) for n in range(count)]
    src_rows, tgt_rows, _ = places(cells, width)
    src_rows = [src_rows[i] for i in which]
    scale = score_gain / math.sqrt(src[0].shape[-1]) * math.log2(math.e)

    def one(p, n, first):
        def sums(rows, total, rowed):
            acc[p, rows, :] = total if first else acc[p, rows, :] + total
            accy[p, rows, :] = rowed if first else accy[p, rows, :] + rowed

        def put(lanes, new, values):
            for ref, value in zip((g0, gq, gy), values):
                ref[p, n, :, lanes] = value if new else ref[p, n, :, lanes] + value

        ref, start = seats[n]
        b = ref[p, start : start + cells, :]
        block([ref[p] for ref in src], b, tgt_rows[bands[n]], src_rows, sums, (put, True), cells, width)

    def pair(p, carry):
        if not handed:
            targets(tgt, p, scale, scaled[0].at[p], 0, cells)
        for n in range(ntgt):
            one(p, n, n == 0)
        return carry

    lax.fori_loop(0, src[0].shape[0], pair, 0)


def late_kernel(*refs, nsrc, ntgt, cells, width, calls):
    src, tgt = refs[:nsrc], refs[nsrc : nsrc + ntgt]
    base = nsrc + ntgt
    before = [(*call, refs[base + 5 * n : base + 5 * n + 5]) for n, call in enumerate(calls)]
    fwd_keep, fwd_send, rev_keep, rev_send, rev, rhs, acc, accy, g0, gq, gy, shift_r, shift_c = refs[base + 5 * len(calls) :]
    fwd = [(fwd_keep, 0), (fwd_keep, 1), (fwd_send, 0), (fwd_send, 1)]
    band_rows = cells // width
    src_rows, tgt_rows, tgt_slot = places(cells, width)
    scale = score_gain / math.sqrt(src[0].shape[-1]) * math.log2(math.e)
    early = ntgt - 1
    lane = lax.broadcasted_iota(jnp.int32, (16, width), 1)
    row16 = lax.broadcasted_iota(jnp.int32, (16, width), 0)
    ramp = (2 * lane - (width - 1)).astype(jnp.float32)
    pick_rows = jnp.where(row16 == 0, 1.0, jnp.where(row16 == 1, ramp, 0.0)).astype(jnp.bfloat16)
    pick_rows = jnp.concatenate([pick_rows, pick_rows], axis=1)
    sub = lax.broadcasted_iota(jnp.int32, (8, width), 0).astype(jnp.float32)

    def safe(x):
        return jnp.all((x > 2.0**-90) & (x < 2.0**110))

    def lanes(ref, sl):
        x = ref[sl, :]
        hi = x.astype(jnp.bfloat16)
        lo = (x - hi.astype(jnp.float32)).astype(jnp.bfloat16)
        return lax.dot_general(pick_rows, jnp.concatenate([hi, lo], axis=1), NT, preferred_element_type=jnp.float32)

    def emit(p, cols_of, tops):
        ok = None
        for i in range(nsrc):
            sl = slice(i * cells, (i + 1) * cells)
            one = lanes(acc, sl)
            two = lanes(accy, sl)
            good = safe(one[0:1])
            ok = good if ok is None else ok & good
            ref, at = fwd[i]
            for r in range(band_rows):
                cs = slice(r * width, (r + 1) * width)
                ref[at, p, band_rows + r : band_rows + r + 1, :] = one[0:1, cs]
                ref[at, p, 2 * band_rows + r : 2 * band_rows + r + 1, :] = one[1:2, cs] * (1.0 / width)
                ref[at, p, 3 * band_rows + r : 3 * band_rows + r + 1, :] = two[0:1, cs] * (1.0 / 32)
                top = jnp.zeros((1, width), jnp.float32)
                if tops:
                    m = shift_r[i * cells + r * width : i * cells + (r + 1) * width, :]
                    top = jnp.transpose(m)[0:1, :]
                ref[at, p, r : r + 1, :] = top
        for j in range(ntgt):
            for r in range(band_rows):
                cs = slice(r * width, (r + 1) * width)
                t, xq, ty = cols_of(j, cs)
                tot = jnp.sum(t, axis=0, keepdims=True)
                ok = ok & safe(tot)
                slot = tgt_slot[j]
                x = (129.0 + 2.0 * sub) * t - 16.0 * xq
                rev[slot, p, band_rows + r : band_rows + r + 1, :] = tot
                rev[slot, p, 2 * band_rows + r : 2 * band_rows + r + 1, :] = jnp.sum(x, axis=0, keepdims=True) * (1.0 / width)
                rev[slot, p, 3 * band_rows + r : 3 * band_rows + r + 1, :] = jnp.sum(ty, axis=0, keepdims=True) * (1.0 / 32)
                rev[slot, p, r : r + 1, :] = shift_c[j, 0:1, cs] if tops else jnp.zeros((1, width), jnp.float32)
        return ok

    def put(jb):
        def inner(lane_slice, new, values):
            for ref, value in zip((g0, gq, gy), values):
                ref[jb, :, lane_slice] = value if new else ref[jb, :, lane_slice] + value

        return inner

    def pair(p, carry):
        targets(tgt[early:], p, scale, rhs, early, cells)
        sources = [ref[p] for ref in src]
        for jb in range(early, ntgt):

            def sums(rows, total, rowed):
                i, r0 = divmod(rows.start, cells)
                for which, _, old in before:
                    if i in which:
                        at = which.index(i) * cells + r0
                        total = total + old[0][p, at : at + 8, :]
                        rowed = rowed + old[1][p, at : at + 8, :]
                acc[rows, :] = total
                accy[rows, :] = rowed

            b = rhs[jb * cells : (jb + 1) * cells, :]
            block(sources, b, tgt_rows[jb], src_rows, sums, (put(jb), True), cells, width)

        def cols_of(j, cs):
            if j >= early:
                return g0[j, :, cs], gq[j, :, cs], gy[j, :, cs]
            olds = [(old, bands.index(j)) for _, bands, old in before if j in bands]
            return [functools.reduce(jnp.add, [old[n][p, at, :, cs] for old, at in olds]) for n in (2, 3, 4)]

        ok = emit(p, cols_of, False)

        @pl.when(jnp.logical_not(ok))
        def _():
            targets(tgt[:early], p, scale, rhs, 0, cells)
            shift_r[...] = jnp.full_like(shift_r, -1e30)
            shift_c[...] = jnp.full_like(shift_c, -1e30)

            def tops(jb, c):
                b = rhs[pl.ds(pl.multiple_of(jb * cells, cells), cells), :]
                for i in range(nsrc):

                    def part(q, c2):
                        a = src[i][p, pl.ds(pl.multiple_of(q * width, width), width), :]
                        s = lax.dot_general(jnp.concatenate([a, a], axis=1), b, NT, preferred_element_type=jnp.float32)
                        sl = pl.ds(pl.multiple_of(i * cells + q * width, width), width)
                        m = shift_r[sl, :]
                        for c3 in range(band_rows):
                            m = jnp.maximum(m, s[:, c3 * width : (c3 + 1) * width])
                        shift_r[sl, :] = m
                        t = shift_c[jb]
                        shift_c[jb] = jnp.maximum(t, jnp.broadcast_to(jnp.max(s, axis=0, keepdims=True), t.shape))
                        return c2

                    lax.fori_loop(0, band_rows, part, 0)
                return c

            lax.fori_loop(0, ntgt, tops, 0)

            def level(n, c):
                sl = pl.ds(pl.multiple_of(n * width, width), width)
                m = shift_r[sl, :]
                shift_r[sl, :] = jnp.broadcast_to(jnp.max(m, axis=1, keepdims=True), m.shape)
                return c

            lax.fori_loop(0, nsrc * band_rows, level, 0)
            acc[...] = jnp.zeros_like(acc)
            accy[...] = jnp.zeros_like(accy)

            def again(jb, c):
                def more(rows, total, rowed):
                    acc[rows, :] = acc[rows, :] + total
                    accy[rows, :] = accy[rows, :] + rowed

                shifts = (shift_r, lambda c4: shift_c[jb, :, c4 * width : (c4 + 1) * width])
                b = rhs[pl.ds(pl.multiple_of(jb * cells, cells), cells), :]
                block(sources, b, chosen(tgt_rows, jb), src_rows, more, (put(jb), True), cells, width, shifts)
                return c

            lax.fori_loop(0, ntgt, again, 0)
            emit(p, lambda j, cs: (g0[j, :, cs], gq[j, :, cs], gy[j, :, cs]), True)

        return carry

    lax.fori_loop(0, src[0].shape[0], pair, 0)
    rev_keep[...] = rev[0:2]
    rev_send[...] = rev[2:4]


def cost(pairs, blocks):
    return pl.CostEstimate(
        flops=134_000_000 * pairs * blocks, bytes_accessed=100_000 * pairs * blocks, transcendentals=262_144 * pairs * blocks
    )


def match_early(src, which, bands, tgt=None, scaled=()):
    pairs, cells, chans = src[0].shape
    width = 128
    nsrc, ntgt = len(src), len(bands)
    rows = jax.ShapeDtypeStruct((pairs, nsrc * cells, width), jnp.float32)
    cols = jax.ShapeDtypeStruct((pairs, ntgt, 8, cells), jnp.float32)
    shapes = [rows, rows, cols, cols, cols]
    if tgt:
        shapes.append(jax.ShapeDtypeStruct((pairs, ntgt * cells, 2 * chans), jnp.bfloat16))
    operands = (*src, *tgt) if tgt else (*src, *scaled)
    given = tuple(part.shape[1] // cells for part in scaled)
    return pl.pallas_call(
        functools.partial(early_kernel, which=which, bands=bands, cells=cells, width=width, given=given),
        out_shape=shapes,
        in_specs=[VMEM] * len(operands),
        out_specs=[VMEM] * len(shapes),
        compiler_params=pltpu.CompilerParams(vmem_limit_bytes=14 << 20),
        cost_estimate=cost(pairs, nsrc * ntgt),
    )(*operands)


def match_late(src, tgt, early, calls):
    pairs, cells, chans = src[0].shape
    width = 128
    nsrc, ntgt = len(src), len(tgt)
    stats = jax.ShapeDtypeStruct((2, pairs, 4 * cells // width, width), jnp.float32)
    return pl.pallas_call(
        functools.partial(late_kernel, nsrc=nsrc, ntgt=ntgt, cells=cells, width=width, calls=calls),
        out_shape=[stats] * 4,
        in_specs=[VMEM] * (nsrc + ntgt + len(early)),
        out_specs=[VMEM] * 4,
        scratch_shapes=[
            pltpu.VMEM((4,) + stats.shape[1:], jnp.float32),
            pltpu.VMEM((ntgt * cells, 2 * chans), jnp.bfloat16),
            pltpu.VMEM((nsrc * cells, width), jnp.float32),
            pltpu.VMEM((nsrc * cells, width), jnp.float32),
            pltpu.VMEM((ntgt, 8, cells), jnp.float32),
            pltpu.VMEM((ntgt, 8, cells), jnp.float32),
            pltpu.VMEM((ntgt, 8, cells), jnp.float32),
            pltpu.VMEM((nsrc * cells, width), jnp.float32),
            pltpu.VMEM((ntgt, 8, cells), jnp.float32),
        ],
        compiler_params=pltpu.CompilerParams(vmem_limit_bytes=24 << 20),
        cost_estimate=cost(pairs, nsrc),
    )(*src, *tgt, *early)


def joined(left, right, band_rows):
    part = lambda x, k: x[k * band_rows : (k + 1) * band_rows]
    top = jnp.maximum(part(left, 0), part(right, 0))
    scale_l = jnp.exp2(part(left, 0) - top)
    scale_r = jnp.exp2(part(right, 0) - top)
    return [top] + [part(left, k) * scale_l + part(right, k) * scale_r for k in range(1, 4)]


def half_kernel(fwd, fwd_in, rev, rev_in, *outs, band_rows):
    for way, (own, other) in enumerate(((fwd, fwd_in), (rev, rev_in))):
        for side in range(2):
            for p in range(own.shape[1]):
                for k, value in enumerate(joined(own[side, p], other[side, p], band_rows)):
                    outs[2 * way + side][p, k * band_rows : (k + 1) * band_rows] = value


def half(fwd, fwd_in, rev, rev_in, band_rows):
    shape = jax.ShapeDtypeStruct(fwd.shape[1:], jnp.float32)
    return pl.pallas_call(
        functools.partial(half_kernel, band_rows=band_rows),
        out_shape=[shape] * 4,
        in_specs=[VMEM] * 4,
        out_specs=[VMEM] * 4,
        compiler_params=pltpu.CompilerParams(vmem_limit_bytes=4 << 20),
    )(fwd, fwd_in, rev, rev_in)


def merge_kernel(fwd, fwd_in, rev, rev_in, out, *, band_rows, width):
    band = (lax.axis_index("bh") * SIZES[3] + lax.axis_index("bz")) * SIZES[4] + lax.axis_index("bc")
    col = (2 * lax.broadcasted_iota(jnp.int32, (band_rows, width), 1) - (width - 1)).astype(jnp.float32) * (1.0 / width)
    row = lax.broadcasted_iota(jnp.int32, (band_rows, width), 0) + band * band_rows
    row = (2 * row - 63).astype(jnp.float32) * (1.0 / 64)
    for p in range(out.shape[0]):
        for way, (own, other) in enumerate(((fwd, fwd_in), (rev, rev_in))):
            _, total, cols, rows = joined(own[p], other[p], band_rows)
            out[p, way, 0] = cols / total - col
            out[p, way, 1] = rows / total - row


def merge(fwd, fwd_in, rev, rev_in, band_rows, width):
    return pl.pallas_call(
        functools.partial(merge_kernel, band_rows=band_rows, width=width),
        out_shape=jax.ShapeDtypeStruct((fwd.shape[0], 2, 2, band_rows, width), jnp.float32),
        in_specs=[VMEM] * 4,
        out_specs=VMEM,
        compiler_params=pltpu.CompilerParams(vmem_limit_bytes=4 << 20),
    )(fwd, fwd_in, rev, rev_in)


def refine_kernel(weight, bias, chip, own, core, out, mask, *cur, layers):
    pairs, ways, comps, band_rows, width = own.shape
    high = 3 * band_rows
    total = pairs * ways * high
    band = (lax.axis_index("bh") * SIZES[3] + lax.axis_index("bz")) * SIZES[4] + lax.axis_index("bc")
    last = SIZES[2] * SIZES[3] * SIZES[4] - 1
    odd = lax.axis_index("bc") == 1
    full = lambda value: jnp.full((band_rows, width), value, jnp.float32)
    for p in range(pairs):
        for d in range(ways):
            base = (p * ways + d) * high
            mask[base : base + band_rows] = full(jnp.where(band == 0, 0.0, 1.0))
            mask[base + band_rows : base + 2 * band_rows] = full(1.0)
            mask[base + 2 * band_rows : base + high] = full(jnp.where(band == last, 0.0, 1.0))
            for i in range(comps):
                near, far = core[p, d, i], chip[p, d, i]
                cur[i][base : base + band_rows] = jnp.where(odd, near, far)
                cur[i][base + band_rows : base + 2 * band_rows] = own[p, d, i]
                cur[i][base + 2 * band_rows : base + high] = jnp.where(odd, far, near)
    inside = mask[...]
    lane = lax.broadcasted_iota(jnp.int32, (total, width), 1)
    keep_left = (lane > 0).astype(jnp.float32)
    keep_right = (lane < width - 1).astype(jnp.float32)
    for layer in range(layers):
        taps = []
        for i in range(comps):
            act = jnp.tanh(2.0 * cur[i][...]) * inside
            taps.append((pltpu.roll(act, 1, 1) * keep_left, act, pltpu.roll(act, width - 1, 1) * keep_right))
        for o in range(comps):
            lines = []
            for r in range(3):
                line = None
                for i in range(comps):
                    for c in range(3):
                        term = taps[i][c] * weight[(((layer * comps + o) * comps + i) * 3 + r) * 3 + c]
                        line = term if line is None else line + term
                lines.append(line)
            grown = pltpu.roll(lines[0], 1, 0) + lines[1] + pltpu.roll(lines[2], total - 1, 0)
            cur[o][...] = cur[o][...] + (grown + bias[layer * comps + o])
    for i in range(comps):
        for p in range(pairs):
            for d in range(ways):
                base = (p * ways + d) * high + band_rows
                out[p, d, i] = cur[i][base : base + band_rows]


def refine(weight, bias, chip, own, core):
    pairs, ways, comps, band_rows, width = own.shape
    return pl.pallas_call(
        functools.partial(refine_kernel, layers=weight.shape[0]),
        out_shape=jax.ShapeDtypeStruct(own.shape, jnp.float32),
        in_specs=[SMEM, SMEM, VMEM, VMEM, VMEM],
        out_specs=VMEM,
        scratch_shapes=[pltpu.VMEM((pairs * ways * 3 * band_rows, width), jnp.float32)] * (comps + 1),
        compiler_params=pltpu.CompilerParams(vmem_limit_bytes=4 << 20),
    )(weight.reshape(-1), bias.reshape(-1), chip, own, core)


def split_kernel(whole, first, second):
    cut = first.shape[1]
    first[...] = whole[:, :cut]
    second[...] = whole[:, cut:]


def split(whole, cut):
    frames, cells, chans = whole.shape
    return pl.pallas_call(
        split_kernel,
        out_shape=[jax.ShapeDtypeStruct((frames, size, chans), whole.dtype) for size in (cut, cells - cut)],
        in_specs=[VMEM],
        out_specs=[VMEM, VMEM],
        compiler_params=pltpu.CompilerParams(vmem_limit_bytes=4 << 20),
    )(whole)


def gather_frames(blocks, table):
    orders = (
        (by_core(flip_y, flip_b), by_core(flip_a, flip_y), by_core(flip_b, flip_a)),
        (flip_a, flip_b, flip_y),
    )
    first = lax.optimization_barrier([hop(block, order[0]) for block, order in zip(blocks, orders)])
    send = [jnp.concatenate(both, axis=0) for both in zip(blocks, first)]
    second = [hop(part, order[1]) for part, order in zip(send, orders)]
    tables = [hop(table, order[2]) for order in orders]
    second, tables = lax.optimization_barrier((second, tables))
    held = [[part, piece] for part, piece in zip(send, second)]
    sent = [hop(part, order[2]) for part, order in zip(offer(tables, held), orders)]
    return pick(table, [have + [piece] for have, piece in zip(held, sent)])


def matched(src0, tgt0):
    tgt1 = hop(tgt0, ring)
    tgt2 = hop(tgt0, back)
    src1 = hop(src0, flip_h)
    src2 = hop(src0, flip_c)
    *own, scaled0 = match_early((src0, src2), (0, 2), (0,), tgt=(tgt0,))
    tgt3 = hop(tgt1, ring)
    *near, scaled1 = match_early((src0, src2), (0, 2), (1, 2), tgt=(tgt1, tgt2))
    src3 = hop(src1, flip_c)
    other = match_early((src1, src3), (1, 3), (0, 1, 2), scaled=(scaled0, scaled1))
    calls = (((0, 2), (0,)), ((0, 2), (1, 2)), ((1, 3), (0, 1, 2)))
    return match_late((src0, src1, src2, src3), (tgt0, tgt1, tgt2, tgt3), (*own, *near, *other), calls)


def shards(features, frame_pairs, conv_weight, conv_bias):
    frames, band_rows, width, chans = features.shape
    cells = band_rows * width
    flat_features = features.reshape(frames, cells, chans)
    src0, tgt0 = gather_frames(split(flat_features, cells * 11 // 16), frame_pairs)
    fwd_keep, fwd_send, rev_keep, rev_send = matched(src0, tgt0)
    fwd0, fwd1, rev0, rev1 = half(fwd_keep, hop(fwd_send, flip_c), rev_keep, hop(rev_send, flip_za), band_rows)
    flows = merge(fwd0, hop(fwd1, flip_h), rev0, hop(rev1, flip_zb), band_rows, width)
    core = hop(flows, flip_c)
    chip = hop(flows, next_chip)
    return refine(conv_weight, conv_bias, chip, flows, core)


def solution(mesh):
    finer = Mesh(mesh.devices.reshape(SIZES), AXES)
    frame, band = AXES[:2], AXES[2:]
    placed = (P(frame, band, None, None), P(frame, None), P(), P())
    return jax.shard_map(
        shards,
        mesh=finer,
        in_specs=placed,
        out_specs=P(frame, None, None, band, None),
        check_vma=False,
    )
```

```python
import functools
import itertools
import math

import jax
import jax.numpy as jnp
from jax import lax
from jax.experimental import pallas as pl
from jax.experimental.pallas import tpu as pltpu
from jax.sharding import Mesh
from jax.sharding import PartitionSpec as P

score_gain = 2.5
AXES = ("fx", "fy", "bh", "bz", "bc")
SIZES = (4, 2, 2, 4, 2)
VMEM = pl.BlockSpec(memory_space=pltpu.VMEM)
SMEM = pl.BlockSpec(memory_space=pltpu.SMEM)
NT = (((1,), (1,)), ((), ()))


def flat(coords):
    index = 0
    for value, size in zip(coords, SIZES):
        index = index * size + value
    return index


def hop(value, move):
    route = []
    for coords in itertools.product(*(range(size) for size in SIZES)):
        target = move(*coords)
        if target is not None:
            route.append((flat(coords), flat(target)))
    return lax.ppermute(value, AXES, route)


def flip_y(x, y, h, z, c):
    return x, 1 - y, h, z, c


def flip_a(x, y, h, z, c):
    return x ^ 1, y, h, z, c


def flip_b(x, y, h, z, c):
    return 3 - x, y, h, z, c


def flip_h(x, y, h, z, c):
    return x, y, 1 - h, z, c


def flip_c(x, y, h, z, c):
    return x, y, h, z, 1 - c


def flip_za(x, y, h, z, c):
    return x, y, h, z ^ 1, c


def flip_zb(x, y, h, z, c):
    return x, y, h, 3 - z, c


def ring(x, y, h, z, c):
    return x, y, h, (z + 1 - 2 * c) % SIZES[3], c


def back(x, y, h, z, c):
    return x, y, h, (z - 1 + 2 * c) % SIZES[3], c


def by_core(first, second):
    def move(*coords):
        return (second if coords[4] else first)(*coords)

    return move


def next_chip(x, y, h, z, c):
    band = (h * SIZES[3] + z) * SIZES[4] + c + 2 * c - 1
    if band < 0 or band >= SIZES[2] * SIZES[3] * SIZES[4]:
        return x, y, h, z, c
    return x, y, band // (SIZES[3] * SIZES[4]), band // SIZES[4] % SIZES[3], band % SIZES[4]


def gray(x):
    return (x ^ (x >> 1)) & 1, x >> 1


def seat(frame, frames):
    me_x, me_y, core = lax.axis_index("fx"), lax.axis_index("fy"), lax.axis_index("bc")
    me_a, me_b = gray(me_x)
    group = frame // frames
    to_a, to_b = gray(group // 2)
    fa, fb, fy = to_a ^ me_a, to_b ^ me_b, (group % 2) ^ me_y
    other = core == 1
    first = (jnp.where(other, fb, fy), jnp.where(other, fy, fa), jnp.where(other, fa, fb))
    return (first, (fa, fb, fy)), frame % frames


def copy_held(pieces, bits, which, frames, take, also=True):
    for side, piece in enumerate(pieces):

        @pl.when((bits[1] == side) & also)
        def _():
            take(piece[bits[0] * frames + which])


def offer_kernel(*refs, parts):
    tables, pieces, outs = refs[:parts], refs[parts : 3 * parts], refs[3 * parts :]
    frames = pieces[0].shape[0] // 2
    for v in range(parts):
        for slot in range(tables[v].shape[0]):
            for side in range(2):
                seats, which = seat(tables[v][slot, side], frames)

                def take(value):
                    outs[v][2 * slot + side] = value

                copy_held(pieces[2 * v : 2 * v + 2], seats[v], which, frames, take)


def offer(tables, held):
    pieces = [piece for have in held for piece in have]
    slots = 2 * tables[0].shape[0]
    return pl.pallas_call(
        functools.partial(offer_kernel, parts=len(held)),
        out_shape=[jax.ShapeDtypeStruct((slots,) + have[0].shape[1:], have[0].dtype) for have in held],
        in_specs=[SMEM] * len(held) + [VMEM] * len(pieces),
        out_specs=[VMEM] * len(held),
        compiler_params=pltpu.CompilerParams(vmem_limit_bytes=8 << 20),
    )(*tables, *pieces)


def pick_kernel(table, *refs, parts):
    pieces, outs = refs[: 3 * parts], refs[3 * parts :]
    frames = pieces[0].shape[0] // 2
    for slot in range(table.shape[0]):
        for side in range(2):
            seats, which = seat(table[slot, side], frames)
            start = 0
            for v in range(parts):
                count = pieces[3 * v].shape[1]

                def take(value):
                    outs[side][slot, start : start + count] = value

                copy_held(pieces[3 * v : 3 * v + 2], seats[v], which, frames, take, seats[v][2] == 0)

                @pl.when(seats[v][2] == 1)
                def _():
                    take(pieces[3 * v + 2][2 * slot + side])

                start += count


def pick(table, held):
    pieces = [piece for have in held for piece in have]
    cells = sum(have[0].shape[1] for have in held)
    shape = jax.ShapeDtypeStruct((table.shape[0], cells, pieces[0].shape[2]), pieces[0].dtype)
    return pl.pallas_call(
        functools.partial(pick_kernel, parts=len(held)),
        out_shape=[shape, shape],
        in_specs=[SMEM] + [VMEM] * len(pieces),
        out_specs=[VMEM, VMEM],
        compiler_params=pltpu.CompilerParams(vmem_limit_bytes=12 << 20),
    )(table, *pieces)


def targets(refs, p, scale, rhs, start, cells):
    for j, ref in enumerate(refs):
        b = ref[p].astype(jnp.float32) * scale
        hi = b.astype(jnp.bfloat16)
        lo = (b - hi.astype(jnp.float32)).astype(jnp.bfloat16)
        rhs[(start + j) * cells : (start + j + 1) * cells, :] = jnp.concatenate([hi, lo], axis=1)


def places(cells, width):
    h, z, core = lax.axis_index("bh"), lax.axis_index("bz"), lax.axis_index("bc")
    src_place = [(h, core), (1 - h, core), (h, 1 - core), (1 - h, 1 - core)]
    src_band = [(hh * SIZES[3] + z) * SIZES[4] + cc for hh, cc in src_place]
    step = 1 - 2 * core
    tgt_z = [z, (z - step) % SIZES[3], (z + step) % SIZES[3], (z + 2) % SIZES[3]]
    tgt_band = [(h * SIZES[3] + zz) * SIZES[4] + core for zz in tgt_z]
    tgt_slot = [jnp.where(zz == z, 0, jnp.where(zz == 3 - z, 1, jnp.where(zz == (z ^ 1), 2, 3))) for zz in tgt_z]
    row = lambda band: (band * (cells // width)).astype(jnp.float32) - 27.5
    return [row(band) for band in src_band], [row(band) for band in tgt_band], tgt_slot


def chosen(values, index):
    return functools.reduce(lambda x, j: jnp.where(index == j, values[j], x), range(1, len(values)), values[0])


def block(sources, b, yj, src_rows, sums, cols, cells, width, shifts=None):
    band_rows = cells // width
    groups = width // 8
    a = jnp.concatenate(sources, axis=0)
    s = lax.dot_general(jnp.concatenate([a, a], axis=1), b, NT, preferred_element_type=jnp.float32)
    put, cols_first = cols
    for i in range(len(sources)):
        tt = [None] * band_rows
        uu = [None] * band_rows
        xx = [None] * band_rows
        for q in range(band_rows):
            ps = [None] * band_rows
            qs = [None] * band_rows
            for k in range(groups):
                r0 = i * cells + q * width + k * 8
                t = [s[r0 : r0 + 8, c * width : (c + 1) * width] for c in range(band_rows)]
                rows = slice(r0, r0 + 8)
                if shifts is None:
                    w = [jnp.exp2(x) for x in t]
                    v = w
                else:
                    m = shifts[0][rows, :]
                    w = [jnp.exp2(x - m) for x in t]
                    v = [jnp.exp2(x - shifts[1](c)) for c, x in enumerate(t)]
                a1 = w[0]
                b1 = w[0]
                for c in range(1, band_rows):
                    a1 = a1 + w[c]
                    b1 = b1 + a1
                sums(rows, a1, yj * a1 - b1)
                for c in range(band_rows):
                    ps[c] = v[c] if k == 0 else ps[c] + v[c]
                    qs[c] = ps[c] if k == 0 else qs[c] + ps[c]
            for c in range(band_rows):
                tt[c] = ps[c] if q == 0 else tt[c] + ps[c]
                uu[c] = tt[c] if q == 0 else uu[c] + tt[c]
                xx[c] = qs[c] if q == 0 else xx[c] + qs[c]
        for c in range(band_rows):
            put(slice(c * width, (c + 1) * width), i == 0 and cols_first, (tt[c], xx[c], src_rows[i] * tt[c] - uu[c]))


def early_kernel(*refs, which, bands, cells, width, given):
    nsrc, ntgt = len(which), len(bands)
    handed = bool(given)
    src, refs = refs[:nsrc], refs[nsrc:]
    if given:
        scaled, (acc, accy, g0, gq, gy) = refs[: len(given)], refs[len(given) :]
    else:
        tgt, (acc, accy, g0, gq, gy, rhs) = refs[:ntgt], refs[ntgt:]
        scaled, given = (rhs,), (ntgt,)
    seats = [(ref, n * cells) for ref, count in zip(scaled, given) for n in range(count)]
    src_rows, tgt_rows, _ = places(cells, width)
    src_rows = [src_rows[i] for i in which]
    scale = score_gain / math.sqrt(src[0].shape[-1]) * math.log2(math.e)

    def one(p, n, first):
        def sums(rows, total, rowed):
            acc[p, rows, :] = total if first else acc[p, rows, :] + total
            accy[p, rows, :] = rowed if first else accy[p, rows, :] + rowed

        def put(lanes, new, values):
            for ref, value in zip((g0, gq, gy), values):
                ref[p, n, :, lanes] = value if new else ref[p, n, :, lanes] + value

        ref, start = seats[n]
        b = ref[p, start : start + cells, :]
        block([ref[p] for ref in src], b, tgt_rows[bands[n]], src_rows, sums, (put, True), cells, width)

    def pair(p, carry):
        if not handed:
            targets(tgt, p, scale, scaled[0].at[p], 0, cells)
        for n in range(ntgt):
            one(p, n, n == 0)
        return carry

    lax.fori_loop(0, src[0].shape[0], pair, 0)


def late_kernel(*refs, nsrc, ntgt, cells, width, calls):
    src, tgt = refs[:nsrc], refs[nsrc : nsrc + ntgt]
    base = nsrc + ntgt
    before = [(*call, refs[base + 5 * n : base + 5 * n + 5]) for n, call in enumerate(calls)]
    fwd_keep, fwd_send, rev_keep, rev_send, rev, rhs, acc, accy, g0, gq, gy, shift_r, shift_c = refs[base + 5 * len(calls) :]
    fwd = [(fwd_keep, 0), (fwd_keep, 1), (fwd_send, 0), (fwd_send, 1)]
    band_rows = cells // width
    src_rows, tgt_rows, tgt_slot = places(cells, width)
    scale = score_gain / math.sqrt(src[0].shape[-1]) * math.log2(math.e)
    early = ntgt - 1
    lane = lax.broadcasted_iota(jnp.int32, (16, width), 1)
    row16 = lax.broadcasted_iota(jnp.int32, (16, width), 0)
    ramp = (2 * lane - (width - 1)).astype(jnp.float32)
    pick_rows = jnp.where(row16 == 0, 1.0, jnp.where(row16 == 1, ramp, 0.0)).astype(jnp.bfloat16)
    pick_rows = jnp.concatenate([pick_rows, pick_rows], axis=1)
    sub = lax.broadcasted_iota(jnp.int32, (8, width), 0).astype(jnp.float32)

    def safe(x):
        return jnp.all((x > 2.0**-90) & (x < 2.0**110))

    def lanes(ref, sl):
        x = ref[sl, :]
        hi = x.astype(jnp.bfloat16)
        lo = (x - hi.astype(jnp.float32)).astype(jnp.bfloat16)
        return lax.dot_general(pick_rows, jnp.concatenate([hi, lo], axis=1), NT, preferred_element_type=jnp.float32)

    def emit(p, cols_of, tops):
        ok = None
        for i in range(nsrc):
            sl = slice(i * cells, (i + 1) * cells)
            one = lanes(acc, sl)
            two = lanes(accy, sl)
            good = safe(one[0:1])
            ok = good if ok is None else ok & good
            ref, at = fwd[i]
            for r in range(band_rows):
                cs = slice(r * width, (r + 1) * width)
                ref[at, p, band_rows + r : band_rows + r + 1, :] = one[0:1, cs]
                ref[at, p, 2 * band_rows + r : 2 * band_rows + r + 1, :] = one[1:2, cs] * (1.0 / width)
                ref[at, p, 3 * band_rows + r : 3 * band_rows + r + 1, :] = two[0:1, cs] * (1.0 / 32)
                top = jnp.zeros((1, width), jnp.float32)
                if tops:
                    m = shift_r[i * cells + r * width : i * cells + (r + 1) * width, :]
                    top = jnp.transpose(m)[0:1, :]
                ref[at, p, r : r + 1, :] = top
        for j in range(ntgt):
            for r in range(band_rows):
                cs = slice(r * width, (r + 1) * width)
                t, xq, ty = cols_of(j, cs)
                tot = jnp.sum(t, axis=0, keepdims=True)
                ok = ok & safe(tot)
                slot = tgt_slot[j]
                x = (129.0 + 2.0 * sub) * t - 16.0 * xq
                rev[slot, p, band_rows + r : band_rows + r + 1, :] = tot
                rev[slot, p, 2 * band_rows + r : 2 * band_rows + r + 1, :] = jnp.sum(x, axis=0, keepdims=True) * (1.0 / width)
                rev[slot, p, 3 * band_rows + r : 3 * band_rows + r + 1, :] = jnp.sum(ty, axis=0, keepdims=True) * (1.0 / 32)
                rev[slot, p, r : r + 1, :] = shift_c[j, 0:1, cs] if tops else jnp.zeros((1, width), jnp.float32)
        return ok

    def put(jb):
        def inner(lane_slice, new, values):
            for ref, value in zip((g0, gq, gy), values):
                ref[jb, :, lane_slice] = value if new else ref[jb, :, lane_slice] + value

        return inner

    def pair(p, carry):
        targets(tgt[early:], p, scale, rhs, early, cells)
        sources = [ref[p] for ref in src]
        for jb in range(early, ntgt):

            def sums(rows, total, rowed):
                i, r0 = divmod(rows.start, cells)
                for which, _, old in before:
                    if i in which:
                        at = which.index(i) * cells + r0
                        total = total + old[0][p, at : at + 8, :]
                        rowed = rowed + old[1][p, at : at + 8, :]
                acc[rows, :] = total
                accy[rows, :] = rowed

            b = rhs[jb * cells : (jb + 1) * cells, :]
            block(sources, b, tgt_rows[jb], src_rows, sums, (put(jb), True), cells, width)

        def cols_of(j, cs):
            if j >= early:
                return g0[j, :, cs], gq[j, :, cs], gy[j, :, cs]
            olds = [(old, bands.index(j)) for _, bands, old in before if j in bands]
            return [functools.reduce(jnp.add, [old[n][p, at, :, cs] for old, at in olds]) for n in (2, 3, 4)]

        ok = emit(p, cols_of, False)

        @pl.when(jnp.logical_not(ok))
        def _():
            targets(tgt[:early], p, scale, rhs, 0, cells)
            shift_r[...] = jnp.full_like(shift_r, -1e30)
            shift_c[...] = jnp.full_like(shift_c, -1e30)

            def tops(jb, c):
                b = rhs[pl.ds(pl.multiple_of(jb * cells, cells), cells), :]
                for i in range(nsrc):

                    def part(q, c2):
                        a = src[i][p, pl.ds(pl.multiple_of(q * width, width), width), :]
                        s = lax.dot_general(jnp.concatenate([a, a], axis=1), b, NT, preferred_element_type=jnp.float32)
                        sl = pl.ds(pl.multiple_of(i * cells + q * width, width), width)
                        m = shift_r[sl, :]
                        for c3 in range(band_rows):
                            m = jnp.maximum(m, s[:, c3 * width : (c3 + 1) * width])
                        shift_r[sl, :] = m
                        t = shift_c[jb]
                        shift_c[jb] = jnp.maximum(t, jnp.broadcast_to(jnp.max(s, axis=0, keepdims=True), t.shape))
                        return c2

                    lax.fori_loop(0, band_rows, part, 0)
                return c

            lax.fori_loop(0, ntgt, tops, 0)

            def level(n, c):
                sl = pl.ds(pl.multiple_of(n * width, width), width)
                m = shift_r[sl, :]
                shift_r[sl, :] = jnp.broadcast_to(jnp.max(m, axis=1, keepdims=True), m.shape)
                return c

            lax.fori_loop(0, nsrc * band_rows, level, 0)
            acc[...] = jnp.zeros_like(acc)
            accy[...] = jnp.zeros_like(accy)

            def again(jb, c):
                def more(rows, total, rowed):
                    acc[rows, :] = acc[rows, :] + total
                    accy[rows, :] = accy[rows, :] + rowed

                shifts = (shift_r, lambda c4: shift_c[jb, :, c4 * width : (c4 + 1) * width])
                b = rhs[pl.ds(pl.multiple_of(jb * cells, cells), cells), :]
                block(sources, b, chosen(tgt_rows, jb), src_rows, more, (put(jb), True), cells, width, shifts)
                return c

            lax.fori_loop(0, ntgt, again, 0)
            emit(p, lambda j, cs: (g0[j, :, cs], gq[j, :, cs], gy[j, :, cs]), True)

        return carry

    lax.fori_loop(0, src[0].shape[0], pair, 0)
    rev_keep[...] = rev[0:2]
    rev_send[...] = rev[2:4]


def cost(pairs, blocks):
    return pl.CostEstimate(
        flops=134_000_000 * pairs * blocks, bytes_accessed=100_000 * pairs * blocks, transcendentals=262_144 * pairs * blocks
    )


def match_early(src, which, bands, tgt=None, scaled=()):
    pairs, cells, chans = src[0].shape
    width = 128
    nsrc, ntgt = len(src), len(bands)
    rows = jax.ShapeDtypeStruct((pairs, nsrc * cells, width), jnp.float32)
    cols = jax.ShapeDtypeStruct((pairs, ntgt, 8, cells), jnp.float32)
    shapes = [rows, rows, cols, cols, cols]
    if tgt:
        shapes.append(jax.ShapeDtypeStruct((pairs, ntgt * cells, 2 * chans), jnp.bfloat16))
    operands = (*src, *tgt) if tgt else (*src, *scaled)
    given = tuple(part.shape[1] // cells for part in scaled)
    return pl.pallas_call(
        functools.partial(early_kernel, which=which, bands=bands, cells=cells, width=width, given=given),
        out_shape=shapes,
        in_specs=[VMEM] * len(operands),
        out_specs=[VMEM] * len(shapes),
        compiler_params=pltpu.CompilerParams(vmem_limit_bytes=14 << 20),
        cost_estimate=cost(pairs, nsrc * ntgt),
    )(*operands)


def match_late(src, tgt, early, calls):
    pairs, cells, chans = src[0].shape
    width = 128
    nsrc, ntgt = len(src), len(tgt)
    stats = jax.ShapeDtypeStruct((2, pairs, 4 * cells // width, width), jnp.float32)
    return pl.pallas_call(
        functools.partial(late_kernel, nsrc=nsrc, ntgt=ntgt, cells=cells, width=width, calls=calls),
        out_shape=[stats] * 4,
        in_specs=[VMEM] * (nsrc + ntgt + len(early)),
        out_specs=[VMEM] * 4,
        scratch_shapes=[
            pltpu.VMEM((4,) + stats.shape[1:], jnp.float32),
            pltpu.VMEM((ntgt * cells, 2 * chans), jnp.bfloat16),
            pltpu.VMEM((nsrc * cells, width), jnp.float32),
            pltpu.VMEM((nsrc * cells, width), jnp.float32),
            pltpu.VMEM((ntgt, 8, cells), jnp.float32),
            pltpu.VMEM((ntgt, 8, cells), jnp.float32),
            pltpu.VMEM((ntgt, 8, cells), jnp.float32),
            pltpu.VMEM((nsrc * cells, width), jnp.float32),
            pltpu.VMEM((ntgt, 8, cells), jnp.float32),
        ],
        compiler_params=pltpu.CompilerParams(vmem_limit_bytes=24 << 20),
        cost_estimate=cost(pairs, nsrc),
    )(*src, *tgt, *early)


def joined(left, right, band_rows):
    part = lambda x, k: x[k * band_rows : (k + 1) * band_rows]
    top = jnp.maximum(part(left, 0), part(right, 0))
    scale_l = jnp.exp2(part(left, 0) - top)
    scale_r = jnp.exp2(part(right, 0) - top)
    return [top] + [part(left, k) * scale_l + part(right, k) * scale_r for k in range(1, 4)]


def half_kernel(fwd, fwd_in, rev, rev_in, *outs, band_rows):
    for way, (own, other) in enumerate(((fwd, fwd_in), (rev, rev_in))):
        for side in range(2):
            for p in range(own.shape[1]):
                for k, value in enumerate(joined(own[side, p], other[side, p], band_rows)):
                    outs[2 * way + side][p, k * band_rows : (k + 1) * band_rows] = value


def half(fwd, fwd_in, rev, rev_in, band_rows):
    shape = jax.ShapeDtypeStruct(fwd.shape[1:], jnp.float32)
    return pl.pallas_call(
        functools.partial(half_kernel, band_rows=band_rows),
        out_shape=[shape] * 4,
        in_specs=[VMEM] * 4,
        out_specs=[VMEM] * 4,
        compiler_params=pltpu.CompilerParams(vmem_limit_bytes=4 << 20),
    )(fwd, fwd_in, rev, rev_in)


def merge_kernel(fwd, fwd_in, rev, rev_in, out, *, band_rows, width):
    band = (lax.axis_index("bh") * SIZES[3] + lax.axis_index("bz")) * SIZES[4] + lax.axis_index("bc")
    col = (2 * lax.broadcasted_iota(jnp.int32, (band_rows, width), 1) - (width - 1)).astype(jnp.float32) * (1.0 / width)
    row = lax.broadcasted_iota(jnp.int32, (band_rows, width), 0) + band * band_rows
    row = (2 * row - 63).astype(jnp.float32) * (1.0 / 64)
    for p in range(out.shape[0]):
        for way, (own, other) in enumerate(((fwd, fwd_in), (rev, rev_in))):
            _, total, cols, rows = joined(own[p], other[p], band_rows)
            out[p, way, 0] = cols / total - col
            out[p, way, 1] = rows / total - row


def merge(fwd, fwd_in, rev, rev_in, band_rows, width):
    return pl.pallas_call(
        functools.partial(merge_kernel, band_rows=band_rows, width=width),
        out_shape=jax.ShapeDtypeStruct((fwd.shape[0], 2, 2, band_rows, width), jnp.float32),
        in_specs=[VMEM] * 4,
        out_specs=VMEM,
        compiler_params=pltpu.CompilerParams(vmem_limit_bytes=4 << 20),
    )(fwd, fwd_in, rev, rev_in)


def refine_kernel(weight, bias, chip, own, core, out, mask, *cur, layers):
    pairs, ways, comps, band_rows, width = own.shape
    high = 3 * band_rows
    total = pairs * ways * high
    band = (lax.axis_index("bh") * SIZES[3] + lax.axis_index("bz")) * SIZES[4] + lax.axis_index("bc")
    last = SIZES[2] * SIZES[3] * SIZES[4] - 1
    odd = lax.axis_index("bc") == 1
    full = lambda value: jnp.full((band_rows, width), value, jnp.float32)
    for p in range(pairs):
        for d in range(ways):
            base = (p * ways + d) * high
            mask[base : base + band_rows] = full(jnp.where(band == 0, 0.0, 1.0))
            mask[base + band_rows : base + 2 * band_rows] = full(1.0)
            mask[base + 2 * band_rows : base + high] = full(jnp.where(band == last, 0.0, 1.0))
            for i in range(comps):
                near, far = core[p, d, i], chip[p, d, i]
                cur[i][base : base + band_rows] = jnp.where(odd, near, far)
                cur[i][base + band_rows : base + 2 * band_rows] = own[p, d, i]
                cur[i][base + 2 * band_rows : base + high] = jnp.where(odd, far, near)
    inside = mask[...]
    lane = lax.broadcasted_iota(jnp.int32, (total, width), 1)
    keep_left = (lane > 0).astype(jnp.float32)
    keep_right = (lane < width - 1).astype(jnp.float32)
    for layer in range(layers):
        taps = []
        for i in range(comps):
            act = jnp.tanh(2.0 * cur[i][...]) * inside
            taps.append((pltpu.roll(act, 1, 1) * keep_left, act, pltpu.roll(act, width - 1, 1) * keep_right))
        for o in range(comps):
            lines = []
            for r in range(3):
                line = None
                for i in range(comps):
                    for c in range(3):
                        term = taps[i][c] * weight[(((layer * comps + o) * comps + i) * 3 + r) * 3 + c]
                        line = term if line is None else line + term
                lines.append(line)
            grown = pltpu.roll(lines[0], 1, 0) + lines[1] + pltpu.roll(lines[2], total - 1, 0)
            cur[o][...] = cur[o][...] + (grown + bias[layer * comps + o])
    for i in range(comps):
        for p in range(pairs):
            for d in range(ways):
                base = (p * ways + d) * high + band_rows
                out[p, d, i] = cur[i][base : base + band_rows]


def refine(weight, bias, chip, own, core, layers):
    pairs, ways, comps, band_rows, width = own.shape
    return pl.pallas_call(
        functools.partial(refine_kernel, layers=layers),
        out_shape=jax.ShapeDtypeStruct(own.shape, jnp.float32),
        in_specs=[SMEM, SMEM, VMEM, VMEM, VMEM],
        out_specs=VMEM,
        scratch_shapes=[pltpu.VMEM((pairs * ways * 3 * band_rows, width), jnp.float32)] * (comps + 1),
        compiler_params=pltpu.CompilerParams(vmem_limit_bytes=4 << 20),
    )(weight, bias, chip, own, core)


def split_kernel(whole, first, second):
    cut = first.shape[1]
    first[...] = whole[:, :cut]
    second[...] = whole[:, cut:]


def split(whole, cut):
    frames, cells, chans = whole.shape
    return pl.pallas_call(
        split_kernel,
        out_shape=[jax.ShapeDtypeStruct((frames, size, chans), whole.dtype) for size in (cut, cells - cut)],
        in_specs=[VMEM],
        out_specs=[VMEM, VMEM],
        compiler_params=pltpu.CompilerParams(vmem_limit_bytes=4 << 20),
    )(whole)


def gather_frames(blocks, table, extra):
    orders = (
        (by_core(flip_y, flip_b), by_core(flip_a, flip_y), by_core(flip_b, flip_a)),
        (flip_a, flip_b, flip_y),
    )
    first = lax.optimization_barrier([hop(block, order[0]) for block, order in zip(blocks, orders)])
    send = [jnp.concatenate(both, axis=0) for both in zip(blocks, first)]
    second = [hop(part, order[1]) for part, order in zip(send, orders)]
    tables = [hop(table, order[2]) for order in orders]
    second, tables, extra = lax.optimization_barrier((second, tables, extra))
    held = [[part, piece] for part, piece in zip(send, second)]
    sent = [hop(part, order[2]) for part, order in zip(offer(tables, held), orders)]
    return (*pick(table, [have + [piece] for have, piece in zip(held, sent)]), *extra)


def matched(src0, tgt0):
    tgt1 = hop(tgt0, ring)
    tgt2 = hop(tgt0, back)
    src1 = hop(src0, flip_h)
    src2 = hop(src0, flip_c)
    *own, scaled0 = match_early((src0, src2), (0, 2), (0,), tgt=(tgt0,))
    tgt3 = hop(tgt1, ring)
    *near, scaled1 = match_early((src0, src2), (0, 2), (1, 2), tgt=(tgt1, tgt2))
    src3 = hop(src1, flip_c)
    other = match_early((src1, src3), (1, 3), (0, 1, 2), scaled=(scaled0, scaled1))
    calls = (((0, 2), (0,)), ((0, 2), (1, 2)), ((1, 3), (0, 1, 2)))
    return match_late((src0, src1, src2, src3), (tgt0, tgt1, tgt2, tgt3), (*own, *near, *other), calls)


def shards(features, frame_pairs, conv_weight, conv_bias):
    frames, band_rows, width, chans = features.shape
    cells = band_rows * width
    flat_features = features.reshape(frames, cells, chans)
    weight = conv_weight.reshape(-1)
    bias = conv_bias.reshape(-1)
    flat_conv = (weight, bias)
    src0, tgt0, weight, bias = gather_frames(split(flat_features, cells * 11 // 16), frame_pairs, flat_conv)
    fwd_keep, fwd_send, rev_keep, rev_send = matched(src0, tgt0)
    fwd0, fwd1, rev0, rev1 = half(fwd_keep, hop(fwd_send, flip_c), rev_keep, hop(rev_send, flip_za), band_rows)
    flows = merge(fwd0, hop(fwd1, flip_h), rev0, hop(rev1, flip_zb), band_rows, width)
    chip = hop(flows, next_chip)
    core = hop(flows, flip_c)
    return refine(weight, bias, chip, flows, core, conv_weight.shape[0])


def solution(mesh):
    finer = Mesh(mesh.devices.reshape(SIZES), AXES)
    frame, band = AXES[:2], AXES[2:]
    placed = (P(frame, band, None, None), P(frame, None), P(), P())
    return jax.shard_map(
        shards,
        mesh=finer,
        in_specs=placed,
        out_specs=P(frame, None, None, band, None),
        check_vma=False,
    )
```
